256 devices in a mesh: dp: 4 (over y), expert: 64 (over x, z, core).
Axes of the slice: x: 4, y: 4, z: 8, core: 2. Of those that a mesh axis runs over, the one named last changes fastest.
Arguments:
- tokens: bfloat16 [4096, 2048], P(('dp', 'expert')), parts along dimension 0, may hold values from -6 to 6
- routes: int32 [4096, 8], P(('dp', 'expert')), parts along dimension 0, may hold values from 0 to 63, as said below
- gate_weights: float32 [4096, 8], P(('dp', 'expert')), parts along dimension 0, may hold values from 0.05 to 0.5
- w_gate: bfloat16 [64, 2048, 768], P('expert'), may hold values from -0.125 to 0.125
- w_up: bfloat16 [64, 2048, 768], P('expert'), may hold values from -0.125 to 0.125
- w_down: bfloat16 [64, 768, 2048], P('expert'), may hold values from -0.21875 to 0.21875
Outputs:
- combined: bfloat16 [4096, 2048], P(('dp', 'expert')), parts along dimension 0
The draws below stay inside these ranges and needn't reach their ends.
There are 4 independent parts, one for each index of `dp`. The reference program is written for one: setup_inputs(seed, part) draws one part's arguments, and reference() takes and returns one part's arrays. A program takes and returns all parts, laid end to end along the dimension named above; an argument that names none is the same for every part. Nothing has to cross between parts.
Inputs may be any that keep to these rules, and one draw needn't show every extreme that they name: `routes`: within a part, column 0 names the same expert in every row (the step's hot expert). The other 7 columns of a row name different experts, all unlike the hot one. Of the rows of one device, at most 2 name a given expert outside column 0, and some expert reaches that count on every device.
All inputs are finite; a program needn't handle non-finite values.
Results may differ from the reference program's by a relative error of at most 0.0056.
Values may be sent and summed in bfloat16 or wider, within the bound.
A program may use at most 128 MiB of HBM per device.

```python
import math
import jax
import jax.numpy as jnp
from jax import lax

D = 2048
FF = 768
TOP = 8
ROWS_DEV = 16
EXPERTS = 64
TOKENS = 1024
COLD_CAP = 2
N_EXPERT = 64


def draw_routes(key, part):
    hot_expert = jax.random.randint(jax.random.fold_in(key, 11), (), 0, EXPERTS)
    blocks = TOKENS // ROWS_DEV
    block_keys = jax.random.split(jax.random.fold_in(key, 23), blocks)
    shuffled = jax.vmap(lambda one_key: jax.random.permutation(one_key, EXPERTS - 1))(block_keys)
    position = jnp.arange(ROWS_DEV, dtype=jnp.int32)[:, None] * (TOP - 1) + jnp.arange(TOP - 1, dtype=jnp.int32)[None, :]
    cold_pick = shuffled[:, position % (EXPERTS - 1)]
    cold_pick = cold_pick + (cold_pick >= hot_expert).astype(jnp.int32)
    first_column = jnp.full((blocks, ROWS_DEV, 1), hot_expert, jnp.int32)
    return jnp.concatenate([first_column, cold_pick.astype(jnp.int32)], axis=2).reshape(TOKENS, TOP).astype(jnp.int32)


def shard_levels(rng, shape, cuts, least, top_value):
    level, own = 1.0, jax.random.fold_in(rng, 6)
    for dim, parts in cuts:
        heights = jnp.exp(jax.random.uniform(jax.random.fold_in(own, dim), (parts,), jnp.float32, least / len(cuts), top_value / len(cuts)))
        level = level * jnp.repeat(heights, shape[dim] // parts).reshape([-1 if axis == dim else 1 for axis in range(len(shape))])
    return level


def normal_values(key, shape, deviation, most, pieces=(), kind=jnp.bfloat16):
    values = jax.random.normal(key, shape, jnp.float32) * deviation
    if len(pieces) > 0:
        values = shard_levels(key, shape, pieces, -0.22, 0.18) * values
    return jnp.clip(values, min=-most, max=most).astype(kind)


def setup_inputs(seed: int = 0, part: int = 0) -> dict:
    key_of = jax.random.split(jax.random.key(seed), 7)
    own_keys = jax.random.split(jax.random.fold_in(key_of[6], part), 7)
    return {
        "tokens": normal_values(own_keys[0], (TOKENS, D), 1.0, 6.0, ((0, 64),)),
        "routes": draw_routes(jax.random.fold_in(jax.random.fold_in(key_of[6], part), 71), part),
        "gate_weights": jnp.clip(jnp.exp(math.log(0.5) - 2.3025851 * jax.random.uniform(own_keys[2], (TOKENS, TOP), jnp.float32) ** shard_levels(own_keys[2], (TOKENS, TOP), ((0, 64),), -0.2, 0.2)), 0.05, 0.5),
        "w_gate": normal_values(key_of[3], (EXPERTS, D, FF), D ** -0.5, 0.125, ((0, 64),)),
        "w_up": normal_values(key_of[4], (EXPERTS, D, FF), D ** -0.5, 0.125, ((0, 64),)),
        "w_down": normal_values(key_of[5], (EXPERTS, FF, D), FF ** -0.5, 0.21875, ((0, 64),)),
    }


def expert_apply(row_block, gate_w, up_w, down_w):
    gate_part = jnp.dot(row_block, gate_w, preferred_element_type=jnp.float32)
    up_part = jnp.dot(row_block, up_w, preferred_element_type=jnp.float32)
    hidden = (jax.nn.silu(gate_part) * up_part).astype(jnp.bfloat16)
    return jnp.dot(hidden, down_w, preferred_element_type=jnp.float32).astype(jnp.bfloat16)


def reference(tokens, routes, gate_weights, w_gate, w_up, w_down):
    hot_expert = routes[0, 0].astype(jnp.int32)
    hot_out = expert_apply(tokens, w_gate[hot_expert], w_up[hot_expert], w_down[hot_expert])
    cold_ids = routes[:, 1:].reshape(-1).astype(jnp.int32)
    cold_total = cold_ids.shape[0]
    window = N_EXPERT * COLD_CAP
    cold_order = jnp.argsort(cold_ids, stable=True).astype(jnp.int32)
    expert_iota = jnp.arange(EXPERTS, dtype=jnp.int32)
    counts = jnp.sum((cold_ids[:, None] == expert_iota[None, :]).astype(jnp.int32), axis=0).astype(jnp.int32)
    starts = (jnp.cumsum(counts) - counts).astype(jnp.int32)
    padded_order = jnp.concatenate([cold_order, jnp.zeros((window,), jnp.int32)])

    def one_expert(stored, expert):
        picked = lax.dynamic_slice(padded_order, (starts[expert],), (window,)).astype(jnp.int32)
        is_valid = jnp.arange(window, dtype=jnp.int32) < counts[expert]
        row_block = tokens[picked // (TOP - 1)]
        result = expert_apply(row_block, w_gate[expert], w_up[expert], w_down[expert])
        target = jnp.where(is_valid, picked, cold_total).astype(jnp.int32)
        return stored.at[target].set(result), expert

    initial = jnp.zeros((cold_total + 1, D), jnp.bfloat16)
    filled, unused = lax.scan(one_expert, initial, expert_iota)
    cold_out = filled[:cold_total].reshape(TOKENS, TOP - 1, D).astype(jnp.float32)
    combined = gate_weights[:, 0:1] * hot_out.astype(jnp.float32) + jnp.sum(gate_weights[:, 1:, None] * cold_out, axis=1)
    return combined.astype(jnp.bfloat16)
```

```python
import jax
import jax.numpy as jnp
from jax import lax
from jax.sharding import PartitionSpec as P


def feed_forward(row_block, gate_w, up_w, down_w):
    gate_part = jnp.dot(row_block, gate_w, preferred_element_type=jnp.float32)
    up_part = jnp.dot(row_block, up_w, preferred_element_type=jnp.float32)
    hidden = (jax.nn.silu(gate_part) * up_part).astype(jnp.bfloat16)
    return jnp.dot(hidden, down_w, preferred_element_type=jnp.float32).astype(jnp.bfloat16)


def shards(tokens, routes, gate_weights, w_gate, w_up, w_down):
    devices = lax.axis_size("expert")
    experts = w_gate.shape[0] * devices
    row_count = routes.shape[0]
    top_count = routes.shape[1]
    model_width = tokens.shape[1]
    slot_count = (row_count * (top_count - 1) + experts - 2) // (experts - 1)
    cold_ids = routes[:, 1:]
    flat_ids = cold_ids.reshape(-1)
    expert_iota = jnp.arange(experts, dtype=jnp.int32)
    one_hot = (flat_ids[:, None] == expert_iota[None, :]).astype(jnp.int32)
    slot_rank = (jnp.sum(jnp.cumsum(one_hot, axis=0) * one_hot, axis=1) - 1).reshape(cold_ids.shape)
    slot_iota = jnp.arange(slot_count, dtype=jnp.int32)
    select = (cold_ids[:, :, None, None] == expert_iota[None, None, :, None]) & (
        slot_rank[:, :, None, None] == slot_iota[None, None, None, :]
    )
    placing = jnp.sum(select.astype(jnp.bfloat16), axis=1)
    outgoing = jnp.einsum(
        "res,rd->esd", placing, tokens, preferred_element_type=jnp.float32
    ).astype(jnp.bfloat16)
    local_gate = w_gate[0]
    local_up = w_up[0]
    local_down = w_down[0]
    arrived = lax.all_to_all(outgoing, "expert", split_axis=0, concat_axis=0, tiled=True)
    flat_rows = arrived.reshape(-1, model_width)
    answered = feed_forward(flat_rows, local_gate, local_up, local_down).reshape(arrived.shape)
    returned = lax.all_to_all(answered, "expert", split_axis=0, concat_axis=0, tiled=True)
    picked = returned.reshape(-1, model_width)[cold_ids * slot_count + slot_rank]
    hot_expert = routes[0, 0]
    is_owner = lax.axis_index("expert") == hot_expert
    gathered = lax.all_gather(tokens, "expert", axis=0, tiled=True)
    answered = lax.cond(
        is_owner,
        lambda row_block: feed_forward(row_block, local_gate, local_up, local_down),
        lambda row_block: jnp.zeros_like(row_block),
        gathered,
    )
    hot_out = lax.psum_scatter(answered, "expert", scatter_dimension=0, tiled=True)
    combined = gate_weights[:, 0:1] * hot_out.astype(jnp.float32) + jnp.sum(
        gate_weights[:, 1:, None] * picked.astype(jnp.float32), axis=1
    )
    return combined.astype(jnp.bfloat16)


def solution(mesh):
    in_specs = (
        P(("dp", "expert"), None),
        P(("dp", "expert"), None),
        P(("dp", "expert"), None),
        P("expert", None, None),
        P("expert", None, None),
        P("expert", None, None),
    )
    out_specs = P(("dp", "expert"), None)
    return jax.shard_map(shards, mesh=mesh, in_specs=in_specs, out_specs=out_specs, check_vma=False)
```

```python
import functools

import jax
import jax.numpy as jnp
from jax import lax
from jax.experimental import pallas as pl
from jax.experimental.pallas import tpu as pltpu
from jax.sharding import PartitionSpec as P

MESH = pl.DeviceIdType.MESH


def feed_forward(row_block, gate_w, up_w, down_w):
    gate_part = jnp.dot(row_block, gate_w, preferred_element_type=jnp.float32)
    up_part = jnp.dot(row_block, up_w, preferred_element_type=jnp.float32)
    hidden = (jax.nn.silu(gate_part) * up_part).astype(jnp.bfloat16)
    return jnp.dot(hidden, down_w, preferred_element_type=jnp.float32).astype(jnp.bfloat16)


def torus_shape(mesh):
    n = mesh.shape["expert"]
    try:
        row = mesh.devices.reshape(-1, n)[0]
        xs = {d.coords[0] for d in row}
        zs = {d.coords[2] for d in row}
        X, Z = len(xs), len(zs)
        C = n // (X * Z)
        if X * Z * C != n:
            raise ValueError
    except Exception:
        X, Z, C = 4, 8, 2
        if X * Z * C != n:
            X, Z, C = 1, n // 2, 2
    return X, Z, C


def coordinates(X, Z, C):
    e = lax.axis_index("expert")
    return e // (Z * C), (e // C) % Z, e % C


def device(X, Z, C, x, z, c):
    return {"expert": (x % X) * (Z * C) + (z % Z) * C + (c % C)}


def peers(X, Z, C, x, z, c):
    out = [(x + k, z, c) for k in range(1, X)]
    if Z > 1:
        out.append((x, z + 1, c))
        if Z > 2:
            out.append((x, z - 1, c))
    if C > 1:
        out.append((x, z, c + 1))
    return out


def barrier(X, Z, C, x, z, c):
    sem = pltpu.get_barrier_semaphore()
    targets = peers(X, Z, C, x, z, c)
    for t in targets:
        pl.semaphore_signal(sem, inc=1, device_id=device(X, Z, C, *t), device_id_type=MESH)
    pl.semaphore_wait(sem, len(targets))


def gather_kernel(X, Z, C, tok_ref, out_ref, own_sem, sx_send, sx_recv, sp_send, sp_recv, sm_send, sm_recv, sc_send, sc_recv):
    x, z, c = coordinates(X, Z, C)
    zp, zm = Z // 2, (Z - 1) // 2
    barrier(X, Z, C, x, z, c)

    own = pltpu.make_async_copy(tok_ref, out_ref.at[c, z, x], own_sem.at[0])
    own.start()
    xcopies = []
    for k in range(1, X):
        cp = pltpu.make_async_remote_copy(
            src_ref=tok_ref, dst_ref=out_ref.at[c, z, x], send_sem=sx_send.at[k - 1], recv_sem=sx_recv.at[k - 1],
            device_id=device(X, Z, C, x + k, z, c), device_id_type=MESH)
        cp.start()
        xcopies.append(cp)
    own.wait()
    for cp in xcopies:
        cp.wait_recv()

    ccopies = []

    def to_partner(j, blk):
        if C == 1:
            return
        cp = pltpu.make_async_remote_copy(
            src_ref=out_ref.at[c, blk], dst_ref=out_ref.at[c, blk], send_sem=sc_send.at[j], recv_sem=sc_recv.at[j],
            device_id=device(X, Z, C, x, z, c + 1), device_id_type=MESH)
        cp.start()
        ccopies.append(cp)

    to_partner(0, z)
    plus, minus = [], []
    for s in range(max(zp, zm)):
        if s < zp:
            if s >= 1:
                plus[s - 1].wait_recv()
                to_partner(s, (z - s) % Z)
            cp = pltpu.make_async_remote_copy(
                src_ref=out_ref.at[c, (z - s) % Z], dst_ref=out_ref.at[c, (z - s) % Z], send_sem=sp_send.at[s],
                recv_sem=sp_recv.at[s], device_id=device(X, Z, C, x, z + 1, c), device_id_type=MESH)
            cp.start()
            plus.append(cp)
        if s < zm:
            if s >= 1:
                minus[s - 1].wait_recv()
                to_partner(zp + s, (z + s) % Z)
            cp = pltpu.make_async_remote_copy(
                src_ref=out_ref.at[c, (z + s) % Z], dst_ref=out_ref.at[c, (z + s) % Z], send_sem=sm_send.at[s],
                recv_sem=sm_recv.at[s], device_id=device(X, Z, C, x, z - 1, c), device_id_type=MESH)
            cp.start()
            minus.append(cp)
    if zp:
        plus[zp - 1].wait_recv()
        to_partner(zp, (z - zp) % Z)
    if zm:
        minus[zm - 1].wait_recv()
        to_partner(zp + zm, (z + zm) % Z)
    for cp in ccopies:
        cp.wait_recv()
    for cp in xcopies + plus + minus + ccopies:
        cp.wait_send()


def scatter_kernel(X, Z, C, o_ref, out_ref, pbuf, plus_buf, plus_send, minus_buf, minus_send, xbuf, xsend,
                   sc_send, sc_recv, sp_send, sp_recv, sm_send, sm_recv, sx_send, sx_recv):
    x, z, c = coordinates(X, Z, C)
    zp, zm = Z // 2, (Z - 1) // 2
    barrier(X, Z, C, x, z, c)

    ccopies = []
    if C > 1:
        for blk in range(Z):
            cp = pltpu.make_async_remote_copy(
                src_ref=o_ref.at[(c + 1) % C, blk], dst_ref=pbuf.at[blk], send_sem=sc_send.at[blk], recv_sem=sc_recv.at[blk],
                device_id=device(X, Z, C, x, z, c + 1), device_id_type=MESH)
            cp.start()
            ccopies.append(cp)

    def chip_sum(blk):
        val = o_ref[c, blk].astype(jnp.float32)
        if C > 1:
            val = val + pbuf[blk].astype(jnp.float32)
        return val

    if C > 1:
        for cp in ccopies:
            cp.wait_recv()

    plus, minus = [], []
    for s in range(max(zp, zm)):
        if s < zp:
            val = chip_sum((z + zp - s) % Z)
            if s >= 1:
                plus[s - 1].wait_recv()
                val = val + plus_buf[s - 1].astype(jnp.float32)
            plus_send[s] = val.astype(jnp.bfloat16)
            cp = pltpu.make_async_remote_copy(
                src_ref=plus_send.at[s], dst_ref=plus_buf.at[s], send_sem=sp_send.at[s], recv_sem=sp_recv.at[s],
                device_id=device(X, Z, C, x, z + 1, c), device_id_type=MESH)
            cp.start()
            plus.append(cp)
        if s < zm:
            val = chip_sum((z - zm + s) % Z)
            if s >= 1:
                minus[s - 1].wait_recv()
                val = val + minus_buf[s - 1].astype(jnp.float32)
            minus_send[s] = val.astype(jnp.bfloat16)
            cp = pltpu.make_async_remote_copy(
                src_ref=minus_send.at[s], dst_ref=minus_buf.at[s], send_sem=sm_send.at[s], recv_sem=sm_recv.at[s],
                device_id=device(X, Z, C, x, z - 1, c), device_id_type=MESH)
            cp.start()
            minus.append(cp)
    total = chip_sum(z)
    if zp:
        plus[zp - 1].wait_recv()
        total = total + plus_buf[zp - 1].astype(jnp.float32)
    if zm:
        minus[zm - 1].wait_recv()
        total = total + minus_buf[zm - 1].astype(jnp.float32)
    xsend[...] = total.astype(jnp.bfloat16)
    xcopies = []
    for k in range(1, X):
        cp = pltpu.make_async_remote_copy(
            src_ref=xsend.at[(x + k) % X], dst_ref=xbuf.at[k - 1], send_sem=sx_send.at[k - 1], recv_sem=sx_recv.at[k - 1],
            device_id=device(X, Z, C, x + k, z, c), device_id_type=MESH)
        cp.start()
        xcopies.append(cp)
    result = xsend[x].astype(jnp.float32)
    for k, cp in enumerate(xcopies):
        cp.wait_recv()
        result = result + xbuf[k].astype(jnp.float32)
    out_ref[...] = result.astype(out_ref.dtype)
    for cp in ccopies + plus + minus + xcopies:
        cp.wait_send()


def hot_gather(X, Z, C, tokens):
    R, D = tokens.shape
    zp, zm = Z // 2, (Z - 1) // 2
    dma = pltpu.SemaphoreType.DMA
    return pl.pallas_call(
        functools.partial(gather_kernel, X, Z, C),
        out_shape=jax.ShapeDtypeStruct((C, Z, X, R, D), tokens.dtype),
        in_specs=[pl.BlockSpec(memory_space=pltpu.VMEM)],
        out_specs=pl.BlockSpec(memory_space=pltpu.VMEM),
        scratch_shapes=[
            dma((1,)),
            dma((max(X - 1, 1),)), dma((max(X - 1, 1),)),
            dma((max(zp, 1),)), dma((max(zp, 1),)),
            dma((max(zm, 1),)), dma((max(zm, 1),)),
            dma((Z,)), dma((Z,)),
        ],
        compiler_params=pltpu.CompilerParams(collective_id=0, has_side_effects=True),
    )(tokens)


def hot_scatter(X, Z, C, answered):
    _, _, _, R, D = answered.shape
    zp, zm = Z // 2, (Z - 1) // 2
    dma = pltpu.SemaphoreType.DMA
    bf = answered.dtype
    return pl.pallas_call(
        functools.partial(scatter_kernel, X, Z, C),
        out_shape=jax.ShapeDtypeStruct((R, D), bf),
        in_specs=[pl.BlockSpec(memory_space=pltpu.VMEM)],
        out_specs=pl.BlockSpec(memory_space=pltpu.VMEM),
        scratch_shapes=[
            pltpu.VMEM((Z, X, R, D), bf),
            pltpu.VMEM((max(zp, 1), X, R, D), bf), pltpu.VMEM((max(zp, 1), X, R, D), bf),
            pltpu.VMEM((max(zm, 1), X, R, D), bf), pltpu.VMEM((max(zm, 1), X, R, D), bf),
            pltpu.VMEM((max(X - 1, 1), R, D), bf), pltpu.VMEM((X, R, D), bf),
            dma((Z,)), dma((Z,)),
            dma((max(zp, 1),)), dma((max(zp, 1),)),
            dma((max(zm, 1),)), dma((max(zm, 1),)),
            dma((max(X - 1, 1),)), dma((max(X - 1, 1),)),
        ],
        compiler_params=pltpu.CompilerParams(collective_id=1, has_side_effects=True),
    )(answered)


def shards(X, Z, C, tokens, routes, gate_weights, w_gate, w_up, w_down):
    devices = lax.axis_size("expert")
    experts = w_gate.shape[0] * devices
    row_count = routes.shape[0]
    top_count = routes.shape[1]
    model_width = tokens.shape[1]
    slot_count = (row_count * (top_count - 1) + experts - 2) // (experts - 1)
    cold_ids = routes[:, 1:]
    flat_ids = cold_ids.reshape(-1)
    expert_iota = jnp.arange(experts, dtype=jnp.int32)
    one_hot = (flat_ids[:, None] == expert_iota[None, :]).astype(jnp.int32)
    slot_rank = (jnp.sum(jnp.cumsum(one_hot, axis=0) * one_hot, axis=1) - 1).reshape(cold_ids.shape)
    slot_iota = jnp.arange(slot_count, dtype=jnp.int32)
    select = (cold_ids[:, :, None, None] == expert_iota[None, None, :, None]) & (
        slot_rank[:, :, None, None] == slot_iota[None, None, None, :]
    )
    placing = jnp.sum(select.astype(jnp.bfloat16), axis=1)
    outgoing = jnp.einsum(
        "res,rd->esd", placing, tokens, preferred_element_type=jnp.float32
    ).astype(jnp.bfloat16)
    local_gate = w_gate[0]
    local_up = w_up[0]
    local_down = w_down[0]
    arrived = lax.all_to_all(outgoing, "expert", split_axis=0, concat_axis=0, tiled=True)
    flat_rows = arrived.reshape(-1, model_width)
    answered = feed_forward(flat_rows, local_gate, local_up, local_down).reshape(arrived.shape)
    returned = lax.all_to_all(answered, "expert", split_axis=0, concat_axis=0, tiled=True)
    picked = returned.reshape(-1, model_width)[cold_ids * slot_count + slot_rank]
    hot_expert = routes[0, 0]
    is_owner = lax.axis_index("expert") == hot_expert
    gathered = hot_gather(X, Z, C, tokens)
    hot_answer = lax.cond(
        is_owner,
        lambda row_block: feed_forward(row_block.reshape(-1, model_width), local_gate, local_up, local_down).reshape(row_block.shape),
        lambda row_block: jnp.zeros_like(row_block),
        gathered,
    )
    hot_out = hot_scatter(X, Z, C, hot_answer)
    combined = gate_weights[:, 0:1] * hot_out.astype(jnp.float32) + jnp.sum(
        gate_weights[:, 1:, None] * picked.astype(jnp.float32), axis=1
    )
    return combined.astype(jnp.bfloat16)


def solution(mesh):
    X, Z, C = torus_shape(mesh)
    in_specs = (
        P(("dp", "expert"), None),
        P(("dp", "expert"), None),
        P(("dp", "expert"), None),
        P("expert", None, None),
        P("expert", None, None),
        P("expert", None, None),
    )
    out_specs = P(("dp", "expert"), None)
    return jax.shard_map(functools.partial(shards, X, Z, C), mesh=mesh, in_specs=in_specs, out_specs=out_specs, check_vma=False)
```

```python
import functools

import jax
import jax.numpy as jnp
from jax import lax
from jax.experimental import pallas as pl
from jax.experimental.pallas import tpu as pltpu
from jax.sharding import PartitionSpec as P

MESH = pl.DeviceIdType.MESH


def feed_forward(row_block, gate_w, up_w, down_w):
    gate_part = jnp.dot(row_block, gate_w, preferred_element_type=jnp.float32)
    up_part = jnp.dot(row_block, up_w, preferred_element_type=jnp.float32)
    hidden = lax.optimization_barrier((jax.nn.silu(gate_part) * up_part).astype(jnp.bfloat16))
    return jnp.dot(hidden, down_w, preferred_element_type=jnp.float32).astype(jnp.bfloat16)


def torus_shape(mesh):
    n = mesh.shape["expert"]
    try:
        row = mesh.devices.reshape(-1, n)[0]
        xs = {d.coords[0] for d in row}
        zs = {d.coords[2] for d in row}
        X, Z = len(xs), len(zs)
        C = n // (X * Z)
        if X * Z * C != n:
            raise ValueError
    except Exception:
        X, Z, C = 4, 8, 2
        if X * Z * C != n:
            X, Z, C = 1, n // 2, 2
    return X, Z, C


def coordinates(X, Z, C):
    e = lax.axis_index("expert")
    return e // (Z * C), (e // C) % Z, e % C


def wrap(v, n):
    return (v + 4 * n) % n


def device(X, Z, C, x, z, c):
    return {"expert": wrap(x, X) * (Z * C) + wrap(z, Z) * C + wrap(c, C)}


def peers(X, Z, C, x, z, c):
    out = [(x + k, z, c) for k in range(1, X)]
    if Z > 1:
        out.append((x, z + 1, c))
        if Z > 2:
            out.append((x, z - 1, c))
    if C > 1:
        out.append((x, z, c + 1))
    return out


def barrier(X, Z, C, x, z, c):
    sem = pltpu.get_barrier_semaphore()
    targets = peers(X, Z, C, x, z, c)
    for t in targets:
        pl.semaphore_signal(sem, inc=1, device_id=device(X, Z, C, *t), device_id_type=MESH)
    pl.semaphore_wait(sem, len(targets))


def gather_kernel(X, Z, C, tok_ref, out_ref, own_sem, sx_send, sx_recv, sp_send, sp_recv, sm_send, sm_recv, sc_send, sc_recv):
    x, z, c = coordinates(X, Z, C)
    zp, zm = Z // 2, (Z - 1) // 2
    dirn = 1 - 2 * (c % 2)
    barrier(X, Z, C, x, z, c)

    own = pltpu.make_async_copy(tok_ref, out_ref.at[c, z, x], own_sem.at[0])
    own.start()
    xcopies = []
    for k in range(1, X):
        cp = pltpu.make_async_remote_copy(
            src_ref=tok_ref, dst_ref=out_ref.at[c, z, x], send_sem=sx_send.at[k - 1], recv_sem=sx_recv.at[k - 1],
            device_id=device(X, Z, C, x + k, z, c), device_id_type=MESH)
        cp.start()
        xcopies.append(cp)
    own.wait()
    for cp in xcopies:
        cp.wait_recv()

    ccopies = []

    def to_partner(j, blk):
        if C == 1:
            return
        cp = pltpu.make_async_remote_copy(
            src_ref=out_ref.at[c, blk], dst_ref=out_ref.at[c, blk], send_sem=sc_send.at[j], recv_sem=sc_recv.at[j],
            device_id=device(X, Z, C, x, z, c + 1), device_id_type=MESH)
        cp.start()
        ccopies.append(cp)

    to_partner(0, z)
    plus, minus = [], []
    for s in range(max(zp, zm)):
        if s < zp:
            if s >= 1:
                plus[s - 1].wait_recv()
                to_partner(s, wrap(z - s * dirn, Z))
            cp = pltpu.make_async_remote_copy(
                src_ref=out_ref.at[c, wrap(z - s * dirn, Z)], dst_ref=out_ref.at[c, wrap(z - s * dirn, Z)], send_sem=sp_send.at[s],
                recv_sem=sp_recv.at[s], device_id=device(X, Z, C, x, z + dirn, c), device_id_type=MESH)
            cp.start()
            plus.append(cp)
        if s < zm:
            if s >= 1:
                minus[s - 1].wait_recv()
                to_partner(zp + s, wrap(z + s * dirn, Z))
            cp = pltpu.make_async_remote_copy(
                src_ref=out_ref.at[c, wrap(z + s * dirn, Z)], dst_ref=out_ref.at[c, wrap(z + s * dirn, Z)], send_sem=sm_send.at[s],
                recv_sem=sm_recv.at[s], device_id=device(X, Z, C, x, z - dirn, c), device_id_type=MESH)
            cp.start()
            minus.append(cp)
    if zp:
        plus[zp - 1].wait_recv()
        to_partner(zp, wrap(z - zp * dirn, Z))
    if zm:
        minus[zm - 1].wait_recv()
        to_partner(zp + zm, wrap(z + zm * dirn, Z))
    for cp in ccopies:
        cp.wait_recv()
    for cp in xcopies + plus + minus + ccopies:
        cp.wait_send()


def scatter_kernel(X, Z, C, o_ref, out_ref, pbuf, plus_buf, plus_send, minus_buf, minus_send, xbuf, xsend,
                   sc_send, sc_recv, sp_send, sp_recv, sm_send, sm_recv, sx_send, sx_recv):
    x, z, c = coordinates(X, Z, C)
    zp, zm = Z // 2, (Z - 1) // 2
    dirn = 1 - 2 * (c % 2)
    barrier(X, Z, C, x, z, c)

    ccopies = []
    if C > 1:
        for blk in range(Z):
            cp = pltpu.make_async_remote_copy(
                src_ref=o_ref.at[(c + 1) % C, blk], dst_ref=pbuf.at[blk], send_sem=sc_send.at[blk], recv_sem=sc_recv.at[blk],
                device_id=device(X, Z, C, x, z, c + 1), device_id_type=MESH)
            cp.start()
            ccopies.append(cp)

    def chip_sum(blk):
        val = o_ref[c, blk].astype(jnp.float32)
        if C > 1:
            val = val + pbuf[blk].astype(jnp.float32)
        return val

    if C > 1:
        for cp in ccopies:
            cp.wait_recv()

    plus, minus = [], []
    for s in range(max(zp, zm)):
        if s < zp:
            val = chip_sum(wrap(z + (zp - s) * dirn, Z))
            if s >= 1:
                plus[s - 1].wait_recv()
                val = val + plus_buf[s - 1].astype(jnp.float32)
            plus_send[s] = val.astype(jnp.bfloat16)
            cp = pltpu.make_async_remote_copy(
                src_ref=plus_send.at[s], dst_ref=plus_buf.at[s], send_sem=sp_send.at[s], recv_sem=sp_recv.at[s],
                device_id=device(X, Z, C, x, z + dirn, c), device_id_type=MESH)
            cp.start()
            plus.append(cp)
        if s < zm:
            val = chip_sum(wrap(z - (zm - s) * dirn, Z))
            if s >= 1:
                minus[s - 1].wait_recv()
                val = val + minus_buf[s - 1].astype(jnp.float32)
            minus_send[s] = val.astype(jnp.bfloat16)
            cp = pltpu.make_async_remote_copy(
                src_ref=minus_send.at[s], dst_ref=minus_buf.at[s], send_sem=sm_send.at[s], recv_sem=sm_recv.at[s],
                device_id=device(X, Z, C, x, z - dirn, c), device_id_type=MESH)
            cp.start()
            minus.append(cp)
    total = chip_sum(z)
    if zp:
        plus[zp - 1].wait_recv()
        total = total + plus_buf[zp - 1].astype(jnp.float32)
    if zm:
        minus[zm - 1].wait_recv()
        total = total + minus_buf[zm - 1].astype(jnp.float32)
    xsend[...] = total.astype(jnp.bfloat16)
    xcopies = []
    for k in range(1, X):
        cp = pltpu.make_async_remote_copy(
            src_ref=xsend.at[(x + k) % X], dst_ref=xbuf.at[k - 1], send_sem=sx_send.at[k - 1], recv_sem=sx_recv.at[k - 1],
            device_id=device(X, Z, C, x + k, z, c), device_id_type=MESH)
        cp.start()
        xcopies.append(cp)
    result = xsend[x].astype(jnp.float32)
    for k, cp in enumerate(xcopies):
        cp.wait_recv()
        result = result + xbuf[k].astype(jnp.float32)
    out_ref[...] = result.astype(out_ref.dtype)
    for cp in ccopies + plus + minus + xcopies:
        cp.wait_send()


def hot_gather(X, Z, C, tokens):
    R, D = tokens.shape
    zp, zm = Z // 2, (Z - 1) // 2
    dma = pltpu.SemaphoreType.DMA
    return pl.pallas_call(
        functools.partial(gather_kernel, X, Z, C),
        out_shape=jax.ShapeDtypeStruct((C, Z, X, R, D), tokens.dtype),
        in_specs=[pl.BlockSpec(memory_space=pltpu.VMEM)],
        out_specs=pl.BlockSpec(memory_space=pltpu.VMEM),
        scratch_shapes=[
            dma((1,)),
            dma((max(X - 1, 1),)), dma((max(X - 1, 1),)),
            dma((max(zp, 1),)), dma((max(zp, 1),)),
            dma((max(zm, 1),)), dma((max(zm, 1),)),
            dma((Z,)), dma((Z,)),
        ],
        compiler_params=pltpu.CompilerParams(collective_id=0, has_side_effects=True),
    )(tokens)


def hot_scatter(X, Z, C, answered):
    _, _, _, R, D = answered.shape
    zp, zm = Z // 2, (Z - 1) // 2
    dma = pltpu.SemaphoreType.DMA
    bf = answered.dtype
    return pl.pallas_call(
        functools.partial(scatter_kernel, X, Z, C),
        out_shape=jax.ShapeDtypeStruct((R, D), bf),
        in_specs=[pl.BlockSpec(memory_space=pltpu.VMEM)],
        out_specs=pl.BlockSpec(memory_space=pltpu.VMEM),
        scratch_shapes=[
            pltpu.VMEM((Z, X, R, D), bf),
            pltpu.VMEM((max(zp, 1), X, R, D), bf), pltpu.VMEM((max(zp, 1), X, R, D), bf),
            pltpu.VMEM((max(zm, 1), X, R, D), bf), pltpu.VMEM((max(zm, 1), X, R, D), bf),
            pltpu.VMEM((max(X - 1, 1), R, D), bf), pltpu.VMEM((X, R, D), bf),
            dma((Z,)), dma((Z,)),
            dma((max(zp, 1),)), dma((max(zp, 1),)),
            dma((max(zm, 1),)), dma((max(zm, 1),)),
            dma((max(X - 1, 1),)), dma((max(X - 1, 1),)),
        ],
        compiler_params=pltpu.CompilerParams(collective_id=1, has_side_effects=True),
    )(answered)


def shards(X, Z, C, tokens, routes, gate_weights, w_gate, w_up, w_down):
    devices = lax.axis_size("expert")
    experts = w_gate.shape[0] * devices
    row_count = routes.shape[0]
    top_count = routes.shape[1]
    model_width = tokens.shape[1]
    slot_count = (row_count * (top_count - 1) + experts - 2) // (experts - 1)
    cold_ids = routes[:, 1:]
    flat_ids = cold_ids.reshape(-1)
    expert_iota = jnp.arange(experts, dtype=jnp.int32)
    one_hot = (flat_ids[:, None] == expert_iota[None, :]).astype(jnp.int32)
    slot_rank = (jnp.sum(jnp.cumsum(one_hot, axis=0) * one_hot, axis=1) - 1).reshape(cold_ids.shape)
    slot_iota = jnp.arange(slot_count, dtype=jnp.int32)
    select = (cold_ids[:, :, None, None] == expert_iota[None, None, :, None]) & (
        slot_rank[:, :, None, None] == slot_iota[None, None, None, :]
    )
    placing = jnp.sum(select.astype(jnp.bfloat16), axis=1)
    outgoing = jnp.einsum(
        "res,rd->esd", placing, tokens, preferred_element_type=jnp.float32
    ).astype(jnp.bfloat16)
    local_gate = w_gate[0]
    local_up = w_up[0]
    local_down = w_down[0]
    arrived = lax.all_to_all(outgoing, "expert", split_axis=0, concat_axis=0, tiled=True)
    flat_rows = arrived.reshape(-1, model_width)
    answered = feed_forward(flat_rows, local_gate, local_up, local_down).reshape(arrived.shape)
    returned = lax.all_to_all(answered, "expert", split_axis=0, concat_axis=0, tiled=True)
    picked = returned.reshape(-1, model_width)[cold_ids * slot_count + slot_rank]
    hot_expert = routes[0, 0]
    is_owner = lax.axis_index("expert") == hot_expert
    gathered = hot_gather(X, Z, C, tokens)
    hot_answer = lax.cond(
        is_owner,
        lambda row_block: feed_forward(row_block.reshape(-1, model_width), local_gate, local_up, local_down).reshape(row_block.shape),
        lambda row_block: jnp.zeros_like(row_block),
        gathered,
    )
    hot_out = hot_scatter(X, Z, C, hot_answer)
    combined = gate_weights[:, 0:1] * hot_out.astype(jnp.float32) + jnp.sum(
        gate_weights[:, 1:, None] * picked.astype(jnp.float32), axis=1
    )
    return combined.astype(jnp.bfloat16)


def solution(mesh):
    X, Z, C = torus_shape(mesh)
    in_specs = (
        P(("dp", "expert"), None),
        P(("dp", "expert"), None),
        P(("dp", "expert"), None),
        P("expert", None, None),
        P("expert", None, None),
        P("expert", None, None),
    )
    out_specs = P(("dp", "expert"), None)
    return jax.shard_map(functools.partial(shards, X, Z, C), mesh=mesh, in_specs=in_specs, out_specs=out_specs, check_vma=False)
```

```python
import functools

import jax
import jax.numpy as jnp
from jax import lax
from jax.experimental import pallas as pl
from jax.experimental.pallas import tpu as pltpu
from jax.sharding import PartitionSpec as P

MESH = pl.DeviceIdType.MESH


def feed_forward(row_block, gate_w, up_w, down_w):
    gate_part = jnp.dot(row_block, gate_w, preferred_element_type=jnp.float32)
    up_part = jnp.dot(row_block, up_w, preferred_element_type=jnp.float32)
    hidden = lax.optimization_barrier((jax.nn.silu(gate_part) * up_part).astype(jnp.bfloat16))
    return jnp.dot(hidden, down_w, preferred_element_type=jnp.float32).astype(jnp.bfloat16)


def torus_shape(mesh):
    n = mesh.shape["expert"]
    try:
        row = mesh.devices.reshape(-1, n)[0]
        xs = {d.coords[0] for d in row}
        zs = {d.coords[2] for d in row}
        X, Z = len(xs), len(zs)
        C = n // (X * Z)
        if X * Z * C != n:
            raise ValueError
    except Exception:
        X, Z, C = 4, 8, 2
        if X * Z * C != n:
            X, Z, C = 1, n // 2, 2
    return X, Z, C


def coordinates(X, Z, C):
    e = lax.axis_index("expert")
    return e // (Z * C), (e // C) % Z, e % C


def wrap(v, n):
    return (v + 4 * n) % n


def device(X, Z, C, x, z, c):
    return {"expert": wrap(x, X) * (Z * C) + wrap(z, Z) * C + wrap(c, C)}


def peers(X, Z, C, x, z, c):
    out = [(x + k, z, c) for k in range(1, X)]
    if Z > 1:
        out.append((x, z + 1, c))
        if Z > 2:
            out.append((x, z - 1, c))
    if C > 1:
        out.append((x, z, c + 1))
    return out


def barrier(X, Z, C, x, z, c):
    sem = pltpu.get_barrier_semaphore()
    targets = peers(X, Z, C, x, z, c)
    for t in targets:
        pl.semaphore_signal(sem, inc=1, device_id=device(X, Z, C, *t), device_id_type=MESH)
    pl.semaphore_wait(sem, len(targets))


def barrier_all():
    n = lax.axis_size("expert")
    me = lax.axis_index("expert")
    sem = pltpu.get_barrier_semaphore()

    def signal(k, carry):
        pl.semaphore_signal(sem, inc=1, device_id={"expert": (me + k) % n}, device_id_type=MESH)
        return carry

    lax.fori_loop(1, n, signal, 0)
    pl.semaphore_wait(sem, n - 1)


def exchange_copy(src_ref, dst_ref, k, send_sem, recv_sem):
    n = lax.axis_size("expert")
    me = lax.axis_index("expert")
    target = (me + k) % n
    return pltpu.make_async_remote_copy(
        src_ref=src_ref.at[target], dst_ref=dst_ref.at[me], send_sem=send_sem.at[k - 1], recv_sem=recv_sem.at[k - 1],
        device_id={"expert": target}, device_id_type=MESH)


def exchange(src_ref, dst_ref, own_sem, send_sem, recv_sem):
    n = lax.axis_size("expert")
    me = lax.axis_index("expert")
    own = pltpu.make_async_copy(src_ref.at[me], dst_ref.at[me], own_sem)
    own.start()

    def start(k, carry):
        exchange_copy(src_ref, dst_ref, k, send_sem, recv_sem).start()
        return carry

    lax.fori_loop(1, n, start, 0)
    return own


def exchange_wait(src_ref, dst_ref, own, send_sem, recv_sem):
    n = lax.axis_size("expert")
    own.wait()

    def wait(k, carry):
        cp = exchange_copy(src_ref, dst_ref, k, send_sem, recv_sem)
        cp.wait_recv()
        cp.wait_send()
        return carry

    lax.fori_loop(1, n, wait, 0)


def gather_kernel(X, Z, C, tok_ref, cold_ref, out_ref, cold_out, own_sem, cs_send, cs_recv, sx_send, sx_recv, sp_send, sp_recv, sm_send, sm_recv, sc_send, sc_recv):
    x, z, c = coordinates(X, Z, C)
    zp, zm = Z // 2, (Z - 1) // 2
    dirn = 1 - 2 * (c % 2)
    barrier_all()
    cold_own = exchange(cold_ref, cold_out, own_sem.at[1], cs_send, cs_recv)

    own = pltpu.make_async_copy(tok_ref, out_ref.at[c, z, x], own_sem.at[0])
    own.start()
    xcopies = []
    for k in range(1, X):
        cp = pltpu.make_async_remote_copy(
            src_ref=tok_ref, dst_ref=out_ref.at[c, z, x], send_sem=sx_send.at[k - 1], recv_sem=sx_recv.at[k - 1],
            device_id=device(X, Z, C, x + k, z, c), device_id_type=MESH)
        cp.start()
        xcopies.append(cp)
    own.wait()
    for cp in xcopies:
        cp.wait_recv()

    ccopies = []

    def to_partner(j, blk):
        if C == 1:
            return
        cp = pltpu.make_async_remote_copy(
            src_ref=out_ref.at[c, blk], dst_ref=out_ref.at[c, blk], send_sem=sc_send.at[j], recv_sem=sc_recv.at[j],
            device_id=device(X, Z, C, x, z, c + 1), device_id_type=MESH)
        cp.start()
        ccopies.append(cp)

    to_partner(0, z)
    plus, minus = [], []
    for s in range(max(zp, zm)):
        if s < zp:
            if s >= 1:
                plus[s - 1].wait_recv()
                to_partner(s, wrap(z - s * dirn, Z))
            cp = pltpu.make_async_remote_copy(
                src_ref=out_ref.at[c, wrap(z - s * dirn, Z)], dst_ref=out_ref.at[c, wrap(z - s * dirn, Z)], send_sem=sp_send.at[s],
                recv_sem=sp_recv.at[s], device_id=device(X, Z, C, x, z + dirn, c), device_id_type=MESH)
            cp.start()
            plus.append(cp)
        if s < zm:
            if s >= 1:
                minus[s - 1].wait_recv()
                to_partner(zp + s, wrap(z + s * dirn, Z))
            cp = pltpu.make_async_remote_copy(
                src_ref=out_ref.at[c, wrap(z + s * dirn, Z)], dst_ref=out_ref.at[c, wrap(z + s * dirn, Z)], send_sem=sm_send.at[s],
                recv_sem=sm_recv.at[s], device_id=device(X, Z, C, x, z - dirn, c), device_id_type=MESH)
            cp.start()
            minus.append(cp)
    if zp:
        plus[zp - 1].wait_recv()
        to_partner(zp, wrap(z - zp * dirn, Z))
    if zm:
        minus[zm - 1].wait_recv()
        to_partner(zp + zm, wrap(z + zm * dirn, Z))
    for cp in ccopies:
        cp.wait_recv()
    for cp in xcopies + plus + minus + ccopies:
        cp.wait_send()
    exchange_wait(cold_ref, cold_out, cold_own, cs_send, cs_recv)


def scatter_kernel(X, Z, C, o_ref, cold_ref, out_ref, cold_out, own_sem, cs_send, cs_recv, pbuf, plus_buf, plus_send, minus_buf, minus_send, xbuf, xsend,
                   sc_send, sc_recv, sp_send, sp_recv, sm_send, sm_recv, sx_send, sx_recv):
    x, z, c = coordinates(X, Z, C)
    zp, zm = Z // 2, (Z - 1) // 2
    dirn = 1 - 2 * (c % 2)
    barrier_all()
    cold_own = exchange(cold_ref, cold_out, own_sem.at[0], cs_send, cs_recv)

    ccopies = []
    if C > 1:
        for blk in range(Z):
            cp = pltpu.make_async_remote_copy(
                src_ref=o_ref.at[(c + 1) % C, blk], dst_ref=pbuf.at[blk], send_sem=sc_send.at[blk], recv_sem=sc_recv.at[blk],
                device_id=device(X, Z, C, x, z, c + 1), device_id_type=MESH)
            cp.start()
            ccopies.append(cp)

    def chip_sum(blk):
        val = o_ref[c, blk].astype(jnp.float32)
        if C > 1:
            val = val + pbuf[blk].astype(jnp.float32)
        return val

    if C > 1:
        for cp in ccopies:
            cp.wait_recv()

    plus, minus = [], []
    for s in range(max(zp, zm)):
        if s < zp:
            val = chip_sum(wrap(z + (zp - s) * dirn, Z))
            if s >= 1:
                plus[s - 1].wait_recv()
                val = val + plus_buf[s - 1].astype(jnp.float32)
            plus_send[s] = val.astype(jnp.bfloat16)
            cp = pltpu.make_async_remote_copy(
                src_ref=plus_send.at[s], dst_ref=plus_buf.at[s], send_sem=sp_send.at[s], recv_sem=sp_recv.at[s],
                device_id=device(X, Z, C, x, z + dirn, c), device_id_type=MESH)
            cp.start()
            plus.append(cp)
        if s < zm:
            val = chip_sum(wrap(z - (zm - s) * dirn, Z))
            if s >= 1:
                minus[s - 1].wait_recv()
                val = val + minus_buf[s - 1].astype(jnp.float32)
            minus_send[s] = val.astype(jnp.bfloat16)
            cp = pltpu.make_async_remote_copy(
                src_ref=minus_send.at[s], dst_ref=minus_buf.at[s], send_sem=sm_send.at[s], recv_sem=sm_recv.at[s],
                device_id=device(X, Z, C, x, z - dirn, c), device_id_type=MESH)
            cp.start()
            minus.append(cp)
    total = chip_sum(z)
    if zp:
        plus[zp - 1].wait_recv()
        total = total + plus_buf[zp - 1].astype(jnp.float32)
    if zm:
        minus[zm - 1].wait_recv()
        total = total + minus_buf[zm - 1].astype(jnp.float32)
    xsend[...] = total.astype(jnp.bfloat16)
    xcopies = []
    for k in range(1, X):
        cp = pltpu.make_async_remote_copy(
            src_ref=xsend.at[(x + k) % X], dst_ref=xbuf.at[k - 1], send_sem=sx_send.at[k - 1], recv_sem=sx_recv.at[k - 1],
            device_id=device(X, Z, C, x + k, z, c), device_id_type=MESH)
        cp.start()
        xcopies.append(cp)
    result = xsend[x].astype(jnp.float32)
    for k, cp in enumerate(xcopies):
        cp.wait_recv()
        result = result + xbuf[k].astype(jnp.float32)
    out_ref[...] = result.astype(out_ref.dtype)
    for cp in ccopies + plus + minus + xcopies:
        cp.wait_send()
    exchange_wait(cold_ref, cold_out, cold_own, cs_send, cs_recv)


def hot_gather(X, Z, C, tokens, outgoing):
    R, D = tokens.shape
    zp, zm = Z // 2, (Z - 1) // 2
    n = outgoing.shape[0]
    dma = pltpu.SemaphoreType.DMA
    vmem = pl.BlockSpec(memory_space=pltpu.VMEM)
    return pl.pallas_call(
        functools.partial(gather_kernel, X, Z, C),
        out_shape=(jax.ShapeDtypeStruct((C, Z, X, R, D), tokens.dtype), jax.ShapeDtypeStruct(outgoing.shape, outgoing.dtype)),
        in_specs=[vmem, vmem],
        out_specs=(vmem, vmem),
        scratch_shapes=[
            dma((2,)), dma((n - 1,)), dma((n - 1,)),
            dma((max(X - 1, 1),)), dma((max(X - 1, 1),)),
            dma((max(zp, 1),)), dma((max(zp, 1),)),
            dma((max(zm, 1),)), dma((max(zm, 1),)),
            dma((Z,)), dma((Z,)),
        ],
        compiler_params=pltpu.CompilerParams(collective_id=0, has_side_effects=True),
    )(tokens, outgoing)


def hot_scatter(X, Z, C, answered, cold_answered):
    _, _, _, R, D = answered.shape
    zp, zm = Z // 2, (Z - 1) // 2
    n = cold_answered.shape[0]
    dma = pltpu.SemaphoreType.DMA
    bf = answered.dtype
    vmem = pl.BlockSpec(memory_space=pltpu.VMEM)
    return pl.pallas_call(
        functools.partial(scatter_kernel, X, Z, C),
        out_shape=(jax.ShapeDtypeStruct((R, D), bf), jax.ShapeDtypeStruct(cold_answered.shape, cold_answered.dtype)),
        in_specs=[vmem, vmem],
        out_specs=(vmem, vmem),
        scratch_shapes=[
            dma((1,)), dma((n - 1,)), dma((n - 1,)),
            pltpu.VMEM((Z, X, R, D), bf),
            pltpu.VMEM((max(zp, 1), X, R, D), bf), pltpu.VMEM((max(zp, 1), X, R, D), bf),
            pltpu.VMEM((max(zm, 1), X, R, D), bf), pltpu.VMEM((max(zm, 1), X, R, D), bf),
            pltpu.VMEM((max(X - 1, 1), R, D), bf), pltpu.VMEM((X, R, D), bf),
            dma((Z,)), dma((Z,)),
            dma((max(zp, 1),)), dma((max(zp, 1),)),
            dma((max(zm, 1),)), dma((max(zm, 1),)),
            dma((max(X - 1, 1),)), dma((max(X - 1, 1),)),
        ],
        compiler_params=pltpu.CompilerParams(collective_id=1, has_side_effects=True),
    )(answered, cold_answered)


def shards(X, Z, C, tokens, routes, gate_weights, w_gate, w_up, w_down):
    devices = lax.axis_size("expert")
    experts = w_gate.shape[0] * devices
    row_count = routes.shape[0]
    top_count = routes.shape[1]
    model_width = tokens.shape[1]
    slot_count = (row_count * (top_count - 1) + experts - 2) // (experts - 1)
    cold_ids = routes[:, 1:]
    flat_ids = cold_ids.reshape(-1)
    expert_iota = jnp.arange(experts, dtype=jnp.int32)
    one_hot = (flat_ids[:, None] == expert_iota[None, :]).astype(jnp.int32)
    slot_rank = (jnp.sum(jnp.cumsum(one_hot, axis=0) * one_hot, axis=1) - 1).reshape(cold_ids.shape)
    slot_iota = jnp.arange(slot_count, dtype=jnp.int32)
    select = (cold_ids[:, :, None, None] == expert_iota[None, None, :, None]) & (
        slot_rank[:, :, None, None] == slot_iota[None, None, None, :]
    )
    placing = jnp.sum(select.astype(jnp.bfloat16), axis=1)
    outgoing = jnp.einsum(
        "res,rd->esd", placing, tokens, preferred_element_type=jnp.float32
    ).astype(jnp.bfloat16)
    local_gate = w_gate[0]
    local_up = w_up[0]
    local_down = w_down[0]
    hot_expert = routes[0, 0]
    is_owner = lax.axis_index("expert") == hot_expert
    gathered, arrived = hot_gather(X, Z, C, tokens, outgoing)
    flat_rows = arrived.reshape(-1, model_width)
    answered = feed_forward(flat_rows, local_gate, local_up, local_down).reshape(arrived.shape)
    hot_answer = lax.cond(
        is_owner,
        lambda row_block: feed_forward(row_block.reshape(-1, model_width), local_gate, local_up, local_down).reshape(row_block.shape),
        lambda row_block: jnp.zeros_like(row_block),
        gathered,
    )
    hot_out, returned = hot_scatter(X, Z, C, hot_answer, answered)
    picked = returned.reshape(-1, model_width)[cold_ids * slot_count + slot_rank]
    combined = gate_weights[:, 0:1] * hot_out.astype(jnp.float32) + jnp.sum(
        gate_weights[:, 1:, None] * picked.astype(jnp.float32), axis=1
    )
    return combined.astype(jnp.bfloat16)


def solution(mesh):
    X, Z, C = torus_shape(mesh)
    in_specs = (
        P(("dp", "expert"), None),
        P(("dp", "expert"), None),
        P(("dp", "expert"), None),
        P("expert", None, None),
        P("expert", None, None),
        P("expert", None, None),
    )
    out_specs = P(("dp", "expert"), None)
    return jax.shard_map(functools.partial(shards, X, Z, C), mesh=mesh, in_specs=in_specs, out_specs=out_specs, check_vma=False)
```

```python
import functools

import jax
import jax.numpy as jnp
from jax import lax
from jax.experimental import pallas as pl
from jax.experimental.pallas import tpu as pltpu
from jax.sharding import PartitionSpec as P

MESH = pl.DeviceIdType.MESH


def feed_forward(row_block, gate_w, up_w, down_w):
    gate_part = jnp.dot(row_block, gate_w, preferred_element_type=jnp.float32)
    up_part = jnp.dot(row_block, up_w, preferred_element_type=jnp.float32)
    hidden = lax.optimization_barrier((jax.nn.silu(gate_part) * up_part).astype(jnp.bfloat16))
    return jnp.dot(hidden, down_w, preferred_element_type=jnp.float32).astype(jnp.bfloat16)


def torus_shape(mesh):
    n = mesh.shape["expert"]
    try:
        row = mesh.devices.reshape(-1, n)[0]
        xs = {d.coords[0] for d in row}
        zs = {d.coords[2] for d in row}
        X, Z = len(xs), len(zs)
        C = n // (X * Z)
        if X * Z * C != n:
            raise ValueError
    except Exception:
        X, Z, C = 4, 8, 2
        if X * Z * C != n:
            X, Z, C = 1, n // 2, 2
    return X, Z, C


def coordinates(X, Z, C):
    e = lax.axis_index("expert")
    return e // (Z * C), (e // C) % Z, e % C


def wrap(v, n):
    return (v + 4 * n) % n


def device(X, Z, C, x, z, c):
    return {"expert": wrap(x, X) * (Z * C) + wrap(z, Z) * C + wrap(c, C)}


def peers(X, Z, C, x, z, c):
    out = [(x + k, z, c) for k in range(1, X)]
    if Z > 1:
        out.append((x, z + 1, c))
        if Z > 2:
            out.append((x, z - 1, c))
    if C > 1:
        out.append((x, z, c + 1))
    return out


def barrier(X, Z, C, x, z, c):
    sem = pltpu.get_barrier_semaphore()
    targets = peers(X, Z, C, x, z, c)
    for t in targets:
        pl.semaphore_signal(sem, inc=1, device_id=device(X, Z, C, *t), device_id_type=MESH)
    pl.semaphore_wait(sem, len(targets))


def barrier_all():
    n = lax.axis_size("expert")
    me = lax.axis_index("expert")
    sem = pltpu.get_barrier_semaphore()

    def signal(k, carry):
        pl.semaphore_signal(sem, inc=1, device_id={"expert": (me + k) % n}, device_id_type=MESH)
        return carry

    lax.fori_loop(1, n, signal, 0)
    pl.semaphore_wait(sem, n - 1)


def exchange_copy(src_ref, dst_ref, k, send_sem, recv_sem):
    n = lax.axis_size("expert")
    me = lax.axis_index("expert")
    target = (me + k) % n
    return pltpu.make_async_remote_copy(
        src_ref=src_ref.at[target], dst_ref=dst_ref.at[me], send_sem=send_sem.at[k - 1], recv_sem=recv_sem.at[k - 1],
        device_id={"expert": target}, device_id_type=MESH)


def exchange(src_ref, dst_ref, own_sem, send_sem, recv_sem):
    n = lax.axis_size("expert")
    me = lax.axis_index("expert")
    own = pltpu.make_async_copy(src_ref.at[me], dst_ref.at[me], own_sem)
    own.start()

    def start(k, carry):
        exchange_copy(src_ref, dst_ref, k, send_sem, recv_sem).start()
        return carry

    lax.fori_loop(1, n, start, 0)
    return own


def exchange_wait(src_ref, dst_ref, own, send_sem, recv_sem):
    n = lax.axis_size("expert")
    own.wait()

    def wait(k, carry):
        cp = exchange_copy(src_ref, dst_ref, k, send_sem, recv_sem)
        cp.wait_recv()
        cp.wait_send()
        return carry

    lax.fori_loop(1, n, wait, 0)


def gather_kernel(X, Z, C, tok_ref, cold_ref, out_ref, cold_out, own_sem, cs_send, cs_recv, sx_send, sx_recv, sp_send, sp_recv, sm_send, sm_recv, sc_send, sc_recv):
    x, z, c = coordinates(X, Z, C)
    zp, zm = Z // 2, (Z - 1) // 2
    dirn = 1 - 2 * (c % 2)
    barrier_all()
    cold_own = exchange(cold_ref, cold_out, own_sem.at[1], cs_send, cs_recv)

    own = pltpu.make_async_copy(tok_ref, out_ref.at[c, z, x], own_sem.at[0])
    own.start()
    xcopies = []
    for k in range(1, X):
        cp = pltpu.make_async_remote_copy(
            src_ref=tok_ref, dst_ref=out_ref.at[c, z, x], send_sem=sx_send.at[k - 1], recv_sem=sx_recv.at[k - 1],
            device_id=device(X, Z, C, x + k, z, c), device_id_type=MESH)
        cp.start()
        xcopies.append(cp)
    own.wait()
    for cp in xcopies:
        cp.wait_recv()

    ccopies = []

    def to_partner(j, blk):
        if C == 1:
            return
        cp = pltpu.make_async_remote_copy(
            src_ref=out_ref.at[c, blk], dst_ref=out_ref.at[c, blk], send_sem=sc_send.at[j], recv_sem=sc_recv.at[j],
            device_id=device(X, Z, C, x, z, c + 1), device_id_type=MESH)
        cp.start()
        ccopies.append(cp)

    to_partner(0, z)
    plus, minus = [], []
    for s in range(max(zp, zm)):
        if s < zp:
            if s >= 1:
                plus[s - 1].wait_recv()
                to_partner(s, wrap(z - s * dirn, Z))
            cp = pltpu.make_async_remote_copy(
                src_ref=out_ref.at[c, wrap(z - s * dirn, Z)], dst_ref=out_ref.at[c, wrap(z - s * dirn, Z)], send_sem=sp_send.at[s],
                recv_sem=sp_recv.at[s], device_id=device(X, Z, C, x, z + dirn, c), device_id_type=MESH)
            cp.start()
            plus.append(cp)
        if s < zm:
            if s >= 1:
                minus[s - 1].wait_recv()
                to_partner(zp + s, wrap(z + s * dirn, Z))
            cp = pltpu.make_async_remote_copy(
                src_ref=out_ref.at[c, wrap(z + s * dirn, Z)], dst_ref=out_ref.at[c, wrap(z + s * dirn, Z)], send_sem=sm_send.at[s],
                recv_sem=sm_recv.at[s], device_id=device(X, Z, C, x, z - dirn, c), device_id_type=MESH)
            cp.start()
            minus.append(cp)
    if zp:
        plus[zp - 1].wait_recv()
        to_partner(zp, wrap(z - zp * dirn, Z))
    if zm:
        minus[zm - 1].wait_recv()
        to_partner(zp + zm, wrap(z + zm * dirn, Z))
    for cp in ccopies:
        cp.wait_recv()
    for cp in xcopies + plus + minus + ccopies:
        cp.wait_send()
    exchange_wait(cold_ref, cold_out, cold_own, cs_send, cs_recv)


def scatter_kernel(X, Z, C, o_ref, cold_ref, out_ref, cold_out, own_sem, cs_send, cs_recv, pbuf, plus_buf, plus_send, minus_buf, minus_send, xbuf, xsend,
                   sc_send, sc_recv, sp_send, sp_recv, sm_send, sm_recv, sx_send, sx_recv):
    x, z, c = coordinates(X, Z, C)
    zp, zm = Z // 2, (Z - 1) // 2
    dirn = 1 - 2 * (c % 2)
    barrier_all()
    cold_own = exchange(cold_ref, cold_out, own_sem.at[0], cs_send, cs_recv)

    ccopies = []
    if C > 1:
        for blk in range(Z):
            cp = pltpu.make_async_remote_copy(
                src_ref=o_ref.at[(c + 1) % C, blk], dst_ref=pbuf.at[blk], send_sem=sc_send.at[blk], recv_sem=sc_recv.at[blk],
                device_id=device(X, Z, C, x, z, c + 1), device_id_type=MESH)
            cp.start()
            ccopies.append(cp)

    def chip_sum(blk):
        val = o_ref[c, blk].astype(jnp.float32)
        if C > 1:
            pltpu.make_async_remote_copy(
                src_ref=o_ref.at[(c + 1) % C, blk], dst_ref=pbuf.at[blk], send_sem=sc_send.at[blk], recv_sem=sc_recv.at[blk],
                device_id=device(X, Z, C, x, z, c + 1), device_id_type=MESH).wait_recv()
            val = val + pbuf[blk].astype(jnp.float32)
        return val

    plus, minus = [], []
    for s in range(max(zp, zm)):
        if s < zp:
            val = chip_sum(wrap(z + (zp - s) * dirn, Z))
            if s >= 1:
                plus[s - 1].wait_recv()
                val = val + plus_buf[s - 1].astype(jnp.float32)
            plus_send[s] = val.astype(jnp.bfloat16)
            cp = pltpu.make_async_remote_copy(
                src_ref=plus_send.at[s], dst_ref=plus_buf.at[s], send_sem=sp_send.at[s], recv_sem=sp_recv.at[s],
                device_id=device(X, Z, C, x, z + dirn, c), device_id_type=MESH)
            cp.start()
            plus.append(cp)
        if s < zm:
            val = chip_sum(wrap(z - (zm - s) * dirn, Z))
            if s >= 1:
                minus[s - 1].wait_recv()
                val = val + minus_buf[s - 1].astype(jnp.float32)
            minus_send[s] = val.astype(jnp.bfloat16)
            cp = pltpu.make_async_remote_copy(
                src_ref=minus_send.at[s], dst_ref=minus_buf.at[s], send_sem=sm_send.at[s], recv_sem=sm_recv.at[s],
                device_id=device(X, Z, C, x, z - dirn, c), device_id_type=MESH)
            cp.start()
            minus.append(cp)
    total = chip_sum(z)
    if zp:
        plus[zp - 1].wait_recv()
        total = total + plus_buf[zp - 1].astype(jnp.float32)
    if zm:
        minus[zm - 1].wait_recv()
        total = total + minus_buf[zm - 1].astype(jnp.float32)
    xsend[...] = total.astype(jnp.bfloat16)
    xcopies = []
    for k in range(1, X):
        cp = pltpu.make_async_remote_copy(
            src_ref=xsend.at[(x + k) % X], dst_ref=xbuf.at[k - 1], send_sem=sx_send.at[k - 1], recv_sem=sx_recv.at[k - 1],
            device_id=device(X, Z, C, x + k, z, c), device_id_type=MESH)
        cp.start()
        xcopies.append(cp)
    result = xsend[x].astype(jnp.float32)
    for k, cp in enumerate(xcopies):
        cp.wait_recv()
        result = result + xbuf[k].astype(jnp.float32)
    out_ref[...] = result.astype(out_ref.dtype)
    for cp in ccopies + plus + minus + xcopies:
        cp.wait_send()
    exchange_wait(cold_ref, cold_out, cold_own, cs_send, cs_recv)


def hot_gather(X, Z, C, tokens, outgoing):
    R, D = tokens.shape
    zp, zm = Z // 2, (Z - 1) // 2
    n = outgoing.shape[0]
    dma = pltpu.SemaphoreType.DMA
    vmem = pl.BlockSpec(memory_space=pltpu.VMEM)
    return pl.pallas_call(
        functools.partial(gather_kernel, X, Z, C),
        out_shape=(jax.ShapeDtypeStruct((C, Z, X, R, D), tokens.dtype), jax.ShapeDtypeStruct(outgoing.shape, outgoing.dtype)),
        in_specs=[vmem, vmem],
        out_specs=(vmem, vmem),
        scratch_shapes=[
            dma((2,)), dma((n - 1,)), dma((n - 1,)),
            dma((max(X - 1, 1),)), dma((max(X - 1, 1),)),
            dma((max(zp, 1),)), dma((max(zp, 1),)),
            dma((max(zm, 1),)), dma((max(zm, 1),)),
            dma((Z,)), dma((Z,)),
        ],
        compiler_params=pltpu.CompilerParams(collective_id=0, has_side_effects=True),
    )(tokens, outgoing)


def hot_scatter(X, Z, C, answered, cold_answered):
    _, _, _, R, D = answered.shape
    zp, zm = Z // 2, (Z - 1) // 2
    n = cold_answered.shape[0]
    dma = pltpu.SemaphoreType.DMA
    bf = answered.dtype
    vmem = pl.BlockSpec(memory_space=pltpu.VMEM)
    return pl.pallas_call(
        functools.partial(scatter_kernel, X, Z, C),
        out_shape=(jax.ShapeDtypeStruct((R, D), bf), jax.ShapeDtypeStruct(cold_answered.shape, cold_answered.dtype)),
        in_specs=[vmem, vmem],
        out_specs=(vmem, vmem),
        scratch_shapes=[
            dma((1,)), dma((n - 1,)), dma((n - 1,)),
            pltpu.VMEM((Z, X, R, D), bf),
            pltpu.VMEM((max(zp, 1), X, R, D), bf), pltpu.VMEM((max(zp, 1), X, R, D), bf),
            pltpu.VMEM((max(zm, 1), X, R, D), bf), pltpu.VMEM((max(zm, 1), X, R, D), bf),
            pltpu.VMEM((max(X - 1, 1), R, D), bf), pltpu.VMEM((X, R, D), bf),
            dma((Z,)), dma((Z,)),
            dma((max(zp, 1),)), dma((max(zp, 1),)),
            dma((max(zm, 1),)), dma((max(zm, 1),)),
            dma((max(X - 1, 1),)), dma((max(X - 1, 1),)),
        ],
        compiler_params=pltpu.CompilerParams(collective_id=1, has_side_effects=True),
    )(answered, cold_answered)


def shards(X, Z, C, tokens, routes, gate_weights, w_gate, w_up, w_down):
    devices = lax.axis_size("expert")
    experts = w_gate.shape[0] * devices
    row_count = routes.shape[0]
    top_count = routes.shape[1]
    model_width = tokens.shape[1]
    slot_count = (row_count * (top_count - 1) + experts - 2) // (experts - 1)
    cold_ids = routes[:, 1:]
    flat_ids = cold_ids.reshape(-1)
    expert_iota = jnp.arange(experts, dtype=jnp.int32)
    one_hot = (flat_ids[:, None] == expert_iota[None, :]).astype(jnp.int32)
    slot_rank = (jnp.sum(jnp.cumsum(one_hot, axis=0) * one_hot, axis=1) - 1).reshape(cold_ids.shape)
    slot_iota = jnp.arange(slot_count, dtype=jnp.int32)
    select = (cold_ids[:, :, None, None] == expert_iota[None, None, :, None]) & (
        slot_rank[:, :, None, None] == slot_iota[None, None, None, :]
    )
    placing = jnp.sum(select.astype(jnp.bfloat16), axis=1)
    outgoing = jnp.einsum(
        "res,rd->esd", placing, tokens, preferred_element_type=jnp.float32
    ).astype(jnp.bfloat16)
    local_gate = w_gate.reshape(w_gate.shape[1:])
    local_up = w_up.reshape(w_up.shape[1:])
    local_down = w_down.reshape(w_down.shape[1:])
    hot_expert = routes[0, 0]
    is_owner = lax.axis_index("expert") == hot_expert
    gathered, arrived = hot_gather(X, Z, C, tokens, outgoing)
    flat_rows = arrived.reshape(-1, model_width)
    answered = feed_forward(flat_rows, local_gate, local_up, local_down).reshape(arrived.shape)
    hot_answer = lax.cond(
        is_owner,
        lambda row_block: feed_forward(row_block.reshape(-1, model_width), local_gate, local_up, local_down).reshape(row_block.shape),
        lambda row_block: jnp.zeros_like(row_block),
        gathered,
    )
    hot_out, returned = hot_scatter(X, Z, C, hot_answer, answered)
    picked = returned.reshape(-1, model_width)[cold_ids * slot_count + slot_rank]
    combined = gate_weights[:, 0:1] * hot_out.astype(jnp.float32) + jnp.sum(
        gate_weights[:, 1:, None] * picked.astype(jnp.float32), axis=1
    )
    return combined.astype(jnp.bfloat16)


def solution(mesh):
    X, Z, C = torus_shape(mesh)
    in_specs = (
        P(("dp", "expert"), None),
        P(("dp", "expert"), None),
        P(("dp", "expert"), None),
        P("expert", None, None),
        P("expert", None, None),
        P("expert", None, None),
    )
    out_specs = P(("dp", "expert"), None)
    return jax.shard_map(functools.partial(shards, X, Z, C), mesh=mesh, in_specs=in_specs, out_specs=out_specs, check_vma=False)
```

```python
import functools

import jax
import jax.numpy as jnp
from jax import lax
from jax.experimental import pallas as pl
from jax.experimental.pallas import tpu as pltpu
from jax.sharding import PartitionSpec as P

MESH = pl.DeviceIdType.MESH


def feed_forward(row_block, gate_w, up_w, down_w):
    gate_part = jnp.dot(row_block, gate_w, preferred_element_type=jnp.float32)
    up_part = jnp.dot(row_block, up_w, preferred_element_type=jnp.float32)
    hidden = lax.optimization_barrier((jax.nn.silu(gate_part) * up_part).astype(jnp.bfloat16))
    return jnp.dot(hidden, down_w, preferred_element_type=jnp.float32).astype(jnp.bfloat16)


def torus_shape(mesh):
    n = mesh.shape["expert"]
    try:
        row = mesh.devices.reshape(-1, n)[0]
        xs = {d.coords[0] for d in row}
        zs = {d.coords[2] for d in row}
        X, Z = len(xs), len(zs)
        C = n // (X * Z)
        if X * Z * C != n:
            raise ValueError
    except Exception:
        X, Z, C = 4, 8, 2
        if X * Z * C != n:
            X, Z, C = 1, n // 2, 2
    return X, Z, C


def coordinates(X, Z, C):
    e = lax.axis_index("expert")
    return e // (Z * C), (e // C) % Z, e % C


def wrap(v, n):
    return (v + 4 * n) % n


def device(X, Z, C, x, z, c):
    return {"expert": wrap(x, X) * (Z * C) + wrap(z, Z) * C + wrap(c, C)}


def peers(X, Z, C, x, z, c):
    out = [(x + k, z, c) for k in range(1, X)]
    if Z > 1:
        out.append((x, z + 1, c))
        if Z > 2:
            out.append((x, z - 1, c))
    if C > 1:
        out.append((x, z, c + 1))
    return out


def barrier(X, Z, C, x, z, c):
    sem = pltpu.get_barrier_semaphore()
    targets = peers(X, Z, C, x, z, c)
    for t in targets:
        pl.semaphore_signal(sem, inc=1, device_id=device(X, Z, C, *t), device_id_type=MESH)
    pl.semaphore_wait(sem, len(targets))


def barrier_all():
    n = lax.axis_size("expert")
    me = lax.axis_index("expert")
    sem = pltpu.get_barrier_semaphore()

    def signal(k, carry):
        pl.semaphore_signal(sem, inc=1, device_id={"expert": (me + k) % n}, device_id_type=MESH)
        return carry

    lax.fori_loop(1, n, signal, 0)
    pl.semaphore_wait(sem, n - 1)


def exchange_copy(src_ref, dst_ref, k, send_sem, recv_sem):
    n = lax.axis_size("expert")
    me = lax.axis_index("expert")
    target = (me + k) % n
    return pltpu.make_async_remote_copy(
        src_ref=src_ref.at[target], dst_ref=dst_ref.at[me], send_sem=send_sem.at[k - 1], recv_sem=recv_sem.at[k - 1],
        device_id={"expert": target}, device_id_type=MESH)


def exchange(src_ref, dst_ref, own_sem, send_sem, recv_sem):
    n = lax.axis_size("expert")
    me = lax.axis_index("expert")
    own = pltpu.make_async_copy(src_ref.at[me], dst_ref.at[me], own_sem)
    own.start()

    def start(k, carry):
        exchange_copy(src_ref, dst_ref, k, send_sem, recv_sem).start()
        return carry

    lax.fori_loop(1, n, start, 0)
    return own


def exchange_wait(src_ref, dst_ref, own, send_sem, recv_sem):
    n = lax.axis_size("expert")
    own.wait()

    def wait(k, carry):
        cp = exchange_copy(src_ref, dst_ref, k, send_sem, recv_sem)
        cp.wait_recv()
        cp.wait_send()
        return carry

    lax.fori_loop(1, n, wait, 0)


def gather_kernel(X, Z, C, tok_ref, cold_ref, wg_ref, wu_ref, wd_ref, out_ref, cold_out, pg_ref, pu_ref, pd_ref,
                  own_sem, cs_send, cs_recv, w_send, w_recv, sx_send, sx_recv, sp_send, sp_recv, sm_send, sm_recv):
    x, z, c = coordinates(X, Z, C)
    zp, zm = Z // 2, (Z - 1) // 2
    dirn = 1 - 2 * (c % 2)
    barrier_all()
    wcopies = []
    if C > 1:
        for j, (src, dst) in enumerate(((wg_ref, pg_ref), (wu_ref, pu_ref), (wd_ref, pd_ref))):
            cp = pltpu.make_async_remote_copy(
                src_ref=src, dst_ref=dst, send_sem=w_send.at[j], recv_sem=w_recv.at[j],
                device_id=device(X, Z, C, x, z, c + 1), device_id_type=MESH)
            cp.start()
            wcopies.append(cp)
    cold_own = exchange(cold_ref, cold_out, own_sem.at[1], cs_send, cs_recv)

    own = pltpu.make_async_copy(tok_ref, out_ref.at[z, x], own_sem.at[0])
    own.start()
    xcopies = []
    for k in range(1, X):
        cp = pltpu.make_async_remote_copy(
            src_ref=tok_ref, dst_ref=out_ref.at[z, x], send_sem=sx_send.at[k - 1], recv_sem=sx_recv.at[k - 1],
            device_id=device(X, Z, C, x + k, z, c), device_id_type=MESH)
        cp.start()
        xcopies.append(cp)
    own.wait()
    for cp in xcopies:
        cp.wait_recv()

    plus, minus = [], []
    for s in range(max(zp, zm)):
        if s < zp:
            if s >= 1:
                plus[s - 1].wait_recv()
            blk = wrap(z - s * dirn, Z)
            cp = pltpu.make_async_remote_copy(
                src_ref=out_ref.at[blk], dst_ref=out_ref.at[blk], send_sem=sp_send.at[s],
                recv_sem=sp_recv.at[s], device_id=device(X, Z, C, x, z + dirn, c), device_id_type=MESH)
            cp.start()
            plus.append(cp)
        if s < zm:
            if s >= 1:
                minus[s - 1].wait_recv()
            blk = wrap(z + s * dirn, Z)
            cp = pltpu.make_async_remote_copy(
                src_ref=out_ref.at[blk], dst_ref=out_ref.at[blk], send_sem=sm_send.at[s],
                recv_sem=sm_recv.at[s], device_id=device(X, Z, C, x, z - dirn, c), device_id_type=MESH)
            cp.start()
            minus.append(cp)
    if zp:
        plus[zp - 1].wait_recv()
    if zm:
        minus[zm - 1].wait_recv()
    for cp in xcopies + plus + minus:
        cp.wait_send()
    exchange_wait(cold_ref, cold_out, cold_own, cs_send, cs_recv)
    for cp in wcopies:
        cp.wait_recv()
        cp.wait_send()


def scatter_kernel(X, Z, C, o_ref, cold_ref, out_ref, cold_out, own_sem, cs_send, cs_recv, plus_buf, plus_send, minus_buf, minus_send, xbuf, xsend,
                   sp_send, sp_recv, sm_send, sm_recv, sx_send, sx_recv):
    x, z, c = coordinates(X, Z, C)
    zp, zm = Z // 2, (Z - 1) // 2
    dirn = 1 - 2 * (c % 2)
    barrier_all()
    cold_own = exchange(cold_ref, cold_out, own_sem.at[0], cs_send, cs_recv)

    def chip_sum(blk):
        return o_ref[blk].astype(jnp.float32)

    plus, minus = [], []
    for s in range(max(zp, zm)):
        if s < zp:
            val = chip_sum(wrap(z + (zp - s) * dirn, Z))
            if s >= 1:
                plus[s - 1].wait_recv()
                val = val + plus_buf[s - 1].astype(jnp.float32)
            plus_send[s] = val.astype(jnp.bfloat16)
            cp = pltpu.make_async_remote_copy(
                src_ref=plus_send.at[s], dst_ref=plus_buf.at[s], send_sem=sp_send.at[s], recv_sem=sp_recv.at[s],
                device_id=device(X, Z, C, x, z + dirn, c), device_id_type=MESH)
            cp.start()
            plus.append(cp)
        if s < zm:
            val = chip_sum(wrap(z - (zm - s) * dirn, Z))
            if s >= 1:
                minus[s - 1].wait_recv()
                val = val + minus_buf[s - 1].astype(jnp.float32)
            minus_send[s] = val.astype(jnp.bfloat16)
            cp = pltpu.make_async_remote_copy(
                src_ref=minus_send.at[s], dst_ref=minus_buf.at[s], send_sem=sm_send.at[s], recv_sem=sm_recv.at[s],
                device_id=device(X, Z, C, x, z - dirn, c), device_id_type=MESH)
            cp.start()
            minus.append(cp)
    total = chip_sum(z)
    if zp:
        plus[zp - 1].wait_recv()
        total = total + plus_buf[zp - 1].astype(jnp.float32)
    if zm:
        minus[zm - 1].wait_recv()
        total = total + minus_buf[zm - 1].astype(jnp.float32)
    xsend[...] = total.astype(jnp.bfloat16)
    xcopies = []
    for k in range(1, X):
        cp = pltpu.make_async_remote_copy(
            src_ref=xsend.at[(x + k) % X], dst_ref=xbuf.at[k - 1], send_sem=sx_send.at[k - 1], recv_sem=sx_recv.at[k - 1],
            device_id=device(X, Z, C, x + k, z, c), device_id_type=MESH)
        cp.start()
        xcopies.append(cp)
    result = xsend[x].astype(jnp.float32)
    for k, cp in enumerate(xcopies):
        cp.wait_recv()
        result = result + xbuf[k].astype(jnp.float32)
    out_ref[...] = result.astype(out_ref.dtype)
    for cp in plus + minus + xcopies:
        cp.wait_send()
    exchange_wait(cold_ref, cold_out, cold_own, cs_send, cs_recv)


def hot_gather(X, Z, C, tokens, outgoing, w_gate, w_up, w_down):
    R, D = tokens.shape
    zp, zm = Z // 2, (Z - 1) // 2
    n = outgoing.shape[0]
    dma = pltpu.SemaphoreType.DMA
    vmem = pl.BlockSpec(memory_space=pltpu.VMEM)
    anywhere = pl.BlockSpec(memory_space=pl.ANY)
    return pl.pallas_call(
        functools.partial(gather_kernel, X, Z, C),
        out_shape=(
            jax.ShapeDtypeStruct((Z, X, R, D), tokens.dtype), jax.ShapeDtypeStruct(outgoing.shape, outgoing.dtype),
            jax.ShapeDtypeStruct(w_gate.shape, w_gate.dtype), jax.ShapeDtypeStruct(w_up.shape, w_up.dtype),
            jax.ShapeDtypeStruct(w_down.shape, w_down.dtype),
        ),
        in_specs=[vmem, vmem, anywhere, anywhere, anywhere],
        out_specs=(vmem, vmem, anywhere, anywhere, anywhere),
        scratch_shapes=[
            dma((2,)), dma((n - 1,)), dma((n - 1,)), dma((3,)), dma((3,)),
            dma((max(X - 1, 1),)), dma((max(X - 1, 1),)),
            dma((max(zp, 1),)), dma((max(zp, 1),)),
            dma((max(zm, 1),)), dma((max(zm, 1),)),
        ],
        compiler_params=pltpu.CompilerParams(collective_id=0, has_side_effects=True),
    )(tokens, outgoing, w_gate, w_up, w_down)


def hot_scatter(X, Z, C, answered, cold_answered):
    _, _, R, D = answered.shape
    zp, zm = Z // 2, (Z - 1) // 2
    n = cold_answered.shape[0]
    dma = pltpu.SemaphoreType.DMA
    bf = answered.dtype
    vmem = pl.BlockSpec(memory_space=pltpu.VMEM)
    return pl.pallas_call(
        functools.partial(scatter_kernel, X, Z, C),
        out_shape=(jax.ShapeDtypeStruct((R, D), bf), jax.ShapeDtypeStruct(cold_answered.shape, cold_answered.dtype)),
        in_specs=[vmem, vmem],
        out_specs=(vmem, vmem),
        scratch_shapes=[
            dma((1,)), dma((n - 1,)), dma((n - 1,)),
            pltpu.VMEM((max(zp, 1), X, R, D), bf), pltpu.VMEM((max(zp, 1), X, R, D), bf),
            pltpu.VMEM((max(zm, 1), X, R, D), bf), pltpu.VMEM((max(zm, 1), X, R, D), bf),
            pltpu.VMEM((max(X - 1, 1), R, D), bf), pltpu.VMEM((X, R, D), bf),
            dma((max(zp, 1),)), dma((max(zp, 1),)),
            dma((max(zm, 1),)), dma((max(zm, 1),)),
            dma((max(X - 1, 1),)), dma((max(X - 1, 1),)),
        ],
        compiler_params=pltpu.CompilerParams(collective_id=1, has_side_effects=True),
    )(answered, cold_answered)


def shards(X, Z, C, tokens, routes, gate_weights, w_gate, w_up, w_down):
    devices = lax.axis_size("expert")
    experts = w_gate.shape[0] * devices
    row_count = routes.shape[0]
    top_count = routes.shape[1]
    model_width = tokens.shape[1]
    slot_count = (row_count * (top_count - 1) + experts - 2) // (experts - 1)
    cold_ids = routes[:, 1:]
    flat_ids = cold_ids.reshape(-1)
    expert_iota = jnp.arange(experts, dtype=jnp.int32)
    one_hot = (flat_ids[:, None] == expert_iota[None, :]).astype(jnp.int32)
    slot_rank = (jnp.sum(jnp.cumsum(one_hot, axis=0) * one_hot, axis=1) - 1).reshape(cold_ids.shape)
    slot_iota = jnp.arange(slot_count, dtype=jnp.int32)
    select = (cold_ids[:, :, None, None] == expert_iota[None, None, :, None]) & (
        slot_rank[:, :, None, None] == slot_iota[None, None, None, :]
    )
    placing = jnp.sum(select.astype(jnp.bfloat16), axis=1)
    outgoing = jnp.einsum(
        "res,rd->esd", placing, tokens, preferred_element_type=jnp.float32
    ).astype(jnp.bfloat16)
    local_gate = w_gate.reshape(w_gate.shape[1:])
    local_up = w_up.reshape(w_up.shape[1:])
    local_down = w_down.reshape(w_down.shape[1:])
    hot_expert = routes[0, 0]
    me = lax.axis_index("expert")
    cores = C
    same_chip = me // cores == hot_expert // cores
    role = jnp.where(me == hot_expert, 0, jnp.where(same_chip, 1, 2))
    gathered, arrived, partner_gate, partner_up, partner_down = hot_gather(X, Z, C, tokens, outgoing, local_gate, local_up, local_down)
    flat_rows = arrived.reshape(-1, model_width)
    answered = feed_forward(flat_rows, local_gate, local_up, local_down).reshape(arrived.shape)

    def hot_ffn(gate_w, up_w, down_w):
        return lambda row_block: feed_forward(row_block.reshape(-1, model_width), gate_w, up_w, down_w).reshape(row_block.shape)

    hot_answer = lax.switch(
        role,
        [hot_ffn(local_gate, local_up, local_down), hot_ffn(partner_gate, partner_up, partner_down), jnp.zeros_like],
        gathered,
    )
    hot_out, returned = hot_scatter(X, Z, C, hot_answer, answered)
    picked = returned.reshape(-1, model_width)[cold_ids * slot_count + slot_rank]
    combined = gate_weights[:, 0:1] * hot_out.astype(jnp.float32) + jnp.sum(
        gate_weights[:, 1:, None] * picked.astype(jnp.float32), axis=1
    )
    return combined.astype(jnp.bfloat16)


def solution(mesh):
    X, Z, C = torus_shape(mesh)
    in_specs = (
        P(("dp", "expert"), None),
        P(("dp", "expert"), None),
        P(("dp", "expert"), None),
        P("expert", None, None),
        P("expert", None, None),
        P("expert", None, None),
    )
    out_specs = P(("dp", "expert"), None)
    return jax.shard_map(functools.partial(shards, X, Z, C), mesh=mesh, in_specs=in_specs, out_specs=out_specs, check_vma=False)
```

```python
import functools

import jax
import jax.numpy as jnp
from jax import lax
from jax.experimental import pallas as pl
from jax.experimental.pallas import tpu as pltpu
from jax.sharding import PartitionSpec as P

MESH = pl.DeviceIdType.MESH


def feed_forward(row_block, gate_w, up_w, down_w):
    gate_part = jnp.dot(row_block, gate_w, preferred_element_type=jnp.float32)
    up_part = jnp.dot(row_block, up_w, preferred_element_type=jnp.float32)
    hidden = lax.optimization_barrier((jax.nn.silu(gate_part) * up_part).astype(jnp.bfloat16))
    return jnp.dot(hidden, down_w, preferred_element_type=jnp.float32).astype(jnp.bfloat16)


def torus_shape(mesh):
    n = mesh.shape["expert"]
    try:
        row = mesh.devices.reshape(-1, n)[0]
        xs = {d.coords[0] for d in row}
        zs = {d.coords[2] for d in row}
        X, Z = len(xs), len(zs)
        C = n // (X * Z)
        if X * Z * C != n:
            raise ValueError
    except Exception:
        X, Z, C = 4, 8, 2
        if X * Z * C != n:
            X, Z, C = 1, n // 2, 2
    return X, Z, C


def coordinates(X, Z, C):
    e = lax.axis_index("expert")
    return e // (Z * C), (e // C) % Z, e % C


def wrap(v, n):
    return (v + 4 * n) % n


def device(X, Z, C, x, z, c):
    return {"expert": wrap(x, X) * (Z * C) + wrap(z, Z) * C + wrap(c, C)}


def peers(X, Z, C, x, z, c):
    out = [(x + k, z, c) for k in range(1, X)]
    if Z > 1:
        out.append((x, z + 1, c))
        if Z > 2:
            out.append((x, z - 1, c))
    if C > 1:
        out.append((x, z, c + 1))
    return out


def barrier(X, Z, C, x, z, c):
    sem = pltpu.get_barrier_semaphore()
    targets = peers(X, Z, C, x, z, c)
    for t in targets:
        pl.semaphore_signal(sem, inc=1, device_id=device(X, Z, C, *t), device_id_type=MESH)
    pl.semaphore_wait(sem, len(targets))


def barrier_all():
    n = lax.axis_size("expert")
    me = lax.axis_index("expert")
    sem = pltpu.get_barrier_semaphore()

    def signal(k, carry):
        pl.semaphore_signal(sem, inc=1, device_id={"expert": (me + k) % n}, device_id_type=MESH)
        return carry

    lax.fori_loop(1, n, signal, 0)
    pl.semaphore_wait(sem, n - 1)


def exchange_copy(src_ref, dst_ref, k, send_sem, recv_sem):
    n = lax.axis_size("expert")
    me = lax.axis_index("expert")
    target = (me + k) % n
    return pltpu.make_async_remote_copy(
        src_ref=src_ref.at[target], dst_ref=dst_ref.at[me], send_sem=send_sem.at[k - 1], recv_sem=recv_sem.at[k - 1],
        device_id={"expert": target}, device_id_type=MESH)


def exchange(src_ref, dst_ref, own_sem, send_sem, recv_sem):
    n = lax.axis_size("expert")
    me = lax.axis_index("expert")
    own = pltpu.make_async_copy(src_ref.at[me], dst_ref.at[me], own_sem)
    own.start()

    def start(k, carry):
        exchange_copy(src_ref, dst_ref, k, send_sem, recv_sem).start()
        return carry

    lax.fori_loop(1, n, start, 0)
    return own


def exchange_wait(src_ref, dst_ref, own, send_sem, recv_sem):
    n = lax.axis_size("expert")
    own.wait()

    def wait(k, carry):
        cp = exchange_copy(src_ref, dst_ref, k, send_sem, recv_sem)
        cp.wait_recv()
        cp.wait_send()
        return carry

    lax.fori_loop(1, n, wait, 0)


def gather_kernel(X, Z, C, tok_ref, cold_ref, wg_ref, wu_ref, wd_ref, out_ref, cold_out, pg_ref, pu_ref, pd_ref,
                  own_sem, cs_send, cs_recv, w_send, w_recv, sx_send, sx_recv, sp_send, sp_recv, sm_send, sm_recv):
    x, z, c = coordinates(X, Z, C)
    zp, zm = Z // 2, (Z - 1) // 2
    dirn = 1 - 2 * (c % 2)
    barrier_all()
    own = pltpu.make_async_copy(tok_ref, out_ref.at[z, x], own_sem.at[0])
    own.start()
    xcopies = []
    for k in range(1, X):
        cp = pltpu.make_async_remote_copy(
            src_ref=tok_ref, dst_ref=out_ref.at[z, x], send_sem=sx_send.at[k - 1], recv_sem=sx_recv.at[k - 1],
            device_id=device(X, Z, C, x + k, z, c), device_id_type=MESH)
        cp.start()
        xcopies.append(cp)
    cold_own = exchange(cold_ref, cold_out, own_sem.at[1], cs_send, cs_recv)
    own.wait()
    for cp in xcopies:
        cp.wait_recv()

    plus, minus = [], []
    for s in range(max(zp, zm)):
        if s < zp:
            if s >= 1:
                plus[s - 1].wait_recv()
            blk = wrap(z - s * dirn, Z)
            cp = pltpu.make_async_remote_copy(
                src_ref=out_ref.at[blk], dst_ref=out_ref.at[blk], send_sem=sp_send.at[s],
                recv_sem=sp_recv.at[s], device_id=device(X, Z, C, x, z + dirn, c), device_id_type=MESH)
            cp.start()
            plus.append(cp)
        if s < zm:
            if s >= 1:
                minus[s - 1].wait_recv()
            blk = wrap(z + s * dirn, Z)
            cp = pltpu.make_async_remote_copy(
                src_ref=out_ref.at[blk], dst_ref=out_ref.at[blk], send_sem=sm_send.at[s],
                recv_sem=sm_recv.at[s], device_id=device(X, Z, C, x, z - dirn, c), device_id_type=MESH)
            cp.start()
            minus.append(cp)
        if s == 0:
            wcopies = []
            if C > 1:
                for j, (src, dst) in enumerate(((wg_ref, pg_ref), (wu_ref, pu_ref), (wd_ref, pd_ref))):
                    cp = pltpu.make_async_remote_copy(
                        src_ref=src, dst_ref=dst, send_sem=w_send.at[j], recv_sem=w_recv.at[j],
                        device_id=device(X, Z, C, x, z, c + 1), device_id_type=MESH)
                    cp.start()
                    wcopies.append(cp)
    if zp:
        plus[zp - 1].wait_recv()
    if zm:
        minus[zm - 1].wait_recv()
    for cp in xcopies + plus + minus:
        cp.wait_send()
    exchange_wait(cold_ref, cold_out, cold_own, cs_send, cs_recv)
    for cp in wcopies:
        cp.wait_recv()
        cp.wait_send()


def scatter_kernel(X, Z, C, o_ref, cold_ref, out_ref, cold_out, own_sem, cs_send, cs_recv, plus_buf, plus_send, minus_buf, minus_send, xbuf, xsend,
                   sp_send, sp_recv, sm_send, sm_recv, sx_send, sx_recv):
    x, z, c = coordinates(X, Z, C)
    zp, zm = Z // 2, (Z - 1) // 2
    dirn = 1 - 2 * (c % 2)
    barrier_all()

    def chip_sum(blk):
        return o_ref[blk].astype(jnp.float32)

    plus, minus = [], []
    for s in range(max(zp, zm)):
        if s < zp:
            val = chip_sum(wrap(z + (zp - s) * dirn, Z))
            if s >= 1:
                plus[s - 1].wait_recv()
                val = val + plus_buf[s - 1].astype(jnp.float32)
            plus_send[s] = val.astype(jnp.bfloat16)
            cp = pltpu.make_async_remote_copy(
                src_ref=plus_send.at[s], dst_ref=plus_buf.at[s], send_sem=sp_send.at[s], recv_sem=sp_recv.at[s],
                device_id=device(X, Z, C, x, z + dirn, c), device_id_type=MESH)
            cp.start()
            plus.append(cp)
        if s < zm:
            val = chip_sum(wrap(z - (zm - s) * dirn, Z))
            if s >= 1:
                minus[s - 1].wait_recv()
                val = val + minus_buf[s - 1].astype(jnp.float32)
            minus_send[s] = val.astype(jnp.bfloat16)
            cp = pltpu.make_async_remote_copy(
                src_ref=minus_send.at[s], dst_ref=minus_buf.at[s], send_sem=sm_send.at[s], recv_sem=sm_recv.at[s],
                device_id=device(X, Z, C, x, z - dirn, c), device_id_type=MESH)
            cp.start()
            minus.append(cp)
        if s == 0:
            cold_own = exchange(cold_ref, cold_out, own_sem.at[0], cs_send, cs_recv)
    total = chip_sum(z)
    if zp:
        plus[zp - 1].wait_recv()
        total = total + plus_buf[zp - 1].astype(jnp.float32)
    if zm:
        minus[zm - 1].wait_recv()
        total = total + minus_buf[zm - 1].astype(jnp.float32)
    xsend[...] = total.astype(jnp.bfloat16)
    xcopies = []
    for k in range(1, X):
        cp = pltpu.make_async_remote_copy(
            src_ref=xsend.at[(x + k) % X], dst_ref=xbuf.at[k - 1], send_sem=sx_send.at[k - 1], recv_sem=sx_recv.at[k - 1],
            device_id=device(X, Z, C, x + k, z, c), device_id_type=MESH)
        cp.start()
        xcopies.append(cp)
    result = xsend[x].astype(jnp.float32)
    for k, cp in enumerate(xcopies):
        cp.wait_recv()
        result = result + xbuf[k].astype(jnp.float32)
    out_ref[...] = result.astype(out_ref.dtype)
    for cp in plus + minus + xcopies:
        cp.wait_send()
    exchange_wait(cold_ref, cold_out, cold_own, cs_send, cs_recv)


def hot_gather(X, Z, C, tokens, outgoing, w_gate, w_up, w_down):
    R, D = tokens.shape
    zp, zm = Z // 2, (Z - 1) // 2
    n = outgoing.shape[0]
    dma = pltpu.SemaphoreType.DMA
    vmem = pl.BlockSpec(memory_space=pltpu.VMEM)
    anywhere = pl.BlockSpec(memory_space=pl.ANY)
    return pl.pallas_call(
        functools.partial(gather_kernel, X, Z, C),
        out_shape=(
            jax.ShapeDtypeStruct((Z, X, R, D), tokens.dtype), jax.ShapeDtypeStruct(outgoing.shape, outgoing.dtype),
            jax.ShapeDtypeStruct(w_gate.shape, w_gate.dtype), jax.ShapeDtypeStruct(w_up.shape, w_up.dtype),
            jax.ShapeDtypeStruct(w_down.shape, w_down.dtype),
        ),
        in_specs=[vmem, vmem, anywhere, anywhere, anywhere],
        out_specs=(vmem, vmem, anywhere, anywhere, anywhere),
        scratch_shapes=[
            dma((2,)), dma((n - 1,)), dma((n - 1,)), dma((3,)), dma((3,)),
            dma((max(X - 1, 1),)), dma((max(X - 1, 1),)),
            dma((max(zp, 1),)), dma((max(zp, 1),)),
            dma((max(zm, 1),)), dma((max(zm, 1),)),
        ],
        compiler_params=pltpu.CompilerParams(collective_id=0, has_side_effects=True),
    )(tokens, outgoing, w_gate, w_up, w_down)


def hot_scatter(X, Z, C, answered, cold_answered):
    _, _, R, D = answered.shape
    zp, zm = Z // 2, (Z - 1) // 2
    n = cold_answered.shape[0]
    dma = pltpu.SemaphoreType.DMA
    bf = answered.dtype
    vmem = pl.BlockSpec(memory_space=pltpu.VMEM)
    return pl.pallas_call(
        functools.partial(scatter_kernel, X, Z, C),
        out_shape=(jax.ShapeDtypeStruct((R, D), bf), jax.ShapeDtypeStruct(cold_answered.shape, cold_answered.dtype)),
        in_specs=[vmem, vmem],
        out_specs=(vmem, vmem),
        scratch_shapes=[
            dma((1,)), dma((n - 1,)), dma((n - 1,)),
            pltpu.VMEM((max(zp, 1), X, R, D), bf), pltpu.VMEM((max(zp, 1), X, R, D), bf),
            pltpu.VMEM((max(zm, 1), X, R, D), bf), pltpu.VMEM((max(zm, 1), X, R, D), bf),
            pltpu.VMEM((max(X - 1, 1), R, D), bf), pltpu.VMEM((X, R, D), bf),
            dma((max(zp, 1),)), dma((max(zp, 1),)),
            dma((max(zm, 1),)), dma((max(zm, 1),)),
            dma((max(X - 1, 1),)), dma((max(X - 1, 1),)),
        ],
        compiler_params=pltpu.CompilerParams(collective_id=1, has_side_effects=True),
    )(answered, cold_answered)


def shards(X, Z, C, tokens, routes, gate_weights, w_gate, w_up, w_down):
    devices = lax.axis_size("expert")
    experts = w_gate.shape[0] * devices
    row_count = routes.shape[0]
    top_count = routes.shape[1]
    model_width = tokens.shape[1]
    slot_count = (row_count * (top_count - 1) + experts - 2) // (experts - 1)
    cold_ids = routes[:, 1:]
    flat_ids = cold_ids.reshape(-1)
    expert_iota = jnp.arange(experts, dtype=jnp.int32)
    one_hot = (flat_ids[:, None] == expert_iota[None, :]).astype(jnp.int32)
    slot_rank = (jnp.sum(jnp.cumsum(one_hot, axis=0) * one_hot, axis=1) - 1).reshape(cold_ids.shape)
    slot_iota = jnp.arange(slot_count, dtype=jnp.int32)
    select = (cold_ids[:, :, None, None] == expert_iota[None, None, :, None]) & (
        slot_rank[:, :, None, None] == slot_iota[None, None, None, :]
    )
    placing = jnp.sum(select.astype(jnp.bfloat16), axis=1)
    outgoing = jnp.einsum(
        "res,rd->esd", placing, tokens, preferred_element_type=jnp.float32
    ).astype(jnp.bfloat16)
    local_gate = w_gate.reshape(w_gate.shape[1:])
    local_up = w_up.reshape(w_up.shape[1:])
    local_down = w_down.reshape(w_down.shape[1:])
    hot_expert = routes[0, 0]
    me = lax.axis_index("expert")
    cores = C
    same_chip = me // cores == hot_expert // cores
    role = jnp.where(me == hot_expert, 0, jnp.where(same_chip, 1, 2))
    gathered, arrived, partner_gate, partner_up, partner_down = hot_gather(X, Z, C, tokens, outgoing, local_gate, local_up, local_down)
    flat_rows = arrived.reshape(-1, model_width)
    answered = feed_forward(flat_rows, local_gate, local_up, local_down).reshape(arrived.shape)

    def hot_ffn(gate_w, up_w, down_w):
        return lambda row_block: feed_forward(row_block.reshape(-1, model_width), gate_w, up_w, down_w).reshape(row_block.shape)

    hot_answer = lax.switch(
        role,
        [hot_ffn(local_gate, local_up, local_down), hot_ffn(partner_gate, partner_up, partner_down), jnp.zeros_like],
        gathered,
    )
    hot_out, returned = hot_scatter(X, Z, C, hot_answer, answered)
    picked = returned.reshape(-1, model_width)[cold_ids * slot_count + slot_rank]
    combined = gate_weights[:, 0:1] * hot_out.astype(jnp.float32) + jnp.sum(
        gate_weights[:, 1:, None] * picked.astype(jnp.float32), axis=1
    )
    return combined.astype(jnp.bfloat16)


def solution(mesh):
    X, Z, C = torus_shape(mesh)
    in_specs = (
        P(("dp", "expert"), None),
        P(("dp", "expert"), None),
        P(("dp", "expert"), None),
        P("expert", None, None),
        P("expert", None, None),
        P("expert", None, None),
    )
    out_specs = P(("dp", "expert"), None)
    return jax.shard_map(functools.partial(shards, X, Z, C), mesh=mesh, in_specs=in_specs, out_specs=out_specs, check_vma=False)
```

```python
import functools

import jax
import jax.numpy as jnp
from jax import lax
from jax.experimental import pallas as pl
from jax.experimental.pallas import tpu as pltpu
from jax.sharding import PartitionSpec as P

MESH = pl.DeviceIdType.MESH


def feed_forward(row_block, gate_w, up_w, down_w):
    gate_part = jnp.dot(row_block, gate_w, preferred_element_type=jnp.float32)
    up_part = jnp.dot(row_block, up_w, preferred_element_type=jnp.float32)
    hidden = lax.optimization_barrier((jax.nn.silu(gate_part) * up_part).astype(jnp.bfloat16))
    return jnp.dot(hidden, down_w, preferred_element_type=jnp.float32).astype(jnp.bfloat16)


def torus_shape(mesh):
    n = mesh.shape["expert"]
    try:
        row = mesh.devices.reshape(-1, n)[0]
        xs = {d.coords[0] for d in row}
        zs = {d.coords[2] for d in row}
        X, Z = len(xs), len(zs)
        C = n // (X * Z)
        if X * Z * C != n:
            raise ValueError
    except Exception:
        X, Z, C = 4, 8, 2
        if X * Z * C != n:
            X, Z, C = 1, n // 2, 2
    return X, Z, C


def coordinates(X, Z, C):
    e = lax.axis_index("expert")
    return e // (Z * C), (e // C) % Z, e % C


def wrap(v, n):
    return (v + 4 * n) % n


def device(X, Z, C, x, z, c):
    return {"expert": wrap(x, X) * (Z * C) + wrap(z, Z) * C + wrap(c, C)}


def peers(X, Z, C, x, z, c):
    out = [(x + k, z, c) for k in range(1, X)]
    if Z > 1:
        out.append((x, z + 1, c))
        if Z > 2:
            out.append((x, z - 1, c))
    if C > 1:
        out.append((x, z, c + 1))
    return out


def barrier(X, Z, C, x, z, c):
    sem = pltpu.get_barrier_semaphore()
    targets = peers(X, Z, C, x, z, c)
    for t in targets:
        pl.semaphore_signal(sem, inc=1, device_id=device(X, Z, C, *t), device_id_type=MESH)
    pl.semaphore_wait(sem, len(targets))


def barrier_all(n):
    me = lax.axis_index("expert")
    sem = pltpu.get_barrier_semaphore()

    for k in range(1, n):
        pl.semaphore_signal(sem, inc=1, device_id={"expert": (me + k) % n}, device_id_type=MESH)
    pl.semaphore_wait(sem, n - 1)


def exchange_copy(src_ref, dst_ref, k, send_sem, recv_sem):
    n = src_ref.shape[0]
    me = lax.axis_index("expert")
    target = (me + k) % n
    return pltpu.make_async_remote_copy(
        src_ref=src_ref.at[target], dst_ref=dst_ref.at[me], send_sem=send_sem.at[k - 1], recv_sem=recv_sem.at[k - 1],
        device_id={"expert": target}, device_id_type=MESH)


def exchange(src_ref, dst_ref, own_sem, send_sem, recv_sem):
    n = src_ref.shape[0]
    me = lax.axis_index("expert")
    own = pltpu.make_async_copy(src_ref.at[me], dst_ref.at[me], own_sem)
    own.start()

    for k in range(1, n):
        exchange_copy(src_ref, dst_ref, k, send_sem, recv_sem).start()
    return own


def exchange_wait(src_ref, dst_ref, own, send_sem, recv_sem):
    n = src_ref.shape[0]
    own.wait()

    for k in range(1, n):
        cp = exchange_copy(src_ref, dst_ref, k, send_sem, recv_sem)
        cp.wait_recv()
        cp.wait_send()


def gather_kernel(X, Z, C, tok_ref, cold_ref, wg_ref, wu_ref, wd_ref, out_ref, cold_out, pg_ref, pu_ref, pd_ref,
                  own_sem, cs_send, cs_recv, w_send, w_recv, sx_send, sx_recv, sp_send, sp_recv, sm_send, sm_recv):
    x, z, c = coordinates(X, Z, C)
    zp, zm = Z // 2, (Z - 1) // 2
    dirn = 1 - 2 * (c % 2)
    barrier_all(cold_ref.shape[0])
    own = pltpu.make_async_copy(tok_ref, out_ref.at[z, x], own_sem.at[0])
    own.start()
    xcopies = []
    for k in range(1, X):
        cp = pltpu.make_async_remote_copy(
            src_ref=tok_ref, dst_ref=out_ref.at[z, x], send_sem=sx_send.at[k - 1], recv_sem=sx_recv.at[k - 1],
            device_id=device(X, Z, C, x + k, z, c), device_id_type=MESH)
        cp.start()
        xcopies.append(cp)
    cold_own = exchange(cold_ref, cold_out, own_sem.at[1], cs_send, cs_recv)
    own.wait()
    for cp in xcopies:
        cp.wait_recv()

    plus, minus = [], []
    for s in range(max(zp, zm)):
        if s < zp:
            if s >= 1:
                plus[s - 1].wait_recv()
            blk = wrap(z - s * dirn, Z)
            cp = pltpu.make_async_remote_copy(
                src_ref=out_ref.at[blk], dst_ref=out_ref.at[blk], send_sem=sp_send.at[s],
                recv_sem=sp_recv.at[s], device_id=device(X, Z, C, x, z + dirn, c), device_id_type=MESH)
            cp.start()
            plus.append(cp)
        if s < zm:
            if s >= 1:
                minus[s - 1].wait_recv()
            blk = wrap(z + s * dirn, Z)
            cp = pltpu.make_async_remote_copy(
                src_ref=out_ref.at[blk], dst_ref=out_ref.at[blk], send_sem=sm_send.at[s],
                recv_sem=sm_recv.at[s], device_id=device(X, Z, C, x, z - dirn, c), device_id_type=MESH)
            cp.start()
            minus.append(cp)
        if s == 0:
            wcopies = []
            if C > 1:
                for j, (src, dst) in enumerate(((wg_ref, pg_ref), (wu_ref, pu_ref), (wd_ref, pd_ref))):
                    cp = pltpu.make_async_remote_copy(
                        src_ref=src, dst_ref=dst, send_sem=w_send.at[j], recv_sem=w_recv.at[j],
                        device_id=device(X, Z, C, x, z, c + 1), device_id_type=MESH)
                    cp.start()
                    wcopies.append(cp)
    if zp:
        plus[zp - 1].wait_recv()
    if zm:
        minus[zm - 1].wait_recv()
    for cp in xcopies + plus + minus:
        cp.wait_send()
    exchange_wait(cold_ref, cold_out, cold_own, cs_send, cs_recv)
    for cp in wcopies:
        cp.wait_recv()
        cp.wait_send()


def scatter_kernel(X, Z, C, o_ref, cold_ref, out_ref, cold_out, own_sem, cs_send, cs_recv, plus_buf, plus_send, minus_buf, minus_send, xbuf, xsend,
                   sp_send, sp_recv, sm_send, sm_recv, sx_send, sx_recv):
    x, z, c = coordinates(X, Z, C)
    zp, zm = Z // 2, (Z - 1) // 2
    dirn = 1 - 2 * (c % 2)
    barrier_all(cold_ref.shape[0])

    def chip_sum(blk):
        return o_ref[blk].astype(jnp.float32)

    plus, minus = [], []
    for s in range(max(zp, zm)):
        if s < zp:
            val = chip_sum(wrap(z + (zp - s) * dirn, Z))
            if s >= 1:
                plus[s - 1].wait_recv()
                val = val + plus_buf[s - 1].astype(jnp.float32)
            plus_send[s] = val.astype(jnp.bfloat16)
            cp = pltpu.make_async_remote_copy(
                src_ref=plus_send.at[s], dst_ref=plus_buf.at[s], send_sem=sp_send.at[s], recv_sem=sp_recv.at[s],
                device_id=device(X, Z, C, x, z + dirn, c), device_id_type=MESH)
            cp.start()
            plus.append(cp)
        if s < zm:
            val = chip_sum(wrap(z - (zm - s) * dirn, Z))
            if s >= 1:
                minus[s - 1].wait_recv()
                val = val + minus_buf[s - 1].astype(jnp.float32)
            minus_send[s] = val.astype(jnp.bfloat16)
            cp = pltpu.make_async_remote_copy(
                src_ref=minus_send.at[s], dst_ref=minus_buf.at[s], send_sem=sm_send.at[s], recv_sem=sm_recv.at[s],
                device_id=device(X, Z, C, x, z - dirn, c), device_id_type=MESH)
            cp.start()
            minus.append(cp)
        if s == 0:
            cold_own = exchange(cold_ref, cold_out, own_sem.at[0], cs_send, cs_recv)
    total = chip_sum(z)
    if zp:
        plus[zp - 1].wait_recv()
        total = total + plus_buf[zp - 1].astype(jnp.float32)
    if zm:
        minus[zm - 1].wait_recv()
        total = total + minus_buf[zm - 1].astype(jnp.float32)
    xsend[...] = total.astype(jnp.bfloat16)
    xcopies = []
    for k in range(1, X):
        cp = pltpu.make_async_remote_copy(
            src_ref=xsend.at[(x + k) % X], dst_ref=xbuf.at[k - 1], send_sem=sx_send.at[k - 1], recv_sem=sx_recv.at[k - 1],
            device_id=device(X, Z, C, x + k, z, c), device_id_type=MESH)
        cp.start()
        xcopies.append(cp)
    result = xsend[x].astype(jnp.float32)
    for k, cp in enumerate(xcopies):
        cp.wait_recv()
        result = result + xbuf[k].astype(jnp.float32)
    out_ref[...] = result.astype(out_ref.dtype)
    for cp in plus + minus + xcopies:
        cp.wait_send()
    exchange_wait(cold_ref, cold_out, cold_own, cs_send, cs_recv)


def hot_gather(X, Z, C, tokens, outgoing, w_gate, w_up, w_down):
    R, D = tokens.shape
    zp, zm = Z // 2, (Z - 1) // 2
    n = outgoing.shape[0]
    dma = pltpu.SemaphoreType.DMA
    vmem = pl.BlockSpec(memory_space=pltpu.VMEM)
    anywhere = pl.BlockSpec(memory_space=pl.ANY)
    return pl.pallas_call(
        functools.partial(gather_kernel, X, Z, C),
        out_shape=(
            jax.ShapeDtypeStruct((Z, X, R, D), tokens.dtype), jax.ShapeDtypeStruct(outgoing.shape, outgoing.dtype),
            jax.ShapeDtypeStruct(w_gate.shape, w_gate.dtype), jax.ShapeDtypeStruct(w_up.shape, w_up.dtype),
            jax.ShapeDtypeStruct(w_down.shape, w_down.dtype),
        ),
        in_specs=[vmem, vmem, anywhere, anywhere, anywhere],
        out_specs=(vmem, vmem, anywhere, anywhere, anywhere),
        scratch_shapes=[
            dma((2,)), dma((n - 1,)), dma((n - 1,)), dma((3,)), dma((3,)),
            dma((max(X - 1, 1),)), dma((max(X - 1, 1),)),
            dma((max(zp, 1),)), dma((max(zp, 1),)),
            dma((max(zm, 1),)), dma((max(zm, 1),)),
        ],
        compiler_params=pltpu.CompilerParams(collective_id=0, has_side_effects=True),
    )(tokens, outgoing, w_gate, w_up, w_down)


def hot_scatter(X, Z, C, answered, cold_answered):
    _, _, R, D = answered.shape
    zp, zm = Z // 2, (Z - 1) // 2
    n = cold_answered.shape[0]
    dma = pltpu.SemaphoreType.DMA
    bf = answered.dtype
    vmem = pl.BlockSpec(memory_space=pltpu.VMEM)
    return pl.pallas_call(
        functools.partial(scatter_kernel, X, Z, C),
        out_shape=(jax.ShapeDtypeStruct((R, D), bf), jax.ShapeDtypeStruct(cold_answered.shape, cold_answered.dtype)),
        in_specs=[vmem, vmem],
        out_specs=(vmem, vmem),
        scratch_shapes=[
            dma((1,)), dma((n - 1,)), dma((n - 1,)),
            pltpu.VMEM((max(zp, 1), X, R, D), bf), pltpu.VMEM((max(zp, 1), X, R, D), bf),
            pltpu.VMEM((max(zm, 1), X, R, D), bf), pltpu.VMEM((max(zm, 1), X, R, D), bf),
            pltpu.VMEM((max(X - 1, 1), R, D), bf), pltpu.VMEM((X, R, D), bf),
            dma((max(zp, 1),)), dma((max(zp, 1),)),
            dma((max(zm, 1),)), dma((max(zm, 1),)),
            dma((max(X - 1, 1),)), dma((max(X - 1, 1),)),
        ],
        compiler_params=pltpu.CompilerParams(collective_id=1, has_side_effects=True),
    )(answered, cold_answered)


def shards(X, Z, C, tokens, routes, gate_weights, w_gate, w_up, w_down):
    devices = lax.axis_size("expert")
    experts = w_gate.shape[0] * devices
    row_count = routes.shape[0]
    top_count = routes.shape[1]
    model_width = tokens.shape[1]
    slot_count = (row_count * (top_count - 1) + experts - 2) // (experts - 1)
    cold_ids = routes[:, 1:]
    flat_ids = cold_ids.reshape(-1)
    expert_iota = jnp.arange(experts, dtype=jnp.int32)
    one_hot = (flat_ids[:, None] == expert_iota[None, :]).astype(jnp.int32)
    slot_rank = (jnp.sum(jnp.cumsum(one_hot, axis=0) * one_hot, axis=1) - 1).reshape(cold_ids.shape)
    slot_iota = jnp.arange(slot_count, dtype=jnp.int32)
    select = (cold_ids[:, :, None, None] == expert_iota[None, None, :, None]) & (
        slot_rank[:, :, None, None] == slot_iota[None, None, None, :]
    )
    placing = jnp.sum(select.astype(jnp.bfloat16), axis=1)
    outgoing = jnp.einsum(
        "res,rd->esd", placing, tokens, preferred_element_type=jnp.float32
    ).astype(jnp.bfloat16)
    local_gate = w_gate.reshape(w_gate.shape[1:])
    local_up = w_up.reshape(w_up.shape[1:])
    local_down = w_down.reshape(w_down.shape[1:])
    hot_expert = routes[0, 0]
    me = lax.axis_index("expert")
    cores = C
    same_chip = me // cores == hot_expert // cores
    role = jnp.where(me == hot_expert, 0, jnp.where(same_chip, 1, 2))
    gathered, arrived, partner_gate, partner_up, partner_down = hot_gather(X, Z, C, tokens, outgoing, local_gate, local_up, local_down)
    flat_rows = arrived.reshape(-1, model_width)
    answered = feed_forward(flat_rows, local_gate, local_up, local_down).reshape(arrived.shape)

    def hot_ffn(gate_w, up_w, down_w):
        return lambda row_block: feed_forward(row_block.reshape(-1, model_width), gate_w, up_w, down_w).reshape(row_block.shape)

    hot_answer = lax.switch(
        role,
        [hot_ffn(local_gate, local_up, local_down), hot_ffn(partner_gate, partner_up, partner_down), jnp.zeros_like],
        gathered,
    )
    hot_out, returned = hot_scatter(X, Z, C, hot_answer, answered)
    picked = returned.reshape(-1, model_width)[cold_ids * slot_count + slot_rank]
    combined = gate_weights[:, 0:1] * hot_out.astype(jnp.float32) + jnp.sum(
        gate_weights[:, 1:, None] * picked.astype(jnp.float32), axis=1
    )
    return combined.astype(jnp.bfloat16)


def solution(mesh):
    X, Z, C = torus_shape(mesh)
    in_specs = (
        P(("dp", "expert"), None),
        P(("dp", "expert"), None),
        P(("dp", "expert"), None),
        P("expert", None, None),
        P("expert", None, None),
        P("expert", None, None),
    )
    out_specs = P(("dp", "expert"), None)
    return jax.shard_map(functools.partial(shards, X, Z, C), mesh=mesh, in_specs=in_specs, out_specs=out_specs, check_vma=False)
```

```python
import functools

import jax
import jax.numpy as jnp
from jax import lax
from jax.experimental import pallas as pl
from jax.experimental.pallas import tpu as pltpu
from jax.sharding import PartitionSpec as P

MESH = pl.DeviceIdType.MESH


def feed_forward(row_block, gate_w, up_w, down_w):
    gate_part = jnp.dot(row_block, gate_w, preferred_element_type=jnp.float32)
    up_part = jnp.dot(row_block, up_w, preferred_element_type=jnp.float32)
    hidden = lax.optimization_barrier((jax.nn.silu(gate_part) * up_part).astype(jnp.bfloat16))
    return jnp.dot(hidden, down_w, preferred_element_type=jnp.float32).astype(jnp.bfloat16)


def torus_shape(mesh):
    n = mesh.shape["expert"]
    try:
        row = mesh.devices.reshape(-1, n)[0]
        xs = {d.coords[0] for d in row}
        zs = {d.coords[2] for d in row}
        X, Z = len(xs), len(zs)
        C = n // (X * Z)
        if X * Z * C != n:
            raise ValueError
    except Exception:
        X, Z, C = 4, 8, 2
        if X * Z * C != n:
            X, Z, C = 1, n // 2, 2
    return X, Z, C


def coordinates(X, Z, C):
    e = lax.axis_index("expert")
    return e // (Z * C), (e // C) % Z, e % C


def wrap(v, n):
    return (v + 4 * n) % n


def device(X, Z, C, x, z, c):
    return {"expert": wrap(x, X) * (Z * C) + wrap(z, Z) * C + wrap(c, C)}


def peers(X, Z, C, x, z, c):
    out = [(x + k, z, c) for k in range(1, X)]
    if Z > 1:
        out.append((x, z + 1, c))
        if Z > 2:
            out.append((x, z - 1, c))
    if C > 1:
        out.append((x, z, c + 1))
    return out


def barrier(X, Z, C, x, z, c):
    sem = pltpu.get_barrier_semaphore()
    targets = peers(X, Z, C, x, z, c)
    for t in targets:
        pl.semaphore_signal(sem, inc=1, device_id=device(X, Z, C, *t), device_id_type=MESH)
    pl.semaphore_wait(sem, len(targets))


def barrier_all(n):
    me = lax.axis_index("expert")
    sem = pltpu.get_barrier_semaphore()

    for k in range(1, n):
        pl.semaphore_signal(sem, inc=1, device_id={"expert": (me + k) % n}, device_id_type=MESH)
    pl.semaphore_wait(sem, n - 1)


def exchange_copy(src_ref, dst_ref, k, send_sem, recv_sem):
    n = src_ref.shape[0]
    me = lax.axis_index("expert")
    target = (me + k) % n
    return pltpu.make_async_remote_copy(
        src_ref=src_ref.at[target], dst_ref=dst_ref.at[me], send_sem=send_sem.at[k - 1], recv_sem=recv_sem.at[k - 1],
        device_id={"expert": target}, device_id_type=MESH)


def exchange(src_ref, dst_ref, own_sem, send_sem, recv_sem):
    n = src_ref.shape[0]
    me = lax.axis_index("expert")
    own = pltpu.make_async_copy(src_ref.at[me], dst_ref.at[me], own_sem)
    own.start()

    for k in range(1, n):
        exchange_copy(src_ref, dst_ref, k, send_sem, recv_sem).start()
    return own


def exchange_wait(src_ref, dst_ref, own, send_sem, recv_sem):
    n = src_ref.shape[0]
    own.wait()

    for k in range(1, n):
        cp = exchange_copy(src_ref, dst_ref, k, send_sem, recv_sem)
        cp.wait_recv()
        cp.wait_send()


def plane_peers(X, Z, C, x, z, c):
    W = Z * C
    w = z * C + c
    return [{"expert": wrap(x + k, X) * W + w} for k in range(1, X)] + [
        {"expert": x * W + wrap(w + k, W)} for k in range(1, W)]


def barrier_plane(X, Z, C, x, z, c):
    sem = pltpu.get_barrier_semaphore()
    targets = plane_peers(X, Z, C, x, z, c)
    for t in targets:
        pl.semaphore_signal(sem, inc=1, device_id=t, device_id_type=MESH)
    pl.semaphore_wait(sem, len(targets))


def two_stage(X, Z, C, x, z, c):
    W = Z * C
    w = z * C + c
    return W, w


def stage_x(X, Z, C, src_of, dst_of, own_sem, send_sem, recv_sem):
    x, z, c = coordinates(X, Z, C)
    W, w = two_stage(X, Z, C, x, z, c)
    own = pltpu.make_async_copy(src_of(x), dst_of(x), own_sem)
    own.start()
    copies = []
    for k in range(1, X):
        cp = pltpu.make_async_remote_copy(
            src_ref=src_of(wrap(x + k, X)), dst_ref=dst_of(x), send_sem=send_sem.at[k - 1], recv_sem=recv_sem.at[k - 1],
            device_id={"expert": wrap(x + k, X) * W + w}, device_id_type=MESH)
        cp.start()
        copies.append(cp)
    return [own] + copies


def stage_w(X, Z, C, src_of, dst_of, own_sem, send_sem, recv_sem):
    x, z, c = coordinates(X, Z, C)
    W, w = two_stage(X, Z, C, x, z, c)
    own = pltpu.make_async_copy(src_of(w), dst_of(w), own_sem)
    own.start()
    copies = []
    for k in range(1, W):
        cp = pltpu.make_async_remote_copy(
            src_ref=src_of(wrap(w + k, W)), dst_ref=dst_of(w), send_sem=send_sem.at[k - 1], recv_sem=recv_sem.at[k - 1],
            device_id={"expert": x * W + wrap(w + k, W)}, device_id_type=MESH)
        cp.start()
        copies.append(cp)
    return [own] + copies


def wait_recvs(copies):
    copies[0].wait()
    for cp in copies[1:]:
        cp.wait_recv()


def wait_sends(copies):
    for cp in copies[1:]:
        cp.wait_send()


def gather_kernel(X, Z, C, tok_ref, cold_ref, wg_ref, wu_ref, wd_ref, out_ref, cold_out, pg_ref, pu_ref, pd_ref,
                  cold_mid, own_sem, c1_send, c1_recv, c2_send, c2_recv, w_send, w_recv, sx_send, sx_recv, sp_send, sp_recv, sm_send, sm_recv):
    x, z, c = coordinates(X, Z, C)
    zp, zm = Z // 2, (Z - 1) // 2
    dirn = 1 - 2 * (c % 2)
    barrier_plane(X, Z, C, x, z, c)
    own = pltpu.make_async_copy(tok_ref, out_ref.at[z, x], own_sem.at[0])
    own.start()
    xcopies = []
    for k in range(1, X):
        cp = pltpu.make_async_remote_copy(
            src_ref=tok_ref, dst_ref=out_ref.at[z, x], send_sem=sx_send.at[k - 1], recv_sem=sx_recv.at[k - 1],
            device_id=device(X, Z, C, x + k, z, c), device_id_type=MESH)
        cp.start()
        xcopies.append(cp)
    cold1 = stage_x(X, Z, C, lambda i: cold_ref.at[i], lambda i: cold_mid.at[:, i], own_sem.at[1], c1_send, c1_recv)
    own.wait()
    for cp in xcopies:
        cp.wait_recv()

    plus, minus = [], []
    for s in range(max(zp, zm)):
        if s < zp:
            if s >= 1:
                plus[s - 1].wait_recv()
            blk = wrap(z - s * dirn, Z)
            cp = pltpu.make_async_remote_copy(
                src_ref=out_ref.at[blk], dst_ref=out_ref.at[blk], send_sem=sp_send.at[s],
                recv_sem=sp_recv.at[s], device_id=device(X, Z, C, x, z + dirn, c), device_id_type=MESH)
            cp.start()
            plus.append(cp)
        if s < zm:
            if s >= 1:
                minus[s - 1].wait_recv()
            blk = wrap(z + s * dirn, Z)
            cp = pltpu.make_async_remote_copy(
                src_ref=out_ref.at[blk], dst_ref=out_ref.at[blk], send_sem=sm_send.at[s],
                recv_sem=sm_recv.at[s], device_id=device(X, Z, C, x, z - dirn, c), device_id_type=MESH)
            cp.start()
            minus.append(cp)
        if s == 0:
            wait_recvs(cold1)
            cold2 = stage_w(X, Z, C, lambda i: cold_mid.at[i], lambda i: cold_out.at[i], own_sem.at[2], c2_send, c2_recv)
            wcopies = []
            if C > 1:
                for j, (src, dst) in enumerate(((wg_ref, pg_ref), (wu_ref, pu_ref), (wd_ref, pd_ref))):
                    cp = pltpu.make_async_remote_copy(
                        src_ref=src, dst_ref=dst, send_sem=w_send.at[j], recv_sem=w_recv.at[j],
                        device_id=device(X, Z, C, x, z, c + 1), device_id_type=MESH)
                    cp.start()
                    wcopies.append(cp)
    if zp:
        plus[zp - 1].wait_recv()
    if zm:
        minus[zm - 1].wait_recv()
    for cp in xcopies + plus + minus:
        cp.wait_send()
    wait_recvs(cold2)
    wait_sends(cold1)
    wait_sends(cold2)
    for cp in wcopies:
        cp.wait_recv()
        cp.wait_send()


def scatter_kernel(X, Z, C, o_ref, cold_ref, out_ref, cold_out, cold_mid, own_sem, c1_send, c1_recv, c2_send, c2_recv, plus_buf, plus_send, minus_buf, minus_send, xbuf, xsend,
                   sp_send, sp_recv, sm_send, sm_recv, sx_send, sx_recv):
    x, z, c = coordinates(X, Z, C)
    zp, zm = Z // 2, (Z - 1) // 2
    dirn = 1 - 2 * (c % 2)
    barrier_plane(X, Z, C, x, z, c)

    def chip_sum(blk):
        return o_ref[blk].astype(jnp.float32)

    plus, minus = [], []
    for s in range(max(zp, zm)):
        if s < zp:
            val = chip_sum(wrap(z + (zp - s) * dirn, Z))
            if s >= 1:
                plus[s - 1].wait_recv()
                val = val + plus_buf[s - 1].astype(jnp.float32)
            plus_send[s] = val.astype(jnp.bfloat16)
            cp = pltpu.make_async_remote_copy(
                src_ref=plus_send.at[s], dst_ref=plus_buf.at[s], send_sem=sp_send.at[s], recv_sem=sp_recv.at[s],
                device_id=device(X, Z, C, x, z + dirn, c), device_id_type=MESH)
            cp.start()
            plus.append(cp)
        if s < zm:
            val = chip_sum(wrap(z - (zm - s) * dirn, Z))
            if s >= 1:
                minus[s - 1].wait_recv()
                val = val + minus_buf[s - 1].astype(jnp.float32)
            minus_send[s] = val.astype(jnp.bfloat16)
            cp = pltpu.make_async_remote_copy(
                src_ref=minus_send.at[s], dst_ref=minus_buf.at[s], send_sem=sm_send.at[s], recv_sem=sm_recv.at[s],
                device_id=device(X, Z, C, x, z - dirn, c), device_id_type=MESH)
            cp.start()
            minus.append(cp)
        if s == 0:
            cold1 = stage_w(X, Z, C, lambda i: cold_ref.at[i], lambda i: cold_mid.at[i], own_sem.at[0], c2_send, c2_recv)
    wait_recvs(cold1)
    cold2 = stage_x(X, Z, C, lambda i: cold_mid.at[:, i], lambda i: cold_out.at[i], own_sem.at[1], c1_send, c1_recv)
    total = chip_sum(z)
    if zp:
        plus[zp - 1].wait_recv()
        total = total + plus_buf[zp - 1].astype(jnp.float32)
    if zm:
        minus[zm - 1].wait_recv()
        total = total + minus_buf[zm - 1].astype(jnp.float32)
    xsend[...] = total.astype(jnp.bfloat16)
    xcopies = []
    for k in range(1, X):
        cp = pltpu.make_async_remote_copy(
            src_ref=xsend.at[(x + k) % X], dst_ref=xbuf.at[k - 1], send_sem=sx_send.at[k - 1], recv_sem=sx_recv.at[k - 1],
            device_id=device(X, Z, C, x + k, z, c), device_id_type=MESH)
        cp.start()
        xcopies.append(cp)
    result = xsend[x].astype(jnp.float32)
    for k, cp in enumerate(xcopies):
        cp.wait_recv()
        result = result + xbuf[k].astype(jnp.float32)
    out_ref[...] = result.astype(out_ref.dtype)
    for cp in plus + minus + xcopies:
        cp.wait_send()
    wait_recvs(cold2)
    wait_sends(cold1)
    wait_sends(cold2)


def hot_gather(X, Z, C, tokens, outgoing, w_gate, w_up, w_down):
    R, D = tokens.shape
    zp, zm = Z // 2, (Z - 1) // 2
    W = Z * C
    n, S, _ = outgoing.shape
    outgoing = outgoing.reshape(X, W, S, D)
    dma = pltpu.SemaphoreType.DMA
    vmem = pl.BlockSpec(memory_space=pltpu.VMEM)
    anywhere = pl.BlockSpec(memory_space=pl.ANY)
    return pl.pallas_call(
        functools.partial(gather_kernel, X, Z, C),
        out_shape=(
            jax.ShapeDtypeStruct((Z, X, R, D), tokens.dtype), jax.ShapeDtypeStruct((W, X, S, D), outgoing.dtype),
            jax.ShapeDtypeStruct(w_gate.shape, w_gate.dtype), jax.ShapeDtypeStruct(w_up.shape, w_up.dtype),
            jax.ShapeDtypeStruct(w_down.shape, w_down.dtype),
        ),
        in_specs=[vmem, vmem, anywhere, anywhere, anywhere],
        out_specs=(vmem, vmem, anywhere, anywhere, anywhere),
        scratch_shapes=[
            pltpu.VMEM((W, X, S, D), outgoing.dtype),
            dma((3,)), dma((max(X - 1, 1),)), dma((max(X - 1, 1),)), dma((W - 1,)), dma((W - 1,)), dma((3,)), dma((3,)),
            dma((max(X - 1, 1),)), dma((max(X - 1, 1),)),
            dma((max(zp, 1),)), dma((max(zp, 1),)),
            dma((max(zm, 1),)), dma((max(zm, 1),)),
        ],
        compiler_params=pltpu.CompilerParams(collective_id=0, has_side_effects=True),
    )(tokens, outgoing, w_gate, w_up, w_down)


def hot_scatter(X, Z, C, answered, cold_answered):
    _, _, R, D = answered.shape
    zp, zm = Z // 2, (Z - 1) // 2
    W, _, S, _ = cold_answered.shape
    dma = pltpu.SemaphoreType.DMA
    bf = answered.dtype
    vmem = pl.BlockSpec(memory_space=pltpu.VMEM)
    return pl.pallas_call(
        functools.partial(scatter_kernel, X, Z, C),
        out_shape=(jax.ShapeDtypeStruct((R, D), bf), jax.ShapeDtypeStruct((X, W, S, D), cold_answered.dtype)),
        in_specs=[vmem, vmem],
        out_specs=(vmem, vmem),
        scratch_shapes=[
            pltpu.VMEM((W, X, S, D), cold_answered.dtype),
            dma((2,)), dma((max(X - 1, 1),)), dma((max(X - 1, 1),)), dma((W - 1,)), dma((W - 1,)),
            pltpu.VMEM((max(zp, 1), X, R, D), bf), pltpu.VMEM((max(zp, 1), X, R, D), bf),
            pltpu.VMEM((max(zm, 1), X, R, D), bf), pltpu.VMEM((max(zm, 1), X, R, D), bf),
            pltpu.VMEM((max(X - 1, 1), R, D), bf), pltpu.VMEM((X, R, D), bf),
            dma((max(zp, 1),)), dma((max(zp, 1),)),
            dma((max(zm, 1),)), dma((max(zm, 1),)),
            dma((max(X - 1, 1),)), dma((max(X - 1, 1),)),
        ],
        compiler_params=pltpu.CompilerParams(collective_id=1, has_side_effects=True),
    )(answered, cold_answered)


def shards(X, Z, C, tokens, routes, gate_weights, w_gate, w_up, w_down):
    devices = lax.axis_size("expert")
    experts = w_gate.shape[0] * devices
    row_count = routes.shape[0]
    top_count = routes.shape[1]
    model_width = tokens.shape[1]
    slot_count = (row_count * (top_count - 1) + experts - 2) // (experts - 1)
    cold_ids = routes[:, 1:]
    flat_ids = cold_ids.reshape(-1)
    expert_iota = jnp.arange(experts, dtype=jnp.int32)
    one_hot = (flat_ids[:, None] == expert_iota[None, :]).astype(jnp.int32)
    slot_rank = (jnp.sum(jnp.cumsum(one_hot, axis=0) * one_hot, axis=1) - 1).reshape(cold_ids.shape)
    slot_iota = jnp.arange(slot_count, dtype=jnp.int32)
    select = (cold_ids[:, :, None, None] == expert_iota[None, None, :, None]) & (
        slot_rank[:, :, None, None] == slot_iota[None, None, None, :]
    )
    placing = jnp.sum(select.astype(jnp.bfloat16), axis=1)
    outgoing = jnp.einsum(
        "res,rd->esd", placing, tokens, preferred_element_type=jnp.float32
    ).astype(jnp.bfloat16)
    local_gate = w_gate.reshape(w_gate.shape[1:])
    local_up = w_up.reshape(w_up.shape[1:])
    local_down = w_down.reshape(w_down.shape[1:])
    hot_expert = routes[0, 0]
    me = lax.axis_index("expert")
    cores = C
    same_chip = me // cores == hot_expert // cores
    role = jnp.where(me == hot_expert, 0, jnp.where(same_chip, 1, 2))
    gathered, arrived, partner_gate, partner_up, partner_down = hot_gather(X, Z, C, tokens, outgoing, local_gate, local_up, local_down)
    flat_rows = arrived.reshape(-1, model_width)
    answered = feed_forward(flat_rows, local_gate, local_up, local_down).reshape(arrived.shape)

    def hot_ffn(gate_w, up_w, down_w):
        return lambda row_block: feed_forward(row_block.reshape(-1, model_width), gate_w, up_w, down_w).reshape(row_block.shape)

    hot_answer = lax.switch(
        role,
        [hot_ffn(local_gate, local_up, local_down), hot_ffn(partner_gate, partner_up, partner_down), jnp.zeros_like],
        gathered,
    )
    hot_out, returned = hot_scatter(X, Z, C, hot_answer, answered)
    returned = returned.reshape(experts, slot_count, model_width)
    picked = returned.reshape(-1, model_width)[cold_ids * slot_count + slot_rank]
    combined = gate_weights[:, 0:1] * hot_out.astype(jnp.float32) + jnp.sum(
        gate_weights[:, 1:, None] * picked.astype(jnp.float32), axis=1
    )
    return combined.astype(jnp.bfloat16)


def solution(mesh):
    X, Z, C = torus_shape(mesh)
    in_specs = (
        P(("dp", "expert"), None),
        P(("dp", "expert"), None),
        P(("dp", "expert"), None),
        P("expert", None, None),
        P("expert", None, None),
        P("expert", None, None),
    )
    out_specs = P(("dp", "expert"), None)
    return jax.shard_map(functools.partial(shards, X, Z, C), mesh=mesh, in_specs=in_specs, out_specs=out_specs, check_vma=False)
```

```python
import functools

import jax
import jax.numpy as jnp
from jax import lax
from jax.experimental import pallas as pl
from jax.experimental.pallas import tpu as pltpu
from jax.sharding import PartitionSpec as P

MESH = pl.DeviceIdType.MESH


def feed_forward(row_block, gate_w, up_w, down_w):
    gate_part = jnp.dot(row_block, gate_w, preferred_element_type=jnp.float32)
    up_part = jnp.dot(row_block, up_w, preferred_element_type=jnp.float32)
    hidden = lax.optimization_barrier((jax.nn.silu(gate_part) * up_part).astype(jnp.bfloat16))
    return jnp.dot(hidden, down_w, preferred_element_type=jnp.float32).astype(jnp.bfloat16)


def torus_shape(mesh):
    n = mesh.shape["expert"]
    try:
        row = mesh.devices.reshape(-1, n)[0]
        xs = {d.coords[0] for d in row}
        zs = {d.coords[2] for d in row}
        X, Z = len(xs), len(zs)
        C = n // (X * Z)
        if X * Z * C != n:
            raise ValueError
    except Exception:
        X, Z, C = 4, 8, 2
        if X * Z * C != n:
            X, Z, C = 1, n // 2, 2
    return X, Z, C


def coordinates(X, Z, C):
    e = lax.axis_index("expert")
    return e // (Z * C), (e // C) % Z, e % C


def wrap(v, n):
    return (v + 4 * n) % n


def device(X, Z, C, x, z, c):
    return {"expert": wrap(x, X) * (Z * C) + wrap(z, Z) * C + wrap(c, C)}


def peers(X, Z, C, x, z, c):
    out = [(x + k, z, c) for k in range(1, X)]
    if Z > 1:
        out.append((x, z + 1, c))
        if Z > 2:
            out.append((x, z - 1, c))
    if C > 1:
        out.append((x, z, c + 1))
    return out


def barrier(X, Z, C, x, z, c):
    sem = pltpu.get_barrier_semaphore()
    targets = peers(X, Z, C, x, z, c)
    for t in targets:
        pl.semaphore_signal(sem, inc=1, device_id=device(X, Z, C, *t), device_id_type=MESH)
    pl.semaphore_wait(sem, len(targets))


def barrier_all(n):
    me = lax.axis_index("expert")
    sem = pltpu.get_barrier_semaphore()

    for k in range(1, n):
        pl.semaphore_signal(sem, inc=1, device_id={"expert": (me + k) % n}, device_id_type=MESH)
    pl.semaphore_wait(sem, n - 1)


def exchange_copy(src_ref, dst_ref, k, send_sem, recv_sem):
    n = src_ref.shape[0]
    me = lax.axis_index("expert")
    target = (me + k) % n
    return pltpu.make_async_remote_copy(
        src_ref=src_ref.at[target], dst_ref=dst_ref.at[me], send_sem=send_sem.at[k - 1], recv_sem=recv_sem.at[k - 1],
        device_id={"expert": target}, device_id_type=MESH)


def exchange(src_ref, dst_ref, own_sem, send_sem, recv_sem):
    n = src_ref.shape[0]
    me = lax.axis_index("expert")
    own = pltpu.make_async_copy(src_ref.at[me], dst_ref.at[me], own_sem)
    own.start()

    for k in range(1, n):
        exchange_copy(src_ref, dst_ref, k, send_sem, recv_sem).start()
    return own


def exchange_wait(src_ref, dst_ref, own, send_sem, recv_sem):
    n = src_ref.shape[0]
    own.wait()

    for k in range(1, n):
        cp = exchange_copy(src_ref, dst_ref, k, send_sem, recv_sem)
        cp.wait_recv()
        cp.wait_send()


def plane_peers(X, Z, C, x, z, c):
    W = Z * C
    w = z * C + c
    return [{"expert": wrap(x + k, X) * W + w} for k in range(1, X)] + [
        {"expert": x * W + wrap(w + k, W)} for k in range(1, W)]


def barrier_plane(X, Z, C, x, z, c):
    sem = pltpu.get_barrier_semaphore()
    targets = plane_peers(X, Z, C, x, z, c)
    for t in targets:
        pl.semaphore_signal(sem, inc=1, device_id=t, device_id_type=MESH)
    pl.semaphore_wait(sem, len(targets))


def two_stage(X, Z, C, x, z, c):
    W = Z * C
    w = z * C + c
    return W, w


def stage_x(X, Z, C, src_of, dst_of, own_sem, send_sem, recv_sem):
    x, z, c = coordinates(X, Z, C)
    W, w = two_stage(X, Z, C, x, z, c)
    own = pltpu.make_async_copy(src_of(x), dst_of(x), own_sem)
    own.start()
    copies = []
    for k in range(1, X):
        cp = pltpu.make_async_remote_copy(
            src_ref=src_of(wrap(x + k, X)), dst_ref=dst_of(x), send_sem=send_sem.at[k - 1], recv_sem=recv_sem.at[k - 1],
            device_id={"expert": wrap(x + k, X) * W + w}, device_id_type=MESH)
        cp.start()
        copies.append(cp)
    return [own] + copies


def stage_w(X, Z, C, src_of, dst_of, own_sem, send_sem, recv_sem):
    x, z, c = coordinates(X, Z, C)
    W, w = two_stage(X, Z, C, x, z, c)
    own = pltpu.make_async_copy(src_of(w), dst_of(w), own_sem)
    own.start()
    copies = []
    for k in range(1, W):
        cp = pltpu.make_async_remote_copy(
            src_ref=src_of(wrap(w + k, W)), dst_ref=dst_of(w), send_sem=send_sem.at[k - 1], recv_sem=recv_sem.at[k - 1],
            device_id={"expert": x * W + wrap(w + k, W)}, device_id_type=MESH)
        cp.start()
        copies.append(cp)
    return [own] + copies


def wait_recvs(copies):
    copies[0].wait()
    for cp in copies[1:]:
        cp.wait_recv()


def wait_sends(copies):
    for cp in copies[1:]:
        cp.wait_send()


def gather_kernel(X, Z, C, tok_ref, wg_ref, wu_ref, wd_ref, out_ref, pg_ref, pu_ref, pd_ref,
                  own_sem, w_send, w_recv, sx_send, sx_recv, sp_send, sp_recv, sm_send, sm_recv, sc_send, sc_recv):
    x, z, c = coordinates(X, Z, C)
    zp, zm = Z // 2, (Z - 1) // 2
    dirn = 1 - 2 * (c % 2)
    barrier_plane(X, Z, C, x, z, c)

    own = pltpu.make_async_copy(tok_ref, out_ref.at[c, z, x], own_sem.at[0])
    own.start()
    xcopies = []
    for k in range(1, X):
        cp = pltpu.make_async_remote_copy(
            src_ref=tok_ref, dst_ref=out_ref.at[c, z, x], send_sem=sx_send.at[k - 1], recv_sem=sx_recv.at[k - 1],
            device_id=device(X, Z, C, x + k, z, c), device_id_type=MESH)
        cp.start()
        xcopies.append(cp)
    own.wait()
    for cp in xcopies:
        cp.wait_recv()

    ccopies = []

    def to_partner(j, blk):
        if C == 1:
            return
        cp = pltpu.make_async_remote_copy(
            src_ref=out_ref.at[c, blk], dst_ref=out_ref.at[c, blk], send_sem=sc_send.at[j], recv_sem=sc_recv.at[j],
            device_id=device(X, Z, C, x, z, c + 1), device_id_type=MESH)
        cp.start()
        ccopies.append(cp)

    to_partner(0, z)
    plus, minus = [], []
    wcopies = []
    for s in range(max(zp, zm)):
        if s < zp:
            if s >= 1:
                plus[s - 1].wait_recv()
                to_partner(s, wrap(z - s * dirn, Z))
            blk = wrap(z - s * dirn, Z)
            cp = pltpu.make_async_remote_copy(
                src_ref=out_ref.at[c, blk], dst_ref=out_ref.at[c, blk], send_sem=sp_send.at[s],
                recv_sem=sp_recv.at[s], device_id=device(X, Z, C, x, z + dirn, c), device_id_type=MESH)
            cp.start()
            plus.append(cp)
        if s < zm:
            if s >= 1:
                minus[s - 1].wait_recv()
                to_partner(zp + s, wrap(z + s * dirn, Z))
            blk = wrap(z + s * dirn, Z)
            cp = pltpu.make_async_remote_copy(
                src_ref=out_ref.at[c, blk], dst_ref=out_ref.at[c, blk], send_sem=sm_send.at[s],
                recv_sem=sm_recv.at[s], device_id=device(X, Z, C, x, z - dirn, c), device_id_type=MESH)
            cp.start()
            minus.append(cp)
        if s == 0 and C > 1:
            for j, (src, dst) in enumerate(((wg_ref, pg_ref), (wu_ref, pu_ref), (wd_ref, pd_ref))):
                cp = pltpu.make_async_remote_copy(
                    src_ref=src, dst_ref=dst, send_sem=w_send.at[j], recv_sem=w_recv.at[j],
                    device_id=device(X, Z, C, x, z, c + 1), device_id_type=MESH)
                cp.start()
                wcopies.append(cp)
    if zp:
        plus[zp - 1].wait_recv()
        to_partner(zp, wrap(z - zp * dirn, Z))
    if zm:
        minus[zm - 1].wait_recv()
        to_partner(zp + zm, wrap(z + zm * dirn, Z))
    for cp in ccopies:
        cp.wait_recv()
    for cp in xcopies + plus + minus + ccopies:
        cp.wait_send()
    for cp in wcopies:
        cp.wait_recv()
        cp.wait_send()


def scatter_kernel(X, Z, C, o_ref, cold_ref, out_ref, cold_out, cold_mid, own_sem, c1_send, c1_recv, c2_send, c2_recv, plus_buf, plus_send, minus_buf, minus_send, xbuf, xsend,
                   sp_send, sp_recv, sm_send, sm_recv, sx_send, sx_recv):
    x, z, c = coordinates(X, Z, C)
    zp, zm = Z // 2, (Z - 1) // 2
    dirn = 1 - 2 * (c % 2)
    barrier_plane(X, Z, C, x, z, c)

    def chip_sum(blk):
        return o_ref[blk].astype(jnp.float32)

    plus, minus = [], []
    for s in range(max(zp, zm)):
        if s < zp:
            val = chip_sum(wrap(z + (zp - s) * dirn, Z))
            if s >= 1:
                plus[s - 1].wait_recv()
                val = val + plus_buf[s - 1].astype(jnp.float32)
            plus_send[s] = val.astype(jnp.bfloat16)
            cp = pltpu.make_async_remote_copy(
                src_ref=plus_send.at[s], dst_ref=plus_buf.at[s], send_sem=sp_send.at[s], recv_sem=sp_recv.at[s],
                device_id=device(X, Z, C, x, z + dirn, c), device_id_type=MESH)
            cp.start()
            plus.append(cp)
        if s < zm:
            val = chip_sum(wrap(z - (zm - s) * dirn, Z))
            if s >= 1:
                minus[s - 1].wait_recv()
                val = val + minus_buf[s - 1].astype(jnp.float32)
            minus_send[s] = val.astype(jnp.bfloat16)
            cp = pltpu.make_async_remote_copy(
                src_ref=minus_send.at[s], dst_ref=minus_buf.at[s], send_sem=sm_send.at[s], recv_sem=sm_recv.at[s],
                device_id=device(X, Z, C, x, z - dirn, c), device_id_type=MESH)
            cp.start()
            minus.append(cp)
        if s == 0:
            cold1 = stage_w(X, Z, C, lambda i: cold_ref.at[i], lambda i: cold_mid.at[i], own_sem.at[0], c2_send, c2_recv)
    wait_recvs(cold1)
    cold2 = stage_x(X, Z, C, lambda i: cold_mid.at[:, i], lambda i: cold_out.at[i], own_sem.at[1], c1_send, c1_recv)
    total = chip_sum(z)
    if zp:
        plus[zp - 1].wait_recv()
        total = total + plus_buf[zp - 1].astype(jnp.float32)
    if zm:
        minus[zm - 1].wait_recv()
        total = total + minus_buf[zm - 1].astype(jnp.float32)
    xsend[...] = total.astype(jnp.bfloat16)
    xcopies = []
    for k in range(1, X):
        cp = pltpu.make_async_remote_copy(
            src_ref=xsend.at[(x + k) % X], dst_ref=xbuf.at[k - 1], send_sem=sx_send.at[k - 1], recv_sem=sx_recv.at[k - 1],
            device_id=device(X, Z, C, x + k, z, c), device_id_type=MESH)
        cp.start()
        xcopies.append(cp)
    result = xsend[x].astype(jnp.float32)
    for k, cp in enumerate(xcopies):
        cp.wait_recv()
        result = result + xbuf[k].astype(jnp.float32)
    out_ref[...] = result.astype(out_ref.dtype)
    for cp in plus + minus + xcopies:
        cp.wait_send()
    wait_recvs(cold2)
    wait_sends(cold1)
    wait_sends(cold2)


def hot_gather(X, Z, C, tokens, w_gate, w_up, w_down):
    R, D = tokens.shape
    zp, zm = Z // 2, (Z - 1) // 2
    dma = pltpu.SemaphoreType.DMA
    vmem = pl.BlockSpec(memory_space=pltpu.VMEM)
    anywhere = pl.BlockSpec(memory_space=pl.ANY)
    return pl.pallas_call(
        functools.partial(gather_kernel, X, Z, C),
        out_shape=(
            jax.ShapeDtypeStruct((C, Z, X, R, D), tokens.dtype),
            jax.ShapeDtypeStruct(w_gate.shape, w_gate.dtype), jax.ShapeDtypeStruct(w_up.shape, w_up.dtype),
            jax.ShapeDtypeStruct(w_down.shape, w_down.dtype),
        ),
        in_specs=[vmem, anywhere, anywhere, anywhere],
        out_specs=(vmem, anywhere, anywhere, anywhere),
        scratch_shapes=[
            dma((1,)), dma((3,)), dma((3,)),
            dma((max(X - 1, 1),)), dma((max(X - 1, 1),)),
            dma((max(zp, 1),)), dma((max(zp, 1),)),
            dma((max(zm, 1),)), dma((max(zm, 1),)),
            dma((Z,)), dma((Z,)),
        ],
        compiler_params=pltpu.CompilerParams(collective_id=0, has_side_effects=True),
    )(tokens, w_gate, w_up, w_down)


def hot_scatter(X, Z, C, answered, cold_answered):
    _, _, R, D = answered.shape
    zp, zm = Z // 2, (Z - 1) // 2
    W, _, S, _ = cold_answered.shape
    dma = pltpu.SemaphoreType.DMA
    bf = answered.dtype
    vmem = pl.BlockSpec(memory_space=pltpu.VMEM)
    return pl.pallas_call(
        functools.partial(scatter_kernel, X, Z, C),
        out_shape=(jax.ShapeDtypeStruct((R, D), bf), jax.ShapeDtypeStruct((X, W, S, D), cold_answered.dtype)),
        in_specs=[vmem, vmem],
        out_specs=(vmem, vmem),
        scratch_shapes=[
            pltpu.VMEM((W, X, S, D), cold_answered.dtype),
            dma((2,)), dma((max(X - 1, 1),)), dma((max(X - 1, 1),)), dma((W - 1,)), dma((W - 1,)),
            pltpu.VMEM((max(zp, 1), X, R, D), bf), pltpu.VMEM((max(zp, 1), X, R, D), bf),
            pltpu.VMEM((max(zm, 1), X, R, D), bf), pltpu.VMEM((max(zm, 1), X, R, D), bf),
            pltpu.VMEM((max(X - 1, 1), R, D), bf), pltpu.VMEM((X, R, D), bf),
            dma((max(zp, 1),)), dma((max(zp, 1),)),
            dma((max(zm, 1),)), dma((max(zm, 1),)),
            dma((max(X - 1, 1),)), dma((max(X - 1, 1),)),
        ],
        compiler_params=pltpu.CompilerParams(collective_id=1, has_side_effects=True),
    )(answered, cold_answered)


def shards(X, Z, C, tokens, routes, gate_weights, w_gate, w_up, w_down):
    devices = lax.axis_size("expert")
    experts = w_gate.shape[0] * devices
    row_count = routes.shape[0]
    top_count = routes.shape[1]
    model_width = tokens.shape[1]
    slot_count = (row_count * (top_count - 1) + experts - 2) // (experts - 1)
    cold_ids = routes[:, 1:]
    flat_ids = cold_ids.reshape(-1)
    expert_iota = jnp.arange(experts, dtype=jnp.int32)
    one_hot = (flat_ids[:, None] == expert_iota[None, :]).astype(jnp.int32)
    slot_rank = (jnp.sum(jnp.cumsum(one_hot, axis=0) * one_hot, axis=1) - 1).reshape(cold_ids.shape)
    slot_iota = jnp.arange(slot_count, dtype=jnp.int32)
    local_gate = w_gate.reshape(w_gate.shape[1:])
    local_up = w_up.reshape(w_up.shape[1:])
    local_down = w_down.reshape(w_down.shape[1:])
    hot_expert = routes[0, 0]
    me = lax.axis_index("expert")
    cores = C
    same_chip = me // cores == hot_expert // cores
    role = jnp.where(me == hot_expert, 0, jnp.where(same_chip, 1, 2))
    lanes = 128
    carried = jnp.zeros((row_count, lanes), jnp.bfloat16).at[:, :top_count].set(routes.astype(jnp.bfloat16))
    rows_out = jnp.concatenate([tokens, carried], axis=1)
    gathered, partner_gate, partner_up, partner_down = hot_gather(X, Z, C, rows_out, local_gate, local_up, local_down)
    all_tokens = gathered[..., :model_width]
    all_routes = gathered[..., model_width:model_width + top_count].astype(jnp.int32)
    mine = all_routes[..., 1:] == me
    flat_mine = mine.reshape(C, Z, X, -1).astype(jnp.int32)
    rank = (jnp.cumsum(flat_mine, axis=-1) - 1).reshape(mine.shape)
    taking = (mine[..., None, :, :] & (rank[..., None, :, :] == slot_iota[:, None, None])).astype(jnp.bfloat16)
    taking = jnp.sum(taking, axis=-1)
    arrived = jnp.einsum("czxsr,czxrd->zcxsd", taking, all_tokens, preferred_element_type=jnp.float32).astype(jnp.bfloat16)
    arrived = arrived.reshape(Z * C, X, slot_count, model_width)
    flat_rows = arrived.reshape(-1, model_width)
    answered = feed_forward(flat_rows, local_gate, local_up, local_down).reshape(arrived.shape)

    def hot_ffn(gate_w, up_w, down_w):
        return lambda row_block: feed_forward(row_block.reshape(-1, model_width), gate_w, up_w, down_w).reshape(row_block.shape)

    own_half = lax.dynamic_index_in_dim(all_tokens, me % cores, 0, keepdims=False)
    hot_answer = lax.switch(
        role,
        [hot_ffn(local_gate, local_up, local_down), hot_ffn(partner_gate, partner_up, partner_down), jnp.zeros_like],
        own_half,
    )
    hot_out, returned = hot_scatter(X, Z, C, hot_answer, answered)
    returned = returned.reshape(experts, slot_count, model_width)
    picked = returned.reshape(-1, model_width)[cold_ids * slot_count + slot_rank]
    combined = gate_weights[:, 0:1] * hot_out.astype(jnp.float32) + jnp.sum(
        gate_weights[:, 1:, None] * picked.astype(jnp.float32), axis=1
    )
    return combined.astype(jnp.bfloat16)


def solution(mesh):
    X, Z, C = torus_shape(mesh)
    in_specs = (
        P(("dp", "expert"), None),
        P(("dp", "expert"), None),
        P(("dp", "expert"), None),
        P("expert", None, None),
        P("expert", None, None),
        P("expert", None, None),
    )
    out_specs = P(("dp", "expert"), None)
    return jax.shard_map(functools.partial(shards, X, Z, C), mesh=mesh, in_specs=in_specs, out_specs=out_specs, check_vma=False)
```

```python
import functools

import jax
import jax.numpy as jnp
from jax import lax
from jax.experimental import pallas as pl
from jax.experimental.pallas import tpu as pltpu
from jax.sharding import PartitionSpec as P

MESH = pl.DeviceIdType.MESH


def feed_forward(row_block, gate_w, up_w, down_w):
    gate_part = jnp.dot(row_block, gate_w, preferred_element_type=jnp.float32)
    up_part = jnp.dot(row_block, up_w, preferred_element_type=jnp.float32)
    hidden = lax.optimization_barrier((jax.nn.silu(gate_part) * up_part).astype(jnp.bfloat16))
    return jnp.dot(hidden, down_w, preferred_element_type=jnp.float32).astype(jnp.bfloat16)


def torus_shape(mesh):
    n = mesh.shape["expert"]
    try:
        row = mesh.devices.reshape(-1, n)[0]
        xs = {d.coords[0] for d in row}
        zs = {d.coords[2] for d in row}
        X, Z = len(xs), len(zs)
        C = n // (X * Z)
        if X * Z * C != n:
            raise ValueError
    except Exception:
        X, Z, C = 4, 8, 2
        if X * Z * C != n:
            X, Z, C = 1, n // 2, 2
    return X, Z, C


def coordinates(X, Z, C):
    e = lax.axis_index("expert")
    return e // (Z * C), (e // C) % Z, e % C


def wrap(v, n):
    return (v + 4 * n) % n


def device(X, Z, C, x, z, c):
    return {"expert": wrap(x, X) * (Z * C) + wrap(z, Z) * C + wrap(c, C)}


def peers(X, Z, C, x, z, c):
    out = [(x + k, z, c) for k in range(1, X)]
    if Z > 1:
        out.append((x, z + 1, c))
        if Z > 2:
            out.append((x, z - 1, c))
    if C > 1:
        out.append((x, z, c + 1))
    return out


def barrier(X, Z, C, x, z, c):
    sem = pltpu.get_barrier_semaphore()
    targets = peers(X, Z, C, x, z, c)
    for t in targets:
        pl.semaphore_signal(sem, inc=1, device_id=device(X, Z, C, *t), device_id_type=MESH)
    pl.semaphore_wait(sem, len(targets))


def barrier_all(n):
    me = lax.axis_index("expert")
    sem = pltpu.get_barrier_semaphore()

    for k in range(1, n):
        pl.semaphore_signal(sem, inc=1, device_id={"expert": (me + k) % n}, device_id_type=MESH)
    pl.semaphore_wait(sem, n - 1)


def exchange_copy(src_ref, dst_ref, k, send_sem, recv_sem):
    n = src_ref.shape[0]
    me = lax.axis_index("expert")
    target = (me + k) % n
    return pltpu.make_async_remote_copy(
        src_ref=src_ref.at[target], dst_ref=dst_ref.at[me], send_sem=send_sem.at[k - 1], recv_sem=recv_sem.at[k - 1],
        device_id={"expert": target}, device_id_type=MESH)


def exchange(src_ref, dst_ref, own_sem, send_sem, recv_sem):
    n = src_ref.shape[0]
    me = lax.axis_index("expert")
    own = pltpu.make_async_copy(src_ref.at[me], dst_ref.at[me], own_sem)
    own.start()

    for k in range(1, n):
        exchange_copy(src_ref, dst_ref, k, send_sem, recv_sem).start()
    return own


def exchange_wait(src_ref, dst_ref, own, send_sem, recv_sem):
    n = src_ref.shape[0]
    own.wait()

    for k in range(1, n):
        cp = exchange_copy(src_ref, dst_ref, k, send_sem, recv_sem)
        cp.wait_recv()
        cp.wait_send()


def plane_peers(X, Z, C, x, z, c):
    W = Z * C
    w = z * C + c
    return [{"expert": wrap(x + k, X) * W + w} for k in range(1, X)] + [
        {"expert": x * W + wrap(w + k, W)} for k in range(1, W)]


def barrier_plane(X, Z, C, x, z, c):
    sem = pltpu.get_barrier_semaphore()
    targets = plane_peers(X, Z, C, x, z, c)
    for t in targets:
        pl.semaphore_signal(sem, inc=1, device_id=t, device_id_type=MESH)
    pl.semaphore_wait(sem, len(targets))


def two_stage(X, Z, C, x, z, c):
    W = Z * C
    w = z * C + c
    return W, w


def stage_x(X, Z, C, src_of, dst_of, own_sem, send_sem, recv_sem):
    x, z, c = coordinates(X, Z, C)
    W, w = two_stage(X, Z, C, x, z, c)
    own = pltpu.make_async_copy(src_of(x), dst_of(x), own_sem)
    own.start()
    copies = []
    for k in range(1, X):
        cp = pltpu.make_async_remote_copy(
            src_ref=src_of(wrap(x + k, X)), dst_ref=dst_of(x), send_sem=send_sem.at[k - 1], recv_sem=recv_sem.at[k - 1],
            device_id={"expert": wrap(x + k, X) * W + w}, device_id_type=MESH)
        cp.start()
        copies.append(cp)
    return [own] + copies


def stage_w(X, Z, C, src_of, dst_of, own_sem, send_sem, recv_sem):
    x, z, c = coordinates(X, Z, C)
    W, w = two_stage(X, Z, C, x, z, c)
    own = pltpu.make_async_copy(src_of(w), dst_of(w), own_sem)
    own.start()
    copies = []
    for k in range(1, W):
        cp = pltpu.make_async_remote_copy(
            src_ref=src_of(wrap(w + k, W)), dst_ref=dst_of(w), send_sem=send_sem.at[k - 1], recv_sem=recv_sem.at[k - 1],
            device_id={"expert": x * W + wrap(w + k, W)}, device_id_type=MESH)
        cp.start()
        copies.append(cp)
    return [own] + copies


def wait_recvs(copies):
    copies[0].wait()
    for cp in copies[1:]:
        cp.wait_recv()


def wait_sends(copies):
    for cp in copies[1:]:
        cp.wait_send()


def gather_kernel(X, Z, C, tok_ref, wg_ref, wu_ref, wd_ref, out_ref, pg_ref, pu_ref, pd_ref,
                  own_sem, w_send, w_recv, sx_send, sx_recv, sp_send, sp_recv, sm_send, sm_recv, sc_send, sc_recv):
    x, z, c = coordinates(X, Z, C)
    zp, zm = Z // 2, (Z - 1) // 2
    dirn = 1 - 2 * (c % 2)
    barrier_plane(X, Z, C, x, z, c)

    own = pltpu.make_async_copy(tok_ref, out_ref.at[c, z, x], own_sem.at[0])
    own.start()
    xcopies = []
    for k in range(1, X):
        cp = pltpu.make_async_remote_copy(
            src_ref=tok_ref, dst_ref=out_ref.at[c, z, x], send_sem=sx_send.at[k - 1], recv_sem=sx_recv.at[k - 1],
            device_id=device(X, Z, C, x + k, z, c), device_id_type=MESH)
        cp.start()
        xcopies.append(cp)
    own.wait()
    for cp in xcopies:
        cp.wait_recv()

    ccopies = []

    def to_partner(j, blk):
        if C == 1:
            return
        cp = pltpu.make_async_remote_copy(
            src_ref=out_ref.at[c, blk], dst_ref=out_ref.at[c, blk], send_sem=sc_send.at[j], recv_sem=sc_recv.at[j],
            device_id=device(X, Z, C, x, z, c + 1), device_id_type=MESH)
        cp.start()
        ccopies.append(cp)

    to_partner(0, z)
    plus, minus = [], []
    wcopies = []
    for s in range(max(zp, zm)):
        if s < zp:
            if s >= 1:
                plus[s - 1].wait_recv()
                to_partner(s, wrap(z - s * dirn, Z))
            blk = wrap(z - s * dirn, Z)
            cp = pltpu.make_async_remote_copy(
                src_ref=out_ref.at[c, blk], dst_ref=out_ref.at[c, blk], send_sem=sp_send.at[s],
                recv_sem=sp_recv.at[s], device_id=device(X, Z, C, x, z + dirn, c), device_id_type=MESH)
            cp.start()
            plus.append(cp)
        if s < zm:
            if s >= 1:
                minus[s - 1].wait_recv()
                to_partner(zp + s, wrap(z + s * dirn, Z))
            blk = wrap(z + s * dirn, Z)
            cp = pltpu.make_async_remote_copy(
                src_ref=out_ref.at[c, blk], dst_ref=out_ref.at[c, blk], send_sem=sm_send.at[s],
                recv_sem=sm_recv.at[s], device_id=device(X, Z, C, x, z - dirn, c), device_id_type=MESH)
            cp.start()
            minus.append(cp)
        if s == 0 and C > 1:
            for j, (src, dst) in enumerate(((wg_ref, pg_ref), (wu_ref, pu_ref), (wd_ref, pd_ref))):
                cp = pltpu.make_async_remote_copy(
                    src_ref=src, dst_ref=dst, send_sem=w_send.at[j], recv_sem=w_recv.at[j],
                    device_id=device(X, Z, C, x, z, c + 1), device_id_type=MESH)
                cp.start()
                wcopies.append(cp)
    if zp:
        plus[zp - 1].wait_recv()
        to_partner(zp, wrap(z - zp * dirn, Z))
    if zm:
        minus[zm - 1].wait_recv()
        to_partner(zp + zm, wrap(z + zm * dirn, Z))
    for cp in ccopies:
        cp.wait_recv()
    for cp in xcopies + plus + minus + ccopies:
        cp.wait_send()
    for cp in wcopies:
        cp.wait_recv()
        cp.wait_send()


def scatter_kernel(X, Z, C, o_ref, cold_ref, out_ref, cold_out, cold_mid, own_sem, c1_send, c1_recv, c2_send, c2_recv, plus_buf, plus_send, minus_buf, minus_send, xbuf, xsend,
                   sp_send, sp_recv, sm_send, sm_recv, sx_send, sx_recv):
    x, z, c = coordinates(X, Z, C)
    zp, zm = Z // 2, (Z - 1) // 2
    dirn = 1 - 2 * (c % 2)
    barrier_plane(X, Z, C, x, z, c)

    def chip_sum(blk):
        return o_ref[blk].astype(jnp.float32)

    plus, minus = [], []
    for s in range(max(zp, zm)):
        if s < zp:
            val = chip_sum(wrap(z + (zp - s) * dirn, Z))
            if s >= 1:
                plus[s - 1].wait_recv()
                val = val + plus_buf[s - 1].astype(jnp.float32)
            plus_send[s] = val.astype(jnp.bfloat16)
            cp = pltpu.make_async_remote_copy(
                src_ref=plus_send.at[s], dst_ref=plus_buf.at[s], send_sem=sp_send.at[s], recv_sem=sp_recv.at[s],
                device_id=device(X, Z, C, x, z + dirn, c), device_id_type=MESH)
            cp.start()
            plus.append(cp)
        if s < zm:
            val = chip_sum(wrap(z - (zm - s) * dirn, Z))
            if s >= 1:
                minus[s - 1].wait_recv()
                val = val + minus_buf[s - 1].astype(jnp.float32)
            minus_send[s] = val.astype(jnp.bfloat16)
            cp = pltpu.make_async_remote_copy(
                src_ref=minus_send.at[s], dst_ref=minus_buf.at[s], send_sem=sm_send.at[s], recv_sem=sm_recv.at[s],
                device_id=device(X, Z, C, x, z - dirn, c), device_id_type=MESH)
            cp.start()
            minus.append(cp)
        if s == 0:
            cold1 = stage_w(X, Z, C, lambda i: cold_ref.at[i], lambda i: cold_mid.at[i], own_sem.at[0], c2_send, c2_recv)
    wait_recvs(cold1)
    cold2 = stage_x(X, Z, C, lambda i: cold_mid.at[:, i], lambda i: cold_out.at[i], own_sem.at[1], c1_send, c1_recv)
    total = chip_sum(z)
    if zp:
        plus[zp - 1].wait_recv()
        total = total + plus_buf[zp - 1].astype(jnp.float32)
    if zm:
        minus[zm - 1].wait_recv()
        total = total + minus_buf[zm - 1].astype(jnp.float32)
    xsend[...] = total.astype(jnp.bfloat16)
    xcopies = []
    for k in range(1, X):
        cp = pltpu.make_async_remote_copy(
            src_ref=xsend.at[(x + k) % X], dst_ref=xbuf.at[k - 1], send_sem=sx_send.at[k - 1], recv_sem=sx_recv.at[k - 1],
            device_id=device(X, Z, C, x + k, z, c), device_id_type=MESH)
        cp.start()
        xcopies.append(cp)
    result = xsend[x].astype(jnp.float32)
    for k, cp in enumerate(xcopies):
        cp.wait_recv()
        result = result + xbuf[k].astype(jnp.float32)
    out_ref[...] = result.astype(out_ref.dtype)
    for cp in plus + minus + xcopies:
        cp.wait_send()
    wait_recvs(cold2)
    wait_sends(cold1)
    wait_sends(cold2)


def hot_gather(X, Z, C, tokens, w_gate, w_up, w_down):
    R, D = tokens.shape
    zp, zm = Z // 2, (Z - 1) // 2
    dma = pltpu.SemaphoreType.DMA
    vmem = pl.BlockSpec(memory_space=pltpu.VMEM)
    anywhere = pl.BlockSpec(memory_space=pl.ANY)
    return pl.pallas_call(
        functools.partial(gather_kernel, X, Z, C),
        out_shape=(
            jax.ShapeDtypeStruct((C, Z, X, R, D), tokens.dtype),
            jax.ShapeDtypeStruct(w_gate.shape, w_gate.dtype), jax.ShapeDtypeStruct(w_up.shape, w_up.dtype),
            jax.ShapeDtypeStruct(w_down.shape, w_down.dtype),
        ),
        in_specs=[vmem, anywhere, anywhere, anywhere],
        out_specs=(vmem, anywhere, anywhere, anywhere),
        scratch_shapes=[
            dma((1,)), dma((3,)), dma((3,)),
            dma((max(X - 1, 1),)), dma((max(X - 1, 1),)),
            dma((max(zp, 1),)), dma((max(zp, 1),)),
            dma((max(zm, 1),)), dma((max(zm, 1),)),
            dma((Z,)), dma((Z,)),
        ],
        compiler_params=pltpu.CompilerParams(collective_id=0, has_side_effects=True),
    )(tokens, w_gate, w_up, w_down)


def hot_scatter(X, Z, C, answered, cold_answered):
    _, _, R, D = answered.shape
    zp, zm = Z // 2, (Z - 1) // 2
    W, _, S, _ = cold_answered.shape
    dma = pltpu.SemaphoreType.DMA
    bf = answered.dtype
    vmem = pl.BlockSpec(memory_space=pltpu.VMEM)
    return pl.pallas_call(
        functools.partial(scatter_kernel, X, Z, C),
        out_shape=(jax.ShapeDtypeStruct((R, D), bf), jax.ShapeDtypeStruct((X, W, S, D), cold_answered.dtype)),
        in_specs=[vmem, vmem],
        out_specs=(vmem, vmem),
        scratch_shapes=[
            pltpu.VMEM((W, X, S, D), cold_answered.dtype),
            dma((2,)), dma((max(X - 1, 1),)), dma((max(X - 1, 1),)), dma((W - 1,)), dma((W - 1,)),
            pltpu.VMEM((max(zp, 1), X, R, D), bf), pltpu.VMEM((max(zp, 1), X, R, D), bf),
            pltpu.VMEM((max(zm, 1), X, R, D), bf), pltpu.VMEM((max(zm, 1), X, R, D), bf),
            pltpu.VMEM((max(X - 1, 1), R, D), bf), pltpu.VMEM((X, R, D), bf),
            dma((max(zp, 1),)), dma((max(zp, 1),)),
            dma((max(zm, 1),)), dma((max(zm, 1),)),
            dma((max(X - 1, 1),)), dma((max(X - 1, 1),)),
        ],
        compiler_params=pltpu.CompilerParams(collective_id=1, has_side_effects=True),
    )(answered, cold_answered)


def shards(X, Z, C, tokens, routes, gate_weights, w_gate, w_up, w_down):
    devices = lax.axis_size("expert")
    experts = w_gate.shape[0] * devices
    row_count = routes.shape[0]
    top_count = routes.shape[1]
    model_width = tokens.shape[1]
    slot_count = (row_count * (top_count - 1) + experts - 2) // (experts - 1)
    cold_ids = routes[:, 1:]
    flat_ids = cold_ids.reshape(-1)
    expert_iota = jnp.arange(experts, dtype=jnp.int32)
    one_hot = (flat_ids[:, None] == expert_iota[None, :]).astype(jnp.int32)
    slot_rank = (jnp.sum(jnp.cumsum(one_hot, axis=0) * one_hot, axis=1) - 1).reshape(cold_ids.shape)
    slot_iota = jnp.arange(slot_count, dtype=jnp.int32)
    local_gate = w_gate.reshape(w_gate.shape[1:])
    local_up = w_up.reshape(w_up.shape[1:])
    local_down = w_down.reshape(w_down.shape[1:])
    hot_expert = routes[0, 0]
    me = lax.axis_index("expert")
    cores = C
    same_chip = me // cores == hot_expert // cores
    role = jnp.where(me == hot_expert, 0, jnp.where(same_chip, 1, 2))
    lanes = 128
    carried = jnp.zeros((row_count, lanes), jnp.bfloat16).at[:, :top_count].set(routes.astype(jnp.bfloat16))
    rows_out = jnp.concatenate([tokens, carried], axis=1)
    gathered, partner_gate, partner_up, partner_down = hot_gather(X, Z, C, rows_out, local_gate, local_up, local_down)
    all_tokens = gathered[..., :model_width]
    all_routes = gathered[..., model_width:model_width + top_count].astype(jnp.int32)
    mine = (all_routes[..., 1:] == me).reshape(C * Z * X, -1)
    width = mine.shape[1]
    earlier = (jnp.arange(width)[:, None] < jnp.arange(width)[None, :]).astype(jnp.float32)
    rank = jnp.dot(mine.astype(jnp.float32), earlier).astype(jnp.int32)
    row_of = (jnp.arange(width, dtype=jnp.int32) // (top_count - 1))[None, :]
    picks = [jnp.sum(jnp.where(mine & (rank == k), row_of, 0), axis=1) for k in range(slot_count)]
    source = jnp.arange(C * Z * X, dtype=jnp.int32)
    index = jnp.stack([source * row_count + p for p in picks], axis=1)
    index = index.reshape(C, Z, X, slot_count).transpose(1, 0, 2, 3).reshape(-1)
    arrived = gathered.reshape(-1, gathered.shape[-1])[index][:, :model_width]
    arrived = arrived.reshape(Z * C, X, slot_count, model_width)
    flat_rows = arrived.reshape(-1, model_width)
    answered = feed_forward(flat_rows, local_gate, local_up, local_down).reshape(arrived.shape)

    def hot_ffn(gate_w, up_w, down_w):
        return lambda row_block: feed_forward(row_block.reshape(-1, model_width), gate_w, up_w, down_w).reshape(row_block.shape)

    own_half = lax.dynamic_index_in_dim(all_tokens, me % cores, 0, keepdims=False)
    hot_answer = lax.switch(
        role,
        [hot_ffn(local_gate, local_up, local_down), hot_ffn(partner_gate, partner_up, partner_down), jnp.zeros_like],
        own_half,
    )
    hot_out, returned = hot_scatter(X, Z, C, hot_answer, answered)
    returned = returned.reshape(experts, slot_count, model_width)
    picked = returned.reshape(-1, model_width)[cold_ids * slot_count + slot_rank]
    combined = gate_weights[:, 0:1] * hot_out.astype(jnp.float32) + jnp.sum(
        gate_weights[:, 1:, None] * picked.astype(jnp.float32), axis=1
    )
    return combined.astype(jnp.bfloat16)


def solution(mesh):
    X, Z, C = torus_shape(mesh)
    in_specs = (
        P(("dp", "expert"), None),
        P(("dp", "expert"), None),
        P(("dp", "expert"), None),
        P("expert", None, None),
        P("expert", None, None),
        P("expert", None, None),
    )
    out_specs = P(("dp", "expert"), None)
    return jax.shard_map(functools.partial(shards, X, Z, C), mesh=mesh, in_specs=in_specs, out_specs=out_specs, check_vma=False)
```

```python
import functools

import jax
import jax.numpy as jnp
from jax import lax
from jax.experimental import pallas as pl
from jax.experimental.pallas import tpu as pltpu
from jax.sharding import PartitionSpec as P

MESH = pl.DeviceIdType.MESH


def feed_forward(row_block, gate_w, up_w, down_w):
    gate_part = jnp.dot(row_block, gate_w, preferred_element_type=jnp.float32)
    up_part = jnp.dot(row_block, up_w, preferred_element_type=jnp.float32)
    hidden = lax.optimization_barrier((jax.nn.silu(gate_part) * up_part).astype(jnp.bfloat16))
    return jnp.dot(hidden, down_w, preferred_element_type=jnp.float32).astype(jnp.bfloat16)


def torus_shape(mesh):
    n = mesh.shape["expert"]
    try:
        row = mesh.devices.reshape(-1, n)[0]
        xs = {d.coords[0] for d in row}
        zs = {d.coords[2] for d in row}
        X, Z = len(xs), len(zs)
        C = n // (X * Z)
        if X * Z * C != n:
            raise ValueError
    except Exception:
        X, Z, C = 4, 8, 2
        if X * Z * C != n:
            X, Z, C = 1, n // 2, 2
    return X, Z, C


def coordinates(X, Z, C):
    e = lax.axis_index("expert")
    return e // (Z * C), (e // C) % Z, e % C


def wrap(v, n):
    return (v + 4 * n) % n


def device(X, Z, C, x, z, c):
    return {"expert": wrap(x, X) * (Z * C) + wrap(z, Z) * C + wrap(c, C)}


def peers(X, Z, C, x, z, c):
    out = [(x + k, z, c) for k in range(1, X)]
    if Z > 1:
        out.append((x, z + 1, c))
        if Z > 2:
            out.append((x, z - 1, c))
    if C > 1:
        out.append((x, z, c + 1))
    return out


def barrier(X, Z, C, x, z, c):
    sem = pltpu.get_barrier_semaphore()
    targets = peers(X, Z, C, x, z, c)
    for t in targets:
        pl.semaphore_signal(sem, inc=1, device_id=device(X, Z, C, *t), device_id_type=MESH)
    pl.semaphore_wait(sem, len(targets))


def barrier_all(n):
    me = lax.axis_index("expert")
    sem = pltpu.get_barrier_semaphore()

    for k in range(1, n):
        pl.semaphore_signal(sem, inc=1, device_id={"expert": (me + k) % n}, device_id_type=MESH)
    pl.semaphore_wait(sem, n - 1)


def exchange_copy(src_ref, dst_ref, k, send_sem, recv_sem):
    n = src_ref.shape[0]
    me = lax.axis_index("expert")
    target = (me + k) % n
    return pltpu.make_async_remote_copy(
        src_ref=src_ref.at[target], dst_ref=dst_ref.at[me], send_sem=send_sem.at[k - 1], recv_sem=recv_sem.at[k - 1],
        device_id={"expert": target}, device_id_type=MESH)


def exchange(src_ref, dst_ref, own_sem, send_sem, recv_sem):
    n = src_ref.shape[0]
    me = lax.axis_index("expert")
    own = pltpu.make_async_copy(src_ref.at[me], dst_ref.at[me], own_sem)
    own.start()

    for k in range(1, n):
        exchange_copy(src_ref, dst_ref, k, send_sem, recv_sem).start()
    return own


def exchange_wait(src_ref, dst_ref, own, send_sem, recv_sem):
    n = src_ref.shape[0]
    own.wait()

    for k in range(1, n):
        cp = exchange_copy(src_ref, dst_ref, k, send_sem, recv_sem)
        cp.wait_recv()
        cp.wait_send()


def plane_peers(X, Z, C, x, z, c):
    W = Z * C
    w = z * C + c
    return [{"expert": wrap(x + k, X) * W + w} for k in range(1, X)] + [
        {"expert": x * W + wrap(w + k, W)} for k in range(1, W)]


def barrier_plane(X, Z, C, x, z, c):
    sem = pltpu.get_barrier_semaphore()
    targets = plane_peers(X, Z, C, x, z, c)
    for t in targets:
        pl.semaphore_signal(sem, inc=1, device_id=t, device_id_type=MESH)
    pl.semaphore_wait(sem, len(targets))


def two_stage(X, Z, C, x, z, c):
    W = Z * C
    w = z * C + c
    return W, w


def stage_x(X, Z, C, src_of, dst_of, own_sem, send_sem, recv_sem):
    x, z, c = coordinates(X, Z, C)
    W, w = two_stage(X, Z, C, x, z, c)
    own = pltpu.make_async_copy(src_of(x), dst_of(x), own_sem)
    own.start()
    copies = []
    for k in range(1, X):
        cp = pltpu.make_async_remote_copy(
            src_ref=src_of(wrap(x + k, X)), dst_ref=dst_of(x), send_sem=send_sem.at[k - 1], recv_sem=recv_sem.at[k - 1],
            device_id={"expert": wrap(x + k, X) * W + w}, device_id_type=MESH)
        cp.start()
        copies.append(cp)
    return [own] + copies


def stage_w(X, Z, C, src_of, dst_of, own_sem, send_sem, recv_sem):
    x, z, c = coordinates(X, Z, C)
    W, w = two_stage(X, Z, C, x, z, c)
    own = pltpu.make_async_copy(src_of(w), dst_of(w), own_sem)
    own.start()
    copies = []
    for k in range(1, W):
        cp = pltpu.make_async_remote_copy(
            src_ref=src_of(wrap(w + k, W)), dst_ref=dst_of(w), send_sem=send_sem.at[k - 1], recv_sem=recv_sem.at[k - 1],
            device_id={"expert": x * W + wrap(w + k, W)}, device_id_type=MESH)
        cp.start()
        copies.append(cp)
    return [own] + copies


def wait_recvs(copies):
    copies[0].wait()
    for cp in copies[1:]:
        cp.wait_recv()


def wait_sends(copies):
    for cp in copies[1:]:
        cp.wait_send()


def gather_kernel(X, Z, C, tok_ref, cold_ref, wg_ref, wu_ref, wd_ref, out_ref, cold_out, pg_ref, pu_ref, pd_ref,
                  cold_mid, own_sem, c1_send, c1_recv, c2_send, c2_recv, w_send, w_recv, sx_send, sx_recv, sp_send, sp_recv, sm_send, sm_recv):
    x, z, c = coordinates(X, Z, C)
    zp, zm = Z // 2, (Z - 1) // 2
    dirn = 1 - 2 * (c % 2)
    barrier_plane(X, Z, C, x, z, c)
    own = pltpu.make_async_copy(tok_ref, out_ref.at[z, x], own_sem.at[0])
    own.start()
    xcopies = []
    for k in range(1, X):
        cp = pltpu.make_async_remote_copy(
            src_ref=tok_ref, dst_ref=out_ref.at[z, x], send_sem=sx_send.at[k - 1], recv_sem=sx_recv.at[k - 1],
            device_id=device(X, Z, C, x + k, z, c), device_id_type=MESH)
        cp.start()
        xcopies.append(cp)
    own.wait()
    for cp in xcopies:
        cp.wait_recv()
    cold1 = stage_x(X, Z, C, lambda i: cold_ref.at[i], lambda i: cold_mid.at[:, i], own_sem.at[1], c1_send, c1_recv)

    plus, minus = [], []
    cold2 = None
    for s in range(max(zp, zm)):
        if s < zp:
            if s >= 1:
                plus[s - 1].wait_recv()
            blk = wrap(z - s * dirn, Z)
            cp = pltpu.make_async_remote_copy(
                src_ref=out_ref.at[blk], dst_ref=out_ref.at[blk], send_sem=sp_send.at[s],
                recv_sem=sp_recv.at[s], device_id=device(X, Z, C, x, z + dirn, c), device_id_type=MESH)
            cp.start()
            plus.append(cp)
        if s < zm:
            if s >= 1:
                minus[s - 1].wait_recv()
            blk = wrap(z + s * dirn, Z)
            cp = pltpu.make_async_remote_copy(
                src_ref=out_ref.at[blk], dst_ref=out_ref.at[blk], send_sem=sm_send.at[s],
                recv_sem=sm_recv.at[s], device_id=device(X, Z, C, x, z - dirn, c), device_id_type=MESH)
            cp.start()
            minus.append(cp)
        if s == 1:
            wait_recvs(cold1)
            cold2 = stage_w(X, Z, C, lambda i: cold_mid.at[i], lambda i: cold_out.at[i], own_sem.at[2], c2_send, c2_recv)
        if s == 0:
            wcopies = []
            if C > 1:
                for j, (src, dst) in enumerate(((wg_ref, pg_ref), (wu_ref, pu_ref), (wd_ref, pd_ref))):
                    cp = pltpu.make_async_remote_copy(
                        src_ref=src, dst_ref=dst, send_sem=w_send.at[j], recv_sem=w_recv.at[j],
                        device_id=device(X, Z, C, x, z, c + 1), device_id_type=MESH)
                    cp.start()
                    wcopies.append(cp)
    if cold2 is None:
        wait_recvs(cold1)
        cold2 = stage_w(X, Z, C, lambda i: cold_mid.at[i], lambda i: cold_out.at[i], own_sem.at[2], c2_send, c2_recv)
    if zp:
        plus[zp - 1].wait_recv()
    if zm:
        minus[zm - 1].wait_recv()
    for cp in xcopies + plus + minus:
        cp.wait_send()
    wait_recvs(cold2)
    wait_sends(cold1)
    wait_sends(cold2)
    for cp in wcopies:
        cp.wait_recv()
        cp.wait_send()


def scatter_kernel(X, Z, C, o_ref, cold_ref, out_ref, cold_out, cold_mid, own_sem, c1_send, c1_recv, c2_send, c2_recv, plus_buf, plus_send, minus_buf, minus_send, xbuf, xsend,
                   sp_send, sp_recv, sm_send, sm_recv, sx_send, sx_recv):
    x, z, c = coordinates(X, Z, C)
    zp, zm = Z // 2, (Z - 1) // 2
    dirn = 1 - 2 * (c % 2)
    barrier_plane(X, Z, C, x, z, c)

    def chip_sum(blk):
        return o_ref[blk].astype(jnp.float32)

    plus, minus = [], []
    for s in range(max(zp, zm)):
        if s < zp:
            val = chip_sum(wrap(z + (zp - s) * dirn, Z))
            if s >= 1:
                plus[s - 1].wait_recv()
                val = val + plus_buf[s - 1].astype(jnp.float32)
            plus_send[s] = val.astype(jnp.bfloat16)
            cp = pltpu.make_async_remote_copy(
                src_ref=plus_send.at[s], dst_ref=plus_buf.at[s], send_sem=sp_send.at[s], recv_sem=sp_recv.at[s],
                device_id=device(X, Z, C, x, z + dirn, c), device_id_type=MESH)
            cp.start()
            plus.append(cp)
        if s < zm:
            val = chip_sum(wrap(z - (zm - s) * dirn, Z))
            if s >= 1:
                minus[s - 1].wait_recv()
                val = val + minus_buf[s - 1].astype(jnp.float32)
            minus_send[s] = val.astype(jnp.bfloat16)
            cp = pltpu.make_async_remote_copy(
                src_ref=minus_send.at[s], dst_ref=minus_buf.at[s], send_sem=sm_send.at[s], recv_sem=sm_recv.at[s],
                device_id=device(X, Z, C, x, z - dirn, c), device_id_type=MESH)
            cp.start()
            minus.append(cp)
        if s == 0:
            cold1 = stage_w(X, Z, C, lambda i: cold_ref.at[i], lambda i: cold_mid.at[i], own_sem.at[0], c2_send, c2_recv)
    wait_recvs(cold1)
    cold2 = stage_x(X, Z, C, lambda i: cold_mid.at[:, i], lambda i: cold_out.at[i], own_sem.at[1], c1_send, c1_recv)
    total = chip_sum(z)
    if zp:
        plus[zp - 1].wait_recv()
        total = total + plus_buf[zp - 1].astype(jnp.float32)
    if zm:
        minus[zm - 1].wait_recv()
        total = total + minus_buf[zm - 1].astype(jnp.float32)
    xsend[...] = total.astype(jnp.bfloat16)
    xcopies = []
    for k in range(1, X):
        cp = pltpu.make_async_remote_copy(
            src_ref=xsend.at[(x + k) % X], dst_ref=xbuf.at[k - 1], send_sem=sx_send.at[k - 1], recv_sem=sx_recv.at[k - 1],
            device_id=device(X, Z, C, x + k, z, c), device_id_type=MESH)
        cp.start()
        xcopies.append(cp)
    result = xsend[x].astype(jnp.float32)
    for k, cp in enumerate(xcopies):
        cp.wait_recv()
        result = result + xbuf[k].astype(jnp.float32)
    out_ref[...] = result.astype(out_ref.dtype)
    for cp in plus + minus + xcopies:
        cp.wait_send()
    wait_recvs(cold2)
    wait_sends(cold1)
    wait_sends(cold2)


def hot_gather(X, Z, C, tokens, outgoing, w_gate, w_up, w_down):
    R, D = tokens.shape
    zp, zm = Z // 2, (Z - 1) // 2
    W = Z * C
    n, S, _ = outgoing.shape
    outgoing = outgoing.reshape(X, W, S, D)
    dma = pltpu.SemaphoreType.DMA
    vmem = pl.BlockSpec(memory_space=pltpu.VMEM)
    anywhere = pl.BlockSpec(memory_space=pl.ANY)
    return pl.pallas_call(
        functools.partial(gather_kernel, X, Z, C),
        out_shape=(
            jax.ShapeDtypeStruct((Z, X, R, D), tokens.dtype), jax.ShapeDtypeStruct((W, X, S, D), outgoing.dtype),
            jax.ShapeDtypeStruct(w_gate.shape, w_gate.dtype), jax.ShapeDtypeStruct(w_up.shape, w_up.dtype),
            jax.ShapeDtypeStruct(w_down.shape, w_down.dtype),
        ),
        in_specs=[vmem, vmem, anywhere, anywhere, anywhere],
        out_specs=(vmem, vmem, anywhere, anywhere, anywhere),
        scratch_shapes=[
            pltpu.VMEM((W, X, S, D), outgoing.dtype),
            dma((3,)), dma((max(X - 1, 1),)), dma((max(X - 1, 1),)), dma((W - 1,)), dma((W - 1,)), dma((3,)), dma((3,)),
            dma((max(X - 1, 1),)), dma((max(X - 1, 1),)),
            dma((max(zp, 1),)), dma((max(zp, 1),)),
            dma((max(zm, 1),)), dma((max(zm, 1),)),
        ],
        compiler_params=pltpu.CompilerParams(collective_id=0, has_side_effects=True),
    )(tokens, outgoing, w_gate, w_up, w_down)


def hot_scatter(X, Z, C, answered, cold_answered):
    _, _, R, D = answered.shape
    zp, zm = Z // 2, (Z - 1) // 2
    W, _, S, _ = cold_answered.shape
    dma = pltpu.SemaphoreType.DMA
    bf = answered.dtype
    vmem = pl.BlockSpec(memory_space=pltpu.VMEM)
    return pl.pallas_call(
        functools.partial(scatter_kernel, X, Z, C),
        out_shape=(jax.ShapeDtypeStruct((R, D), bf), jax.ShapeDtypeStruct((X, W, S, D), cold_answered.dtype)),
        in_specs=[vmem, vmem],
        out_specs=(vmem, vmem),
        scratch_shapes=[
            pltpu.VMEM((W, X, S, D), cold_answered.dtype),
            dma((2,)), dma((max(X - 1, 1),)), dma((max(X - 1, 1),)), dma((W - 1,)), dma((W - 1,)),
            pltpu.VMEM((max(zp, 1), X, R, D), bf), pltpu.VMEM((max(zp, 1), X, R, D), bf),
            pltpu.VMEM((max(zm, 1), X, R, D), bf), pltpu.VMEM((max(zm, 1), X, R, D), bf),
            pltpu.VMEM((max(X - 1, 1), R, D), bf), pltpu.VMEM((X, R, D), bf),
            dma((max(zp, 1),)), dma((max(zp, 1),)),
            dma((max(zm, 1),)), dma((max(zm, 1),)),
            dma((max(X - 1, 1),)), dma((max(X - 1, 1),)),
        ],
        compiler_params=pltpu.CompilerParams(collective_id=1, has_side_effects=True),
    )(answered, cold_answered)


def shards(X, Z, C, tokens, routes, gate_weights, w_gate, w_up, w_down):
    devices = lax.axis_size("expert")
    experts = w_gate.shape[0] * devices
    row_count = routes.shape[0]
    top_count = routes.shape[1]
    model_width = tokens.shape[1]
    slot_count = (row_count * (top_count - 1) + experts - 2) // (experts - 1)
    cold_ids = routes[:, 1:]
    flat_ids = cold_ids.reshape(-1)
    expert_iota = jnp.arange(experts, dtype=jnp.int32)
    one_hot = (flat_ids[:, None] == expert_iota[None, :]).astype(jnp.int32)
    slot_rank = (jnp.sum(jnp.cumsum(one_hot, axis=0) * one_hot, axis=1) - 1).reshape(cold_ids.shape)
    slot_iota = jnp.arange(slot_count, dtype=jnp.int32)
    select = (cold_ids[:, :, None, None] == expert_iota[None, None, :, None]) & (
        slot_rank[:, :, None, None] == slot_iota[None, None, None, :]
    )
    placing = jnp.sum(select.astype(jnp.bfloat16), axis=1)
    outgoing = jnp.einsum(
        "res,rd->esd", placing, tokens, preferred_element_type=jnp.float32
    ).astype(jnp.bfloat16)
    local_gate = w_gate.reshape(w_gate.shape[1:])
    local_up = w_up.reshape(w_up.shape[1:])
    local_down = w_down.reshape(w_down.shape[1:])
    hot_expert = routes[0, 0]
    me = lax.axis_index("expert")
    cores = C
    same_chip = me // cores == hot_expert // cores
    role = jnp.where(me == hot_expert, 0, jnp.where(same_chip, 1, 2))
    gathered, arrived, partner_gate, partner_up, partner_down = hot_gather(X, Z, C, tokens, outgoing, local_gate, local_up, local_down)
    flat_rows = arrived.reshape(-1, model_width)
    answered = feed_forward(flat_rows, local_gate, local_up, local_down).reshape(arrived.shape)

    def hot_ffn(gate_w, up_w, down_w):
        return lambda row_block: feed_forward(row_block.reshape(-1, model_width), gate_w, up_w, down_w).reshape(row_block.shape)

    hot_answer = lax.switch(
        role,
        [hot_ffn(local_gate, local_up, local_down), hot_ffn(partner_gate, partner_up, partner_down), jnp.zeros_like],
        gathered,
    )
    hot_out, returned = hot_scatter(X, Z, C, hot_answer, answered)
    returned = returned.reshape(experts, slot_count, model_width)
    picked = returned.reshape(-1, model_width)[cold_ids * slot_count + slot_rank]
    combined = gate_weights[:, 0:1] * hot_out.astype(jnp.float32) + jnp.sum(
        gate_weights[:, 1:, None] * picked.astype(jnp.float32), axis=1
    )
    return combined.astype(jnp.bfloat16)


def solution(mesh):
    X, Z, C = torus_shape(mesh)
    in_specs = (
        P(("dp", "expert"), None),
        P(("dp", "expert"), None),
        P(("dp", "expert"), None),
        P("expert", None, None),
        P("expert", None, None),
        P("expert", None, None),
    )
    out_specs = P(("dp", "expert"), None)
    return jax.shard_map(functools.partial(shards, X, Z, C), mesh=mesh, in_specs=in_specs, out_specs=out_specs, check_vma=False)
```

```python
import functools

import jax
import jax.numpy as jnp
from jax import lax
from jax.experimental import pallas as pl
from jax.experimental.pallas import tpu as pltpu
from jax.sharding import PartitionSpec as P

MESH = pl.DeviceIdType.MESH


def feed_forward(row_block, gate_w, up_w, down_w):
    gate_part = jnp.dot(row_block, gate_w, preferred_element_type=jnp.float32)
    up_part = jnp.dot(row_block, up_w, preferred_element_type=jnp.float32)
    hidden = lax.optimization_barrier((jax.nn.silu(gate_part) * up_part).astype(jnp.bfloat16))
    return jnp.dot(hidden, down_w, preferred_element_type=jnp.float32).astype(jnp.bfloat16)


def torus_shape(mesh):
    n = mesh.shape["expert"]
    try:
        row = mesh.devices.reshape(-1, n)[0]
        xs = {d.coords[0] for d in row}
        zs = {d.coords[2] for d in row}
        X, Z = len(xs), len(zs)
        C = n // (X * Z)
        if X * Z * C != n:
            raise ValueError
    except Exception:
        X, Z, C = 4, 8, 2
        if X * Z * C != n:
            X, Z, C = 1, n // 2, 2
    return X, Z, C


def coordinates(X, Z, C):
    e = lax.axis_index("expert")
    return e // (Z * C), (e // C) % Z, e % C


def wrap(v, n):
    return (v + 4 * n) % n


def device(X, Z, C, x, z, c):
    return {"expert": wrap(x, X) * (Z * C) + wrap(z, Z) * C + wrap(c, C)}


def peers(X, Z, C, x, z, c):
    out = [(x + k, z, c) for k in range(1, X)]
    if Z > 1:
        out.append((x, z + 1, c))
        if Z > 2:
            out.append((x, z - 1, c))
    if C > 1:
        out.append((x, z, c + 1))
    return out


def barrier(X, Z, C, x, z, c):
    sem = pltpu.get_barrier_semaphore()
    targets = peers(X, Z, C, x, z, c)
    for t in targets:
        pl.semaphore_signal(sem, inc=1, device_id=device(X, Z, C, *t), device_id_type=MESH)
    pl.semaphore_wait(sem, len(targets))


def barrier_all(n):
    me = lax.axis_index("expert")
    sem = pltpu.get_barrier_semaphore()

    for k in range(1, n):
        pl.semaphore_signal(sem, inc=1, device_id={"expert": (me + k) % n}, device_id_type=MESH)
    pl.semaphore_wait(sem, n - 1)


def exchange_copy(src_ref, dst_ref, k, send_sem, recv_sem):
    n = src_ref.shape[0]
    me = lax.axis_index("expert")
    target = (me + k) % n
    return pltpu.make_async_remote_copy(
        src_ref=src_ref.at[target], dst_ref=dst_ref.at[me], send_sem=send_sem.at[k - 1], recv_sem=recv_sem.at[k - 1],
        device_id={"expert": target}, device_id_type=MESH)


def exchange(src_ref, dst_ref, own_sem, send_sem, recv_sem):
    n = src_ref.shape[0]
    me = lax.axis_index("expert")
    own = pltpu.make_async_copy(src_ref.at[me], dst_ref.at[me], own_sem)
    own.start()

    for k in range(1, n):
        exchange_copy(src_ref, dst_ref, k, send_sem, recv_sem).start()
    return own


def exchange_wait(src_ref, dst_ref, own, send_sem, recv_sem):
    n = src_ref.shape[0]
    own.wait()

    for k in range(1, n):
        cp = exchange_copy(src_ref, dst_ref, k, send_sem, recv_sem)
        cp.wait_recv()
        cp.wait_send()


def plane_peers(X, Z, C, x, z, c):
    W = Z * C
    w = z * C + c
    return [{"expert": wrap(x + k, X) * W + w} for k in range(1, X)] + [
        {"expert": x * W + wrap(w + k, W)} for k in range(1, W)]


def barrier_plane(X, Z, C, x, z, c):
    sem = pltpu.get_barrier_semaphore()
    targets = plane_peers(X, Z, C, x, z, c)
    for t in targets:
        pl.semaphore_signal(sem, inc=1, device_id=t, device_id_type=MESH)
    pl.semaphore_wait(sem, len(targets))


def two_stage(X, Z, C, x, z, c):
    W = Z * C
    w = z * C + c
    return W, w


def stage_x(X, Z, C, src_of, dst_of, own_sem, send_sem, recv_sem):
    x, z, c = coordinates(X, Z, C)
    W, w = two_stage(X, Z, C, x, z, c)
    own = pltpu.make_async_copy(src_of(x), dst_of(x), own_sem)
    own.start()
    copies = []
    for k in range(1, X):
        cp = pltpu.make_async_remote_copy(
            src_ref=src_of(wrap(x + k, X)), dst_ref=dst_of(x), send_sem=send_sem.at[k - 1], recv_sem=recv_sem.at[k - 1],
            device_id={"expert": wrap(x + k, X) * W + w}, device_id_type=MESH)
        cp.start()
        copies.append(cp)
    return [own] + copies


def stage_w(X, Z, C, src_of, dst_of, own_sem, send_sem, recv_sem):
    x, z, c = coordinates(X, Z, C)
    W, w = two_stage(X, Z, C, x, z, c)
    own = pltpu.make_async_copy(src_of(w), dst_of(w), own_sem)
    own.start()
    copies = []
    for k in range(1, W):
        cp = pltpu.make_async_remote_copy(
            src_ref=src_of(wrap(w + k, W)), dst_ref=dst_of(w), send_sem=send_sem.at[k - 1], recv_sem=recv_sem.at[k - 1],
            device_id={"expert": x * W + wrap(w + k, W)}, device_id_type=MESH)
        cp.start()
        copies.append(cp)
    return [own] + copies


def wait_recvs(copies):
    copies[0].wait()
    for cp in copies[1:]:
        cp.wait_recv()


def wait_sends(copies):
    for cp in copies[1:]:
        cp.wait_send()


def gather_kernel(X, Z, C, tok_ref, cold_ref, wg_ref, wu_ref, wd_ref, out_ref, cold_out, pg_ref, pu_ref, pd_ref,
                  cold_mid, own_sem, c1_send, c1_recv, c2_send, c2_recv, w_send, w_recv, sx_send, sx_recv, sp_send, sp_recv, sm_send, sm_recv):
    x, z, c = coordinates(X, Z, C)
    zp, zm = Z // 2, (Z - 1) // 2
    dirn = 1 - 2 * (c % 2)
    barrier_plane(X, Z, C, x, z, c)
    own = pltpu.make_async_copy(tok_ref, out_ref.at[z, x], own_sem.at[0])
    own.start()
    xcopies = []
    for k in range(1, X):
        cp = pltpu.make_async_remote_copy(
            src_ref=tok_ref, dst_ref=out_ref.at[z, x], send_sem=sx_send.at[k - 1], recv_sem=sx_recv.at[k - 1],
            device_id=device(X, Z, C, x + k, z, c), device_id_type=MESH)
        cp.start()
        xcopies.append(cp)
    cold1 = stage_x(X, Z, C, lambda i: cold_ref.at[i], lambda i: cold_mid.at[:, i], own_sem.at[1], c1_send, c1_recv)
    own.wait()
    for cp in xcopies:
        cp.wait_recv()

    plus, minus = [], []
    for s in range(max(zp, zm)):
        if s < zp:
            if s >= 1:
                plus[s - 1].wait_recv()
            blk = wrap(z - s * dirn, Z)
            cp = pltpu.make_async_remote_copy(
                src_ref=out_ref.at[blk], dst_ref=out_ref.at[blk], send_sem=sp_send.at[s],
                recv_sem=sp_recv.at[s], device_id=device(X, Z, C, x, z + dirn, c), device_id_type=MESH)
            cp.start()
            plus.append(cp)
        if s < zm:
            if s >= 1:
                minus[s - 1].wait_recv()
            blk = wrap(z + s * dirn, Z)
            cp = pltpu.make_async_remote_copy(
                src_ref=out_ref.at[blk], dst_ref=out_ref.at[blk], send_sem=sm_send.at[s],
                recv_sem=sm_recv.at[s], device_id=device(X, Z, C, x, z - dirn, c), device_id_type=MESH)
            cp.start()
            minus.append(cp)
        if s == 0:
            wait_recvs(cold1)
            cold2 = stage_w(X, Z, C, lambda i: cold_mid.at[i], lambda i: cold_out.at[i], own_sem.at[2], c2_send, c2_recv)
            wcopies = []
            if C > 1:
                for j, (src, dst) in enumerate(((wg_ref, pg_ref), (wu_ref, pu_ref), (wd_ref, pd_ref))):
                    cp = pltpu.make_async_remote_copy(
                        src_ref=src, dst_ref=dst, send_sem=w_send.at[j], recv_sem=w_recv.at[j],
                        device_id=device(X, Z, C, x, z, c + 1), device_id_type=MESH)
                    cp.start()
                    wcopies.append(cp)
    if zp:
        plus[zp - 1].wait_recv()
    if zm:
        minus[zm - 1].wait_recv()
    for cp in xcopies + plus + minus:
        cp.wait_send()
    wait_recvs(cold2)
    wait_sends(cold1)
    wait_sends(cold2)
    for cp in wcopies:
        cp.wait_recv()
        cp.wait_send()


def scatter_kernel(X, Z, C, o_ref, cold_ref, out_ref, cold_out, cold_mid, own_sem, c1_send, c1_recv, c2_send, c2_recv, plus_buf, plus_send, minus_buf, minus_send, xbuf, xsend,
                   sp_send, sp_recv, sm_send, sm_recv, sx_send, sx_recv):
    x, z, c = coordinates(X, Z, C)
    zp, zm = Z // 2, (Z - 1) // 2
    dirn = 1 - 2 * (c % 2)
    barrier_plane(X, Z, C, x, z, c)

    def chip_sum(blk):
        return o_ref[blk].astype(jnp.float32)

    plus, minus = [], []
    for s in range(max(zp, zm)):
        if s < zp:
            val = chip_sum(wrap(z + (zp - s) * dirn, Z))
            if s >= 1:
                plus[s - 1].wait_recv()
                val = val + plus_buf[s - 1].astype(jnp.float32)
            plus_send[s] = val.astype(jnp.bfloat16)
            cp = pltpu.make_async_remote_copy(
                src_ref=plus_send.at[s], dst_ref=plus_buf.at[s], send_sem=sp_send.at[s], recv_sem=sp_recv.at[s],
                device_id=device(X, Z, C, x, z + dirn, c), device_id_type=MESH)
            cp.start()
            plus.append(cp)
        if s < zm:
            val = chip_sum(wrap(z - (zm - s) * dirn, Z))
            if s >= 1:
                minus[s - 1].wait_recv()
                val = val + minus_buf[s - 1].astype(jnp.float32)
            minus_send[s] = val.astype(jnp.bfloat16)
            cp = pltpu.make_async_remote_copy(
                src_ref=minus_send.at[s], dst_ref=minus_buf.at[s], send_sem=sm_send.at[s], recv_sem=sm_recv.at[s],
                device_id=device(X, Z, C, x, z - dirn, c), device_id_type=MESH)
            cp.start()
            minus.append(cp)
        if s == 0:
            cold1 = stage_w(X, Z, C, lambda i: cold_ref.at[i], lambda i: cold_mid.at[i], own_sem.at[0], c2_send, c2_recv)
    wait_recvs(cold1)
    cold2 = stage_x(X, Z, C, lambda i: cold_mid.at[:, i], lambda i: cold_out.at[i], own_sem.at[1], c1_send, c1_recv)
    total = chip_sum(z)
    if zp:
        plus[zp - 1].wait_recv()
        total = total + plus_buf[zp - 1].astype(jnp.float32)
    if zm:
        minus[zm - 1].wait_recv()
        total = total + minus_buf[zm - 1].astype(jnp.float32)
    xsend[...] = total.astype(jnp.bfloat16)
    xcopies = []
    for k in range(1, X):
        cp = pltpu.make_async_remote_copy(
            src_ref=xsend.at[(x + k) % X], dst_ref=xbuf.at[k - 1], send_sem=sx_send.at[k - 1], recv_sem=sx_recv.at[k - 1],
            device_id=device(X, Z, C, x + k, z, c), device_id_type=MESH)
        cp.start()
        xcopies.append(cp)
    result = xsend[x].astype(jnp.float32)
    for k, cp in enumerate(xcopies):
        cp.wait_recv()
        result = result + xbuf[k].astype(jnp.float32)
    out_ref[...] = result.astype(out_ref.dtype)
    for cp in plus + minus + xcopies:
        cp.wait_send()
    wait_recvs(cold2)
    wait_sends(cold1)
    wait_sends(cold2)


def hot_gather(X, Z, C, tokens, outgoing, w_gate, w_up, w_down):
    R, D = tokens.shape
    zp, zm = Z // 2, (Z - 1) // 2
    W = Z * C
    n, S, _ = outgoing.shape
    outgoing = outgoing.reshape(X, W, S, D)
    dma = pltpu.SemaphoreType.DMA
    vmem = pl.BlockSpec(memory_space=pltpu.VMEM)
    anywhere = pl.BlockSpec(memory_space=pl.ANY)
    return pl.pallas_call(
        functools.partial(gather_kernel, X, Z, C),
        out_shape=(
            jax.ShapeDtypeStruct((Z, X, R, D), tokens.dtype), jax.ShapeDtypeStruct((W, X, S, D), outgoing.dtype),
            jax.ShapeDtypeStruct(w_gate.shape, w_gate.dtype), jax.ShapeDtypeStruct(w_up.shape, w_up.dtype),
            jax.ShapeDtypeStruct(w_down.shape, w_down.dtype),
        ),
        in_specs=[vmem, vmem, anywhere, anywhere, anywhere],
        out_specs=(vmem, vmem, anywhere, anywhere, anywhere),
        scratch_shapes=[
            pltpu.VMEM((W, X, S, D), outgoing.dtype),
            dma((3,)), dma((max(X - 1, 1),)), dma((max(X - 1, 1),)), dma((W - 1,)), dma((W - 1,)), dma((3,)), dma((3,)),
            dma((max(X - 1, 1),)), dma((max(X - 1, 1),)),
            dma((max(zp, 1),)), dma((max(zp, 1),)),
            dma((max(zm, 1),)), dma((max(zm, 1),)),
        ],
        compiler_params=pltpu.CompilerParams(collective_id=0, has_side_effects=True),
    )(tokens, outgoing, w_gate, w_up, w_down)


def hot_scatter(X, Z, C, answered, cold_answered):
    _, _, R, D = answered.shape
    zp, zm = Z // 2, (Z - 1) // 2
    W, _, S, _ = cold_answered.shape
    dma = pltpu.SemaphoreType.DMA
    bf = answered.dtype
    vmem = pl.BlockSpec(memory_space=pltpu.VMEM)
    return pl.pallas_call(
        functools.partial(scatter_kernel, X, Z, C),
        out_shape=(jax.ShapeDtypeStruct((R, D), bf), jax.ShapeDtypeStruct((X, W, S, D), cold_answered.dtype)),
        in_specs=[vmem, vmem],
        out_specs=(vmem, vmem),
        scratch_shapes=[
            pltpu.VMEM((W, X, S, D), cold_answered.dtype),
            dma((2,)), dma((max(X - 1, 1),)), dma((max(X - 1, 1),)), dma((W - 1,)), dma((W - 1,)),
            pltpu.VMEM((max(zp, 1), X, R, D), bf), pltpu.VMEM((max(zp, 1), X, R, D), bf),
            pltpu.VMEM((max(zm, 1), X, R, D), bf), pltpu.VMEM((max(zm, 1), X, R, D), bf),
            pltpu.VMEM((max(X - 1, 1), R, D), bf), pltpu.VMEM((X, R, D), bf),
            dma((max(zp, 1),)), dma((max(zp, 1),)),
            dma((max(zm, 1),)), dma((max(zm, 1),)),
            dma((max(X - 1, 1),)), dma((max(X - 1, 1),)),
        ],
        compiler_params=pltpu.CompilerParams(collective_id=1, has_side_effects=True),
    )(answered, cold_answered)


def shards(X, Z, C, tokens, routes, gate_weights, w_gate, w_up, w_down):
    devices = lax.axis_size("expert")
    experts = w_gate.shape[0] * devices
    row_count = routes.shape[0]
    top_count = routes.shape[1]
    model_width = tokens.shape[1]
    slot_count = (row_count * (top_count - 1) + experts - 2) // (experts - 1)
    cold_ids = routes[:, 1:]
    flat_ids = cold_ids.reshape(-1)
    expert_iota = jnp.arange(experts, dtype=jnp.int32)
    one_hot = (flat_ids[:, None] == expert_iota[None, :]).astype(jnp.int32)
    slot_rank = (jnp.sum(jnp.cumsum(one_hot, axis=0) * one_hot, axis=1) - 1).reshape(cold_ids.shape)
    slot_iota = jnp.arange(slot_count, dtype=jnp.int32)
    select = (cold_ids[:, :, None, None] == expert_iota[None, None, :, None]) & (
        slot_rank[:, :, None, None] == slot_iota[None, None, None, :]
    )
    placing = jnp.sum(select.astype(jnp.bfloat16), axis=1)
    outgoing = jnp.einsum(
        "res,rd->esd", placing, tokens, preferred_element_type=jnp.float32
    ).astype(jnp.bfloat16)
    local_gate = w_gate.reshape(w_gate.shape[1:])
    local_up = w_up.reshape(w_up.shape[1:])
    local_down = w_down.reshape(w_down.shape[1:])
    hot_expert = routes[0, 0]
    me = lax.axis_index("expert")
    cores = C
    same_chip = lax.div(me, jnp.int32(cores)) == lax.div(hot_expert, jnp.int32(cores))
    role = jnp.where(me == hot_expert, 0, jnp.where(same_chip, 1, 2))
    gathered, arrived, partner_gate, partner_up, partner_down = hot_gather(X, Z, C, tokens, outgoing, local_gate, local_up, local_down)
    flat_rows = arrived.reshape(-1, model_width)
    answered = feed_forward(flat_rows, local_gate, local_up, local_down).reshape(arrived.shape)

    def hot_ffn(gate_w, up_w, down_w):
        return lambda row_block: feed_forward(row_block.reshape(-1, model_width), gate_w, up_w, down_w).reshape(row_block.shape)

    hot_answer = lax.switch(
        role,
        [hot_ffn(local_gate, local_up, local_down), hot_ffn(partner_gate, partner_up, partner_down), jnp.zeros_like],
        gathered,
    )
    hot_out, returned = hot_scatter(X, Z, C, hot_answer, answered)
    returned = returned.reshape(experts, slot_count, model_width)
    picked = returned.reshape(-1, model_width)[cold_ids * slot_count + slot_rank]
    combined = gate_weights[:, 0:1] * hot_out.astype(jnp.float32) + jnp.sum(
        gate_weights[:, 1:, None] * picked.astype(jnp.float32), axis=1
    )
    return combined.astype(jnp.bfloat16)


def solution(mesh):
    X, Z, C = torus_shape(mesh)
    in_specs = (
        P(("dp", "expert"), None),
        P(("dp", "expert"), None),
        P(("dp", "expert"), None),
        P("expert", None, None),
        P("expert", None, None),
        P("expert", None, None),
    )
    out_specs = P(("dp", "expert"), None)
    return jax.shard_map(functools.partial(shards, X, Z, C), mesh=mesh, in_specs=in_specs, out_specs=out_specs, check_vma=False)
```

```python
import functools

import jax
import jax.numpy as jnp
from jax import lax
from jax.experimental import pallas as pl
from jax.experimental.pallas import tpu as pltpu
from jax.sharding import PartitionSpec as P

MESH = pl.DeviceIdType.MESH


def feed_forward(row_block, gate_w, up_w, down_w):
    gate_part = jnp.dot(row_block, gate_w, preferred_element_type=jnp.float32)
    up_part = jnp.dot(row_block, up_w, preferred_element_type=jnp.float32)
    hidden = lax.optimization_barrier((jax.nn.silu(gate_part) * up_part).astype(jnp.bfloat16))
    return jnp.dot(hidden, down_w, preferred_element_type=jnp.float32).astype(jnp.bfloat16)


def torus_shape(mesh):
    n = mesh.shape["expert"]
    try:
        row = mesh.devices.reshape(-1, n)[0]
        xs = {d.coords[0] for d in row}
        zs = {d.coords[2] for d in row}
        X, Z = len(xs), len(zs)
        C = n // (X * Z)
        if X * Z * C != n:
            raise ValueError
    except Exception:
        X, Z, C = 4, 8, 2
        if X * Z * C != n:
            X, Z, C = 1, n // 2, 2
    return X, Z, C


def coordinates(X, Z, C):
    e = lax.axis_index("expert")
    return e // (Z * C), (e // C) % Z, e % C


def wrap(v, n):
    return (v + 4 * n) % n


def device(X, Z, C, x, z, c):
    return {"expert": wrap(x, X) * (Z * C) + wrap(z, Z) * C + wrap(c, C)}


def peers(X, Z, C, x, z, c):
    out = [(x + k, z, c) for k in range(1, X)]
    if Z > 1:
        out.append((x, z + 1, c))
        if Z > 2:
            out.append((x, z - 1, c))
    if C > 1:
        out.append((x, z, c + 1))
    return out


def barrier(X, Z, C, x, z, c):
    sem = pltpu.get_barrier_semaphore()
    targets = peers(X, Z, C, x, z, c)
    for t in targets:
        pl.semaphore_signal(sem, inc=1, device_id=device(X, Z, C, *t), device_id_type=MESH)
    pl.semaphore_wait(sem, len(targets))


def barrier_all(n):
    me = lax.axis_index("expert")
    sem = pltpu.get_barrier_semaphore()

    for k in range(1, n):
        pl.semaphore_signal(sem, inc=1, device_id={"expert": (me + k) % n}, device_id_type=MESH)
    pl.semaphore_wait(sem, n - 1)


def exchange_copy(src_ref, dst_ref, k, send_sem, recv_sem):
    n = src_ref.shape[0]
    me = lax.axis_index("expert")
    target = (me + k) % n
    return pltpu.make_async_remote_copy(
        src_ref=src_ref.at[target], dst_ref=dst_ref.at[me], send_sem=send_sem.at[k - 1], recv_sem=recv_sem.at[k - 1],
        device_id={"expert": target}, device_id_type=MESH)


def exchange(src_ref, dst_ref, own_sem, send_sem, recv_sem):
    n = src_ref.shape[0]
    me = lax.axis_index("expert")
    own = pltpu.make_async_copy(src_ref.at[me], dst_ref.at[me], own_sem)
    own.start()

    for k in range(1, n):
        exchange_copy(src_ref, dst_ref, k, send_sem, recv_sem).start()
    return own


def exchange_wait(src_ref, dst_ref, own, send_sem, recv_sem):
    n = src_ref.shape[0]
    own.wait()

    for k in range(1, n):
        cp = exchange_copy(src_ref, dst_ref, k, send_sem, recv_sem)
        cp.wait_recv()
        cp.wait_send()


def plane_peers(X, Z, C, x, z, c):
    W = Z * C
    w = z * C + c
    return [{"expert": wrap(x + k, X) * W + w} for k in range(1, X)] + [
        {"expert": x * W + wrap(w + k, W)} for k in range(1, W)]


def barrier_plane(X, Z, C, x, z, c):
    sem = pltpu.get_barrier_semaphore()
    targets = plane_peers(X, Z, C, x, z, c)
    for t in targets:
        pl.semaphore_signal(sem, inc=1, device_id=t, device_id_type=MESH)
    pl.semaphore_wait(sem, len(targets))


def two_stage(X, Z, C, x, z, c):
    W = Z * C
    w = z * C + c
    return W, w


def stage_x(X, Z, C, src_of, dst_of, own_sem, send_sem, recv_sem):
    x, z, c = coordinates(X, Z, C)
    W, w = two_stage(X, Z, C, x, z, c)
    own = pltpu.make_async_copy(src_of(x), dst_of(x), own_sem)
    own.start()
    copies = []
    for k in range(1, X):
        cp = pltpu.make_async_remote_copy(
            src_ref=src_of(wrap(x + k, X)), dst_ref=dst_of(x), send_sem=send_sem.at[k - 1], recv_sem=recv_sem.at[k - 1],
            device_id={"expert": wrap(x + k, X) * W + w}, device_id_type=MESH)
        cp.start()
        copies.append(cp)
    return [own] + copies


def stage_w(X, Z, C, src_of, dst_of, own_sem, send_sem, recv_sem):
    x, z, c = coordinates(X, Z, C)
    W, w = two_stage(X, Z, C, x, z, c)
    own = pltpu.make_async_copy(src_of(w), dst_of(w), own_sem)
    own.start()
    copies = []
    for k in range(1, W):
        cp = pltpu.make_async_remote_copy(
            src_ref=src_of(wrap(w + k, W)), dst_ref=dst_of(w), send_sem=send_sem.at[k - 1], recv_sem=recv_sem.at[k - 1],
            device_id={"expert": x * W + wrap(w + k, W)}, device_id_type=MESH)
        cp.start()
        copies.append(cp)
    return [own] + copies


def wait_recvs(copies):
    copies[0].wait()
    for cp in copies[1:]:
        cp.wait_recv()


def wait_sends(copies):
    for cp in copies[1:]:
        cp.wait_send()


def gather_kernel(X, Z, C, tok_ref, cold_ref, wg_ref, wu_ref, wd_ref, out_ref, cold_out, pg_ref, pu_ref, pd_ref,
                  cold_mid, own_sem, c1_send, c1_recv, c2_send, c2_recv, w_send, w_recv, sx_send, sx_recv, sp_send, sp_recv, sm_send, sm_recv):
    x, z, c = coordinates(X, Z, C)
    zp, zm = Z // 2, (Z - 1) // 2
    dirn = 1 - 2 * (c % 2)
    barrier_plane(X, Z, C, x, z, c)
    own = pltpu.make_async_copy(tok_ref, out_ref.at[z, x], own_sem.at[0])
    own.start()
    xcopies = []
    for k in range(1, X):
        cp = pltpu.make_async_remote_copy(
            src_ref=tok_ref, dst_ref=out_ref.at[z, x], send_sem=sx_send.at[k - 1], recv_sem=sx_recv.at[k - 1],
            device_id=device(X, Z, C, x + k, z, c), device_id_type=MESH)
        cp.start()
        xcopies.append(cp)
    cold1 = stage_x(X, Z, C, lambda i: cold_ref.at[i], lambda i: cold_mid.at[:, i], own_sem.at[1], c1_send, c1_recv)
    own.wait()
    for cp in xcopies:
        cp.wait_recv()

    plus, minus = [], []
    for s in range(max(zp, zm)):
        if s < zp:
            if s >= 1:
                plus[s - 1].wait_recv()
            blk = wrap(z - s * dirn, Z)
            cp = pltpu.make_async_remote_copy(
                src_ref=out_ref.at[blk], dst_ref=out_ref.at[blk], send_sem=sp_send.at[s],
                recv_sem=sp_recv.at[s], device_id=device(X, Z, C, x, z + dirn, c), device_id_type=MESH)
            cp.start()
            plus.append(cp)
        if s < zm:
            if s >= 1:
                minus[s - 1].wait_recv()
            blk = wrap(z + s * dirn, Z)
            cp = pltpu.make_async_remote_copy(
                src_ref=out_ref.at[blk], dst_ref=out_ref.at[blk], send_sem=sm_send.at[s],
                recv_sem=sm_recv.at[s], device_id=device(X, Z, C, x, z - dirn, c), device_id_type=MESH)
            cp.start()
            minus.append(cp)
        if s == 0:
            wait_recvs(cold1)
            cold2 = stage_w(X, Z, C, lambda i: cold_mid.at[i], lambda i: cold_out.at[i], own_sem.at[2], c2_send, c2_recv)
            wcopies = []
            if C > 1:
                for j, (src, dst) in enumerate(((wg_ref, pg_ref), (wu_ref, pu_ref), (wd_ref, pd_ref))):
                    cp = pltpu.make_async_remote_copy(
                        src_ref=src, dst_ref=dst, send_sem=w_send.at[j], recv_sem=w_recv.at[j],
                        device_id=device(X, Z, C, x, z, c + 1), device_id_type=MESH)
                    cp.start()
                    wcopies.append(cp)
    if zp:
        plus[zp - 1].wait_recv()
    if zm:
        minus[zm - 1].wait_recv()
    for cp in xcopies + plus + minus:
        cp.wait_send()
    wait_recvs(cold2)
    wait_sends(cold1)
    wait_sends(cold2)
    for cp in wcopies:
        cp.wait_recv()
        cp.wait_send()


def scatter_kernel(X, Z, C, o_ref, cold_ref, out_ref, cold_out, cold_mid, own_sem, c1_send, c1_recv, c2_send, c2_recv, plus_buf, plus_send, minus_buf, minus_send, xbuf, xsend,
                   sp_send, sp_recv, sm_send, sm_recv, sx_send, sx_recv):
    x, z, c = coordinates(X, Z, C)
    zp, zm = Z // 2, (Z - 1) // 2
    dirn = 1 - 2 * (c % 2)
    barrier_plane(X, Z, C, x, z, c)

    def chip_sum(blk):
        return o_ref[blk].astype(jnp.float32)

    plus, minus = [], []
    for s in range(max(zp, zm)):
        if s < zp:
            val = chip_sum(wrap(z + (zp - s) * dirn, Z))
            if s >= 1:
                plus[s - 1].wait_recv()
                val = val + plus_buf[s - 1].astype(jnp.float32)
            plus_send[s] = val.astype(jnp.bfloat16)
            cp = pltpu.make_async_remote_copy(
                src_ref=plus_send.at[s], dst_ref=plus_buf.at[s], send_sem=sp_send.at[s], recv_sem=sp_recv.at[s],
                device_id=device(X, Z, C, x, z + dirn, c), device_id_type=MESH)
            cp.start()
            plus.append(cp)
        if s < zm:
            val = chip_sum(wrap(z - (zm - s) * dirn, Z))
            if s >= 1:
                minus[s - 1].wait_recv()
                val = val + minus_buf[s - 1].astype(jnp.float32)
            minus_send[s] = val.astype(jnp.bfloat16)
            cp = pltpu.make_async_remote_copy(
                src_ref=minus_send.at[s], dst_ref=minus_buf.at[s], send_sem=sm_send.at[s], recv_sem=sm_recv.at[s],
                device_id=device(X, Z, C, x, z - dirn, c), device_id_type=MESH)
            cp.start()
            minus.append(cp)
        if s == 0:
            cold1 = stage_w(X, Z, C, lambda i: cold_ref.at[i], lambda i: cold_mid.at[i], own_sem.at[0], c2_send, c2_recv)
    wait_recvs(cold1)
    cold2 = stage_x(X, Z, C, lambda i: cold_mid.at[:, i], lambda i: cold_out.at[i], own_sem.at[1], c1_send, c1_recv)
    total = chip_sum(z)
    if zp:
        plus[zp - 1].wait_recv()
        total = total + plus_buf[zp - 1].astype(jnp.float32)
    if zm:
        minus[zm - 1].wait_recv()
        total = total + minus_buf[zm - 1].astype(jnp.float32)
    xsend[...] = total.astype(jnp.bfloat16)
    xcopies = []
    for k in range(1, X):
        cp = pltpu.make_async_remote_copy(
            src_ref=xsend.at[(x + k) % X], dst_ref=xbuf.at[k - 1], send_sem=sx_send.at[k - 1], recv_sem=sx_recv.at[k - 1],
            device_id=device(X, Z, C, x + k, z, c), device_id_type=MESH)
        cp.start()
        xcopies.append(cp)
    result = xsend[x].astype(jnp.float32)
    for k, cp in enumerate(xcopies):
        cp.wait_recv()
        result = result + xbuf[k].astype(jnp.float32)
    out_ref[...] = result.astype(out_ref.dtype)
    for cp in plus + minus + xcopies:
        cp.wait_send()
    wait_recvs(cold2)
    wait_sends(cold1)
    wait_sends(cold2)


def hot_gather(X, Z, C, tokens, outgoing, w_gate, w_up, w_down):
    R, D = tokens.shape
    zp, zm = Z // 2, (Z - 1) // 2
    W = Z * C
    n, S, _ = outgoing.shape
    outgoing = outgoing.reshape(X, W, S, D)
    dma = pltpu.SemaphoreType.DMA
    vmem = pl.BlockSpec(memory_space=pltpu.VMEM)
    anywhere = pl.BlockSpec(memory_space=pl.ANY)
    return pl.pallas_call(
        functools.partial(gather_kernel, X, Z, C),
        out_shape=(
            jax.ShapeDtypeStruct((Z, X, R, D), tokens.dtype), jax.ShapeDtypeStruct((W, X, S, D), outgoing.dtype),
            jax.ShapeDtypeStruct(w_gate.shape, w_gate.dtype), jax.ShapeDtypeStruct(w_up.shape, w_up.dtype),
            jax.ShapeDtypeStruct(w_down.shape, w_down.dtype),
        ),
        in_specs=[vmem, vmem, anywhere, anywhere, anywhere],
        out_specs=(vmem, vmem, anywhere, anywhere, anywhere),
        scratch_shapes=[
            pltpu.VMEM((W, X, S, D), outgoing.dtype),
            dma((3,)), dma((max(X - 1, 1),)), dma((max(X - 1, 1),)), dma((W - 1,)), dma((W - 1,)), dma((3,)), dma((3,)),
            dma((max(X - 1, 1),)), dma((max(X - 1, 1),)),
            dma((max(zp, 1),)), dma((max(zp, 1),)),
            dma((max(zm, 1),)), dma((max(zm, 1),)),
        ],
        compiler_params=pltpu.CompilerParams(collective_id=0, has_side_effects=True),
    )(tokens, outgoing, w_gate, w_up, w_down)


def hot_scatter(X, Z, C, answered, cold_answered):
    _, _, R, D = answered.shape
    zp, zm = Z // 2, (Z - 1) // 2
    W, _, S, _ = cold_answered.shape
    dma = pltpu.SemaphoreType.DMA
    bf = answered.dtype
    vmem = pl.BlockSpec(memory_space=pltpu.VMEM)
    return pl.pallas_call(
        functools.partial(scatter_kernel, X, Z, C),
        out_shape=(jax.ShapeDtypeStruct((R, D), bf), jax.ShapeDtypeStruct((X, W, S, D), cold_answered.dtype)),
        in_specs=[vmem, vmem],
        out_specs=(vmem, vmem),
        scratch_shapes=[
            pltpu.VMEM((W, X, S, D), cold_answered.dtype),
            dma((2,)), dma((max(X - 1, 1),)), dma((max(X - 1, 1),)), dma((W - 1,)), dma((W - 1,)),
            pltpu.VMEM((max(zp, 1), X, R, D), bf), pltpu.VMEM((max(zp, 1), X, R, D), bf),
            pltpu.VMEM((max(zm, 1), X, R, D), bf), pltpu.VMEM((max(zm, 1), X, R, D), bf),
            pltpu.VMEM((max(X - 1, 1), R, D), bf), pltpu.VMEM((X, R, D), bf),
            dma((max(zp, 1),)), dma((max(zp, 1),)),
            dma((max(zm, 1),)), dma((max(zm, 1),)),
            dma((max(X - 1, 1),)), dma((max(X - 1, 1),)),
        ],
        compiler_params=pltpu.CompilerParams(collective_id=1, has_side_effects=True),
    )(answered, cold_answered)


def shards(X, Z, C, tokens, routes, gate_weights, w_gate, w_up, w_down):
    devices = lax.axis_size("expert")
    experts = w_gate.shape[0] * devices
    row_count = routes.shape[0]
    top_count = routes.shape[1]
    model_width = tokens.shape[1]
    slot_count = (row_count * (top_count - 1) + experts - 2) // (experts - 1)
    is_cold = jnp.arange(top_count)[None, :] >= 1
    flat_ids = routes.reshape(-1)
    flat_cold = jnp.broadcast_to(is_cold, routes.shape).reshape(-1)
    expert_iota = jnp.arange(experts, dtype=jnp.int32)
    one_hot = ((flat_ids[:, None] == expert_iota[None, :]) & flat_cold[:, None]).astype(jnp.int32)
    slot_rank = (jnp.sum(jnp.cumsum(one_hot, axis=0) * one_hot, axis=1) - 1).reshape(routes.shape)
    slot_iota = jnp.arange(slot_count, dtype=jnp.int32)
    select = (routes[:, :, None, None] == expert_iota[None, None, :, None]) & (
        slot_rank[:, :, None, None] == slot_iota[None, None, None, :]
    ) & is_cold[:, :, None, None]
    placing = jnp.sum(select.astype(jnp.bfloat16), axis=1)
    outgoing = jnp.einsum(
        "res,rd->esd", placing, tokens, preferred_element_type=jnp.float32
    ).astype(jnp.bfloat16)
    local_gate = w_gate.reshape(w_gate.shape[1:])
    local_up = w_up.reshape(w_up.shape[1:])
    local_down = w_down.reshape(w_down.shape[1:])
    hot_expert = routes[0, 0]
    me = lax.axis_index("expert")
    cores = C
    same_chip = lax.div(me, jnp.int32(cores)) == lax.div(hot_expert, jnp.int32(cores))
    role = jnp.where(me == hot_expert, 0, jnp.where(same_chip, 1, 2))
    gathered, arrived, partner_gate, partner_up, partner_down = hot_gather(X, Z, C, tokens, outgoing, local_gate, local_up, local_down)
    flat_rows = arrived.reshape(-1, model_width)
    answered = feed_forward(flat_rows, local_gate, local_up, local_down).reshape(arrived.shape)

    def hot_ffn(gate_w, up_w, down_w):
        return lambda row_block: feed_forward(row_block.reshape(-1, model_width), gate_w, up_w, down_w).reshape(row_block.shape)

    hot_answer = lax.switch(
        role,
        [hot_ffn(local_gate, local_up, local_down), hot_ffn(partner_gate, partner_up, partner_down), jnp.zeros_like],
        gathered,
    )
    hot_out, returned = hot_scatter(X, Z, C, hot_answer, answered)
    returned = returned.reshape(experts, slot_count, model_width)
    index = jnp.where(is_cold, routes * slot_count + slot_rank, 0)
    picked = returned.reshape(-1, model_width)[index].astype(jnp.float32)
    values = jnp.where(is_cold[:, :, None], picked, hot_out.astype(jnp.float32)[:, None, :])
    combined = jnp.sum(gate_weights[:, :, None] * values, axis=1)
    return combined.astype(jnp.bfloat16)


def solution(mesh):
    X, Z, C = torus_shape(mesh)
    in_specs = (
        P(("dp", "expert"), None),
        P(("dp", "expert"), None),
        P(("dp", "expert"), None),
        P("expert", None, None),
        P("expert", None, None),
        P("expert", None, None),
    )
    out_specs = P(("dp", "expert"), None)
    return jax.shard_map(functools.partial(shards, X, Z, C), mesh=mesh, in_specs=in_specs, out_specs=out_specs, check_vma=False)
```

```python
import functools

import jax
import jax.numpy as jnp
from jax import lax
from jax.experimental import pallas as pl
from jax.experimental.pallas import tpu as pltpu
from jax.sharding import PartitionSpec as P

MESH = pl.DeviceIdType.MESH


def feed_forward(row_block, gate_w, up_w, down_w):
    gate_part = jnp.dot(row_block, gate_w, preferred_element_type=jnp.float32)
    up_part = jnp.dot(row_block, up_w, preferred_element_type=jnp.float32)
    hidden = lax.optimization_barrier((jax.nn.silu(gate_part) * up_part).astype(jnp.bfloat16))
    return jnp.dot(hidden, down_w, preferred_element_type=jnp.float32).astype(jnp.bfloat16)


def torus_shape(mesh):
    n = mesh.shape["expert"]
    try:
        row = mesh.devices.reshape(-1, n)[0]
        xs = {d.coords[0] for d in row}
        zs = {d.coords[2] for d in row}
        X, Z = len(xs), len(zs)
        C = n // (X * Z)
        if X * Z * C != n:
            raise ValueError
    except Exception:
        X, Z, C = 4, 8, 2
        if X * Z * C != n:
            X, Z, C = 1, n // 2, 2
    return X, Z, C


def coordinates(X, Z, C):
    e = lax.axis_index("expert")
    return e // (Z * C), (e // C) % Z, e % C


def wrap(v, n):
    return (v + 4 * n) % n


def device(X, Z, C, x, z, c):
    return {"expert": wrap(x, X) * (Z * C) + wrap(z, Z) * C + wrap(c, C)}


def peers(X, Z, C, x, z, c):
    out = [(x + k, z, c) for k in range(1, X)]
    if Z > 1:
        out.append((x, z + 1, c))
        if Z > 2:
            out.append((x, z - 1, c))
    if C > 1:
        out.append((x, z, c + 1))
    return out


def barrier(X, Z, C, x, z, c):
    sem = pltpu.get_barrier_semaphore()
    targets = peers(X, Z, C, x, z, c)
    for t in targets:
        pl.semaphore_signal(sem, inc=1, device_id=device(X, Z, C, *t), device_id_type=MESH)
    pl.semaphore_wait(sem, len(targets))


def barrier_all(n):
    me = lax.axis_index("expert")
    sem = pltpu.get_barrier_semaphore()

    for k in range(1, n):
        pl.semaphore_signal(sem, inc=1, device_id={"expert": (me + k) % n}, device_id_type=MESH)
    pl.semaphore_wait(sem, n - 1)


def exchange_copy(src_ref, dst_ref, k, send_sem, recv_sem):
    n = src_ref.shape[0]
    me = lax.axis_index("expert")
    target = (me + k) % n
    return pltpu.make_async_remote_copy(
        src_ref=src_ref.at[target], dst_ref=dst_ref.at[me], send_sem=send_sem.at[k - 1], recv_sem=recv_sem.at[k - 1],
        device_id={"expert": target}, device_id_type=MESH)


def exchange(src_ref, dst_ref, own_sem, send_sem, recv_sem):
    n = src_ref.shape[0]
    me = lax.axis_index("expert")
    own = pltpu.make_async_copy(src_ref.at[me], dst_ref.at[me], own_sem)
    own.start()

    for k in range(1, n):
        exchange_copy(src_ref, dst_ref, k, send_sem, recv_sem).start()
    return own


def exchange_wait(src_ref, dst_ref, own, send_sem, recv_sem):
    n = src_ref.shape[0]
    own.wait()

    for k in range(1, n):
        cp = exchange_copy(src_ref, dst_ref, k, send_sem, recv_sem)
        cp.wait_recv()
        cp.wait_send()


def plane_peers(X, Z, C, x, z, c):
    W = Z * C
    w = z * C + c
    return [{"expert": wrap(x + k, X) * W + w} for k in range(1, X)] + [
        {"expert": x * W + wrap(w + k, W)} for k in range(1, W)]


def barrier_plane(X, Z, C, x, z, c):
    sem = pltpu.get_barrier_semaphore()
    targets = plane_peers(X, Z, C, x, z, c)
    for t in targets:
        pl.semaphore_signal(sem, inc=1, device_id=t, device_id_type=MESH)
    pl.semaphore_wait(sem, len(targets))


def two_stage(X, Z, C, x, z, c):
    W = Z * C
    w = z * C + c
    return W, w


def stage_x(X, Z, C, src_of, dst_of, own_sem, send_sem, recv_sem):
    x, z, c = coordinates(X, Z, C)
    W, w = two_stage(X, Z, C, x, z, c)
    own = pltpu.make_async_copy(src_of(x), dst_of(x), own_sem)
    own.start()
    copies = []
    for k in range(1, X):
        cp = pltpu.make_async_remote_copy(
            src_ref=src_of(wrap(x + k, X)), dst_ref=dst_of(x), send_sem=send_sem.at[k - 1], recv_sem=recv_sem.at[k - 1],
            device_id={"expert": wrap(x + k, X) * W + w}, device_id_type=MESH)
        cp.start()
        copies.append(cp)
    return [own] + copies


def stage_w(X, Z, C, src_of, dst_of, own_sem, send_sem, recv_sem):
    x, z, c = coordinates(X, Z, C)
    W, w = two_stage(X, Z, C, x, z, c)
    own = pltpu.make_async_copy(src_of(w), dst_of(w), own_sem)
    own.start()
    copies = []
    for k in range(1, W):
        cp = pltpu.make_async_remote_copy(
            src_ref=src_of(wrap(w + k, W)), dst_ref=dst_of(w), send_sem=send_sem.at[k - 1], recv_sem=recv_sem.at[k - 1],
            device_id={"expert": x * W + wrap(w + k, W)}, device_id_type=MESH)
        cp.start()
        copies.append(cp)
    return [own] + copies


def wait_recvs(copies):
    copies[0].wait()
    for cp in copies[1:]:
        cp.wait_recv()


def wait_sends(copies):
    for cp in copies[1:]:
        cp.wait_send()


def gather_kernel(X, Z, C, tok_ref, cold_ref, wg_ref, wu_ref, wd_ref, out_ref, cold_out, pg_ref, pu_ref, pd_ref,
                  cold_mid, own_sem, c1_send, c1_recv, c2_send, c2_recv, w_send, w_recv, sx_send, sx_recv, sp_send, sp_recv, sm_send, sm_recv):
    x, z, c = coordinates(X, Z, C)
    zp, zm = Z // 2, (Z - 1) // 2
    dirn = 1 - 2 * (c % 2)
    barrier_plane(X, Z, C, x, z, c)
    own = pltpu.make_async_copy(tok_ref, out_ref.at[z, x], own_sem.at[0])
    own.start()
    xcopies = []
    for k in range(1, X):
        cp = pltpu.make_async_remote_copy(
            src_ref=tok_ref, dst_ref=out_ref.at[z, x], send_sem=sx_send.at[k - 1], recv_sem=sx_recv.at[k - 1],
            device_id=device(X, Z, C, x + k, z, c), device_id_type=MESH)
        cp.start()
        xcopies.append(cp)
    cold1 = stage_x(X, Z, C, lambda i: cold_ref.at[i], lambda i: cold_mid.at[:, i], own_sem.at[1], c1_send, c1_recv)
    own.wait()
    for cp in xcopies:
        cp.wait_recv()

    plus, minus = [], []
    for s in range(max(zp, zm)):
        if s < zp:
            if s >= 1:
                plus[s - 1].wait_recv()
            blk = wrap(z - s * dirn, Z)
            cp = pltpu.make_async_remote_copy(
                src_ref=out_ref.at[blk], dst_ref=out_ref.at[blk], send_sem=sp_send.at[s],
                recv_sem=sp_recv.at[s], device_id=device(X, Z, C, x, z + dirn, c), device_id_type=MESH)
            cp.start()
            plus.append(cp)
        if s < zm:
            if s >= 1:
                minus[s - 1].wait_recv()
            blk = wrap(z + s * dirn, Z)
            cp = pltpu.make_async_remote_copy(
                src_ref=out_ref.at[blk], dst_ref=out_ref.at[blk], send_sem=sm_send.at[s],
                recv_sem=sm_recv.at[s], device_id=device(X, Z, C, x, z - dirn, c), device_id_type=MESH)
            cp.start()
            minus.append(cp)
        if s == 0:
            wait_recvs(cold1)
            cold2 = stage_w(X, Z, C, lambda i: cold_mid.at[i], lambda i: cold_out.at[i], own_sem.at[2], c2_send, c2_recv)
            wcopies = []
            if C > 1:
                for j, (src, dst) in enumerate(((wg_ref, pg_ref), (wu_ref, pu_ref), (wd_ref, pd_ref))):
                    cp = pltpu.make_async_remote_copy(
                        src_ref=src, dst_ref=dst, send_sem=w_send.at[j], recv_sem=w_recv.at[j],
                        device_id=device(X, Z, C, x, z, c + 1), device_id_type=MESH)
                    cp.start()
                    wcopies.append(cp)
    if zp:
        plus[zp - 1].wait_recv()
    if zm:
        minus[zm - 1].wait_recv()
    for cp in xcopies + plus + minus:
        cp.wait_send()
    wait_recvs(cold2)
    wait_sends(cold1)
    wait_sends(cold2)
    for cp in wcopies:
        cp.wait_recv()
        cp.wait_send()


def scatter_kernel(X, Z, C, o_ref, cold_ref, out_ref, cold_out, cold_mid, own_sem, c1_send, c1_recv, c2_send, c2_recv, plus_buf, plus_send, minus_buf, minus_send, xbuf, xsend,
                   sp_send, sp_recv, sm_send, sm_recv, sx_send, sx_recv):
    x, z, c = coordinates(X, Z, C)
    zp, zm = Z // 2, (Z - 1) // 2
    dirn = 1 - 2 * (c % 2)
    barrier_plane(X, Z, C, x, z, c)

    def chip_sum(blk):
        return o_ref[blk].astype(jnp.float32)

    plus, minus = [], []
    for s in range(max(zp, zm)):
        if s < zp:
            val = chip_sum(wrap(z + (zp - s) * dirn, Z))
            if s >= 1:
                plus[s - 1].wait_recv()
                val = val + plus_buf[s - 1].astype(jnp.float32)
            plus_send[s] = val.astype(jnp.bfloat16)
            cp = pltpu.make_async_remote_copy(
                src_ref=plus_send.at[s], dst_ref=plus_buf.at[s], send_sem=sp_send.at[s], recv_sem=sp_recv.at[s],
                device_id=device(X, Z, C, x, z + dirn, c), device_id_type=MESH)
            cp.start()
            plus.append(cp)
        if s < zm:
            val = chip_sum(wrap(z - (zm - s) * dirn, Z))
            if s >= 1:
                minus[s - 1].wait_recv()
                val = val + minus_buf[s - 1].astype(jnp.float32)
            minus_send[s] = val.astype(jnp.bfloat16)
            cp = pltpu.make_async_remote_copy(
                src_ref=minus_send.at[s], dst_ref=minus_buf.at[s], send_sem=sm_send.at[s], recv_sem=sm_recv.at[s],
                device_id=device(X, Z, C, x, z - dirn, c), device_id_type=MESH)
            cp.start()
            minus.append(cp)
        if s == 0:
            cold1 = stage_w(X, Z, C, lambda i: cold_ref.at[i], lambda i: cold_mid.at[i], own_sem.at[0], c2_send, c2_recv)
    wait_recvs(cold1)
    cold2 = stage_x(X, Z, C, lambda i: cold_mid.at[:, i], lambda i: cold_out.at[i], own_sem.at[1], c1_send, c1_recv)
    total = chip_sum(z)
    if zp:
        plus[zp - 1].wait_recv()
        total = total + plus_buf[zp - 1].astype(jnp.float32)
    if zm:
        minus[zm - 1].wait_recv()
        total = total + minus_buf[zm - 1].astype(jnp.float32)
    xsend[...] = total.astype(jnp.bfloat16)
    xcopies = []
    for k in range(1, X):
        cp = pltpu.make_async_remote_copy(
            src_ref=xsend.at[(x + k) % X], dst_ref=xbuf.at[k - 1], send_sem=sx_send.at[k - 1], recv_sem=sx_recv.at[k - 1],
            device_id=device(X, Z, C, x + k, z, c), device_id_type=MESH)
        cp.start()
        xcopies.append(cp)
    result = xsend[x].astype(jnp.float32)
    for k, cp in enumerate(xcopies):
        cp.wait_recv()
        result = result + xbuf[k].astype(jnp.float32)
    out_ref[...] = result.astype(out_ref.dtype)
    for cp in plus + minus + xcopies:
        cp.wait_send()
    wait_recvs(cold2)
    wait_sends(cold1)
    wait_sends(cold2)


def hot_gather(X, Z, C, tokens, outgoing, w_gate, w_up, w_down):
    R, D = tokens.shape
    zp, zm = Z // 2, (Z - 1) // 2
    W = Z * C
    n, S, _ = outgoing.shape
    outgoing = outgoing.reshape(X, W, S, D)
    dma = pltpu.SemaphoreType.DMA
    vmem = pl.BlockSpec(memory_space=pltpu.VMEM)
    anywhere = pl.BlockSpec(memory_space=pl.ANY)
    return pl.pallas_call(
        functools.partial(gather_kernel, X, Z, C),
        out_shape=(
            jax.ShapeDtypeStruct((Z, X, R, D), tokens.dtype), jax.ShapeDtypeStruct((W, X, S, D), outgoing.dtype),
            jax.ShapeDtypeStruct(w_gate.shape, w_gate.dtype), jax.ShapeDtypeStruct(w_up.shape, w_up.dtype),
            jax.ShapeDtypeStruct(w_down.shape, w_down.dtype),
        ),
        in_specs=[vmem, vmem, anywhere, anywhere, anywhere],
        out_specs=(vmem, vmem, anywhere, anywhere, anywhere),
        scratch_shapes=[
            pltpu.VMEM((W, X, S, D), outgoing.dtype),
            dma((3,)), dma((max(X - 1, 1),)), dma((max(X - 1, 1),)), dma((W - 1,)), dma((W - 1,)), dma((3,)), dma((3,)),
            dma((max(X - 1, 1),)), dma((max(X - 1, 1),)),
            dma((max(zp, 1),)), dma((max(zp, 1),)),
            dma((max(zm, 1),)), dma((max(zm, 1),)),
        ],
        compiler_params=pltpu.CompilerParams(collective_id=0, has_side_effects=True),
    )(tokens, outgoing, w_gate, w_up, w_down)


def hot_scatter(X, Z, C, answered, cold_answered):
    _, _, R, D = answered.shape
    zp, zm = Z // 2, (Z - 1) // 2
    W, _, S, _ = cold_answered.shape
    dma = pltpu.SemaphoreType.DMA
    bf = answered.dtype
    vmem = pl.BlockSpec(memory_space=pltpu.VMEM)
    return pl.pallas_call(
        functools.partial(scatter_kernel, X, Z, C),
        out_shape=(jax.ShapeDtypeStruct((R, D), bf), jax.ShapeDtypeStruct((X, W, S, D), cold_answered.dtype)),
        in_specs=[vmem, vmem],
        out_specs=(vmem, vmem),
        scratch_shapes=[
            pltpu.VMEM((W, X, S, D), cold_answered.dtype),
            dma((2,)), dma((max(X - 1, 1),)), dma((max(X - 1, 1),)), dma((W - 1,)), dma((W - 1,)),
            pltpu.VMEM((max(zp, 1), X, R, D), bf), pltpu.VMEM((max(zp, 1), X, R, D), bf),
            pltpu.VMEM((max(zm, 1), X, R, D), bf), pltpu.VMEM((max(zm, 1), X, R, D), bf),
            pltpu.VMEM((max(X - 1, 1), R, D), bf), pltpu.VMEM((X, R, D), bf),
            dma((max(zp, 1),)), dma((max(zp, 1),)),
            dma((max(zm, 1),)), dma((max(zm, 1),)),
            dma((max(X - 1, 1),)), dma((max(X - 1, 1),)),
        ],
        compiler_params=pltpu.CompilerParams(collective_id=1, has_side_effects=True),
    )(answered, cold_answered)


def shards(X, Z, C, tokens, routes, gate_weights, w_gate, w_up, w_down):
    devices = lax.axis_size("expert")
    experts = w_gate.shape[0] * devices
    row_count = routes.shape[0]
    top_count = routes.shape[1]
    model_width = tokens.shape[1]
    slot_count = (row_count * (top_count - 1) + experts - 2) // (experts - 1)
    is_cold = jnp.arange(top_count)[None, :] >= 1
    flat_ids = routes.reshape(-1)
    flat_cold = jnp.broadcast_to(is_cold, routes.shape).reshape(-1)
    expert_iota = jnp.arange(experts, dtype=jnp.int32)
    one_hot = ((flat_ids[:, None] == expert_iota[None, :]) & flat_cold[:, None]).astype(jnp.int32)
    slot_rank = (jnp.sum(jnp.cumsum(one_hot, axis=0) * one_hot, axis=1) - 1).reshape(routes.shape)
    slot_iota = jnp.arange(slot_count, dtype=jnp.int32)
    select = (routes[:, :, None, None] == expert_iota[None, None, :, None]) & (
        slot_rank[:, :, None, None] == slot_iota[None, None, None, :]
    ) & is_cold[:, :, None, None]
    placing = jnp.sum(select.astype(jnp.bfloat16), axis=1)
    outgoing = jnp.einsum(
        "res,rd->esd", placing, tokens, preferred_element_type=jnp.float32
    ).astype(jnp.bfloat16)
    local_gate = w_gate.reshape(w_gate.shape[1:])
    local_up = w_up.reshape(w_up.shape[1:])
    local_down = w_down.reshape(w_down.shape[1:])
    hot_expert = routes[0, 0]
    me = lax.axis_index("expert")
    cores = C
    same_chip = lax.div(me, jnp.int32(cores)) == lax.div(hot_expert, jnp.int32(cores))
    role = jnp.where(me == hot_expert, 0, jnp.where(same_chip, 1, 2))
    gathered, arrived, partner_gate, partner_up, partner_down = hot_gather(X, Z, C, tokens, outgoing, local_gate, local_up, local_down)
    answered = feed_forward(arrived, local_gate, local_up, local_down)

    def hot_ffn(gate_w, up_w, down_w):
        return lambda row_block: feed_forward(row_block.reshape(-1, model_width), gate_w, up_w, down_w).reshape(row_block.shape)

    hot_answer = lax.switch(
        role,
        [hot_ffn(local_gate, local_up, local_down), hot_ffn(partner_gate, partner_up, partner_down), jnp.zeros_like],
        gathered,
    )
    hot_out, returned = hot_scatter(X, Z, C, hot_answer, answered)
    returned = returned.reshape(experts, slot_count, model_width)
    picked = returned[jnp.where(is_cold, routes, 0), jnp.where(is_cold, slot_rank, 0)].astype(jnp.float32)
    values = jnp.where(is_cold[:, :, None], picked, hot_out.astype(jnp.float32)[:, None, :])
    combined = jnp.sum(gate_weights[:, :, None] * values, axis=1)
    return combined.astype(jnp.bfloat16)


def solution(mesh):
    X, Z, C = torus_shape(mesh)
    in_specs = (
        P(("dp", "expert"), None),
        P(("dp", "expert"), None),
        P(("dp", "expert"), None),
        P("expert", None, None),
        P("expert", None, None),
        P("expert", None, None),
    )
    out_specs = P(("dp", "expert"), None)
    return jax.shard_map(functools.partial(shards, X, Z, C), mesh=mesh, in_specs=in_specs, out_specs=out_specs, check_vma=False)
```

```python
import functools

import jax
import jax.numpy as jnp
from jax import lax
from jax.experimental import pallas as pl
from jax.experimental.pallas import tpu as pltpu
from jax.sharding import PartitionSpec as P

MESH = pl.DeviceIdType.MESH


def feed_forward(row_block, gate_w, up_w, down_w):
    gate_part = jnp.dot(row_block, gate_w, preferred_element_type=jnp.float32)
    up_part = jnp.dot(row_block, up_w, preferred_element_type=jnp.float32)
    hidden = lax.optimization_barrier((jax.nn.silu(gate_part) * up_part).astype(jnp.bfloat16))
    return jnp.dot(hidden, down_w, preferred_element_type=jnp.float32).astype(jnp.bfloat16)


def torus_shape(mesh):
    n = mesh.shape["expert"]
    try:
        row = mesh.devices.reshape(-1, n)[0]
        xs = {d.coords[0] for d in row}
        zs = {d.coords[2] for d in row}
        X, Z = len(xs), len(zs)
        C = n // (X * Z)
        if X * Z * C != n:
            raise ValueError
    except Exception:
        X, Z, C = 4, 8, 2
        if X * Z * C != n:
            X, Z, C = 1, n // 2, 2
    return X, Z, C


def coordinates(X, Z, C):
    e = lax.axis_index("expert")
    return e // (Z * C), (e // C) % Z, e % C


def wrap(v, n):
    return (v + 4 * n) % n


def device(X, Z, C, x, z, c):
    return {"expert": wrap(x, X) * (Z * C) + wrap(z, Z) * C + wrap(c, C)}


def peers(X, Z, C, x, z, c):
    out = [(x + k, z, c) for k in range(1, X)]
    if Z > 1:
        out.append((x, z + 1, c))
        if Z > 2:
            out.append((x, z - 1, c))
    if C > 1:
        out.append((x, z, c + 1))
    return out


def barrier(X, Z, C, x, z, c):
    sem = pltpu.get_barrier_semaphore()
    targets = peers(X, Z, C, x, z, c)
    for t in targets:
        pl.semaphore_signal(sem, inc=1, device_id=device(X, Z, C, *t), device_id_type=MESH)
    pl.semaphore_wait(sem, len(targets))


def barrier_all(n):
    me = lax.axis_index("expert")
    sem = pltpu.get_barrier_semaphore()

    for k in range(1, n):
        pl.semaphore_signal(sem, inc=1, device_id={"expert": (me + k) % n}, device_id_type=MESH)
    pl.semaphore_wait(sem, n - 1)


def exchange_copy(src_ref, dst_ref, k, send_sem, recv_sem):
    n = src_ref.shape[0]
    me = lax.axis_index("expert")
    target = (me + k) % n
    return pltpu.make_async_remote_copy(
        src_ref=src_ref.at[target], dst_ref=dst_ref.at[me], send_sem=send_sem.at[k - 1], recv_sem=recv_sem.at[k - 1],
        device_id={"expert": target}, device_id_type=MESH)


def exchange(src_ref, dst_ref, own_sem, send_sem, recv_sem):
    n = src_ref.shape[0]
    me = lax.axis_index("expert")
    own = pltpu.make_async_copy(src_ref.at[me], dst_ref.at[me], own_sem)
    own.start()

    for k in range(1, n):
        exchange_copy(src_ref, dst_ref, k, send_sem, recv_sem).start()
    return own


def exchange_wait(src_ref, dst_ref, own, send_sem, recv_sem):
    n = src_ref.shape[0]
    own.wait()

    for k in range(1, n):
        cp = exchange_copy(src_ref, dst_ref, k, send_sem, recv_sem)
        cp.wait_recv()
        cp.wait_send()


def plane_peers(X, Z, C, x, z, c):
    W = Z * C
    w = z * C + c
    return [{"expert": wrap(x + k, X) * W + w} for k in range(1, X)] + [
        {"expert": x * W + wrap(w + k, W)} for k in range(1, W)]


def barrier_plane(X, Z, C, x, z, c):
    sem = pltpu.get_barrier_semaphore()
    targets = plane_peers(X, Z, C, x, z, c)
    for t in targets:
        pl.semaphore_signal(sem, inc=1, device_id=t, device_id_type=MESH)
    pl.semaphore_wait(sem, len(targets))


def two_stage(X, Z, C, x, z, c):
    W = Z * C
    w = z * C + c
    return W, w


def stage_x(X, Z, C, src_of, dst_of, own_sem, send_sem, recv_sem):
    x, z, c = coordinates(X, Z, C)
    W, w = two_stage(X, Z, C, x, z, c)
    own = pltpu.make_async_copy(src_of(x), dst_of(x), own_sem)
    own.start()
    copies = []
    for k in range(1, X):
        cp = pltpu.make_async_remote_copy(
            src_ref=src_of(wrap(x + k, X)), dst_ref=dst_of(x), send_sem=send_sem.at[k - 1], recv_sem=recv_sem.at[k - 1],
            device_id={"expert": wrap(x + k, X) * W + w}, device_id_type=MESH)
        cp.start()
        copies.append(cp)
    return [own] + copies


def stage_w(X, Z, C, src_of, dst_of, own_sem, send_sem, recv_sem):
    x, z, c = coordinates(X, Z, C)
    W, w = two_stage(X, Z, C, x, z, c)
    own = pltpu.make_async_copy(src_of(w), dst_of(w), own_sem)
    own.start()
    copies = []
    for k in range(1, W):
        cp = pltpu.make_async_remote_copy(
            src_ref=src_of(wrap(w + k, W)), dst_ref=dst_of(w), send_sem=send_sem.at[k - 1], recv_sem=recv_sem.at[k - 1],
            device_id={"expert": x * W + wrap(w + k, W)}, device_id_type=MESH)
        cp.start()
        copies.append(cp)
    return [own] + copies


def wait_recvs(copies):
    copies[0].wait()
    for cp in copies[1:]:
        cp.wait_recv()


def wait_sends(copies):
    for cp in copies[1:]:
        cp.wait_send()


def gather_kernel(X, Z, C, tok_ref, cold_ref, wg_ref, wu_ref, wd_ref, out_ref, cold_out, pg_ref, pu_ref, pd_ref,
                  cold_mid, own_sem, c1_send, c1_recv, c2_send, c2_recv, w_send, w_recv, sx_send, sx_recv, sp_send, sp_recv, sm_send, sm_recv):
    x, z, c = coordinates(X, Z, C)
    zp, zm = Z // 2, (Z - 1) // 2
    dirn = 1 - 2 * (c % 2)
    barrier_plane(X, Z, C, x, z, c)
    own = pltpu.make_async_copy(tok_ref, out_ref.at[z, x], own_sem.at[0])
    own.start()
    xcopies = []
    for k in range(1, X):
        cp = pltpu.make_async_remote_copy(
            src_ref=tok_ref, dst_ref=out_ref.at[z, x], send_sem=sx_send.at[k - 1], recv_sem=sx_recv.at[k - 1],
            device_id=device(X, Z, C, x + k, z, c), device_id_type=MESH)
        cp.start()
        xcopies.append(cp)
    cold1 = stage_x(X, Z, C, lambda i: cold_ref.at[i], lambda i: cold_mid.at[:, i], own_sem.at[1], c1_send, c1_recv)
    own.wait()
    for cp in xcopies:
        cp.wait_recv()

    H = 2 if X % 2 == 0 else 1
    part = X // H

    def ring_copy(blk, h, send_sem, recv_sem, target):
        piece = out_ref.at[blk, pl.ds(h * part, part)]
        return pltpu.make_async_remote_copy(
            src_ref=piece, dst_ref=piece, send_sem=send_sem, recv_sem=recv_sem,
            device_id=device(X, Z, C, x, target, c), device_id_type=MESH)

    plus, minus = [], []
    for s in range(max(zp, zm)):
        if s < zp:
            blk = wrap(z - s * dirn, Z)
            step = []
            for h in range(H):
                if s >= 1:
                    plus[s - 1][h].wait_recv()
                cp = ring_copy(blk, h, sp_send.at[s * H + h], sp_recv.at[s * H + h], z + dirn)
                cp.start()
                step.append(cp)
            plus.append(step)
        if s < zm:
            blk = wrap(z + s * dirn, Z)
            step = []
            for h in range(H):
                if s >= 1:
                    minus[s - 1][h].wait_recv()
                cp = ring_copy(blk, h, sm_send.at[s * H + h], sm_recv.at[s * H + h], z - dirn)
                cp.start()
                step.append(cp)
            minus.append(step)
        if s == 0:
            wait_recvs(cold1)
            cold2 = stage_w(X, Z, C, lambda i: cold_mid.at[i], lambda i: cold_out.at[i], own_sem.at[2], c2_send, c2_recv)
            wcopies = []
            if C > 1:
                for j, (src, dst) in enumerate(((wg_ref, pg_ref), (wu_ref, pu_ref), (wd_ref, pd_ref))):
                    cp = pltpu.make_async_remote_copy(
                        src_ref=src, dst_ref=dst, send_sem=w_send.at[j], recv_sem=w_recv.at[j],
                        device_id=device(X, Z, C, x, z, c + 1), device_id_type=MESH)
                    cp.start()
                    wcopies.append(cp)
    for step in plus[-1:] + minus[-1:]:
        for cp in step:
            cp.wait_recv()
    for cp in xcopies + [cp for step in plus + minus for cp in step]:
        cp.wait_send()
    wait_recvs(cold2)
    wait_sends(cold1)
    wait_sends(cold2)
    for cp in wcopies:
        cp.wait_recv()
        cp.wait_send()


def scatter_kernel(X, Z, C, o_ref, cold_ref, out_ref, cold_out, cold_mid, own_sem, c1_send, c1_recv, c2_send, c2_recv, plus_buf, plus_send, minus_buf, minus_send, xbuf, xsend,
                   sp_send, sp_recv, sm_send, sm_recv, sx_send, sx_recv):
    x, z, c = coordinates(X, Z, C)
    zp, zm = Z // 2, (Z - 1) // 2
    dirn = 1 - 2 * (c % 2)
    barrier_plane(X, Z, C, x, z, c)

    def chip_sum(blk):
        return o_ref[blk].astype(jnp.float32)

    plus, minus = [], []
    for s in range(max(zp, zm)):
        if s < zp:
            val = chip_sum(wrap(z + (zp - s) * dirn, Z))
            if s >= 1:
                plus[s - 1].wait_recv()
                val = val + plus_buf[s - 1].astype(jnp.float32)
            plus_send[s] = val.astype(jnp.bfloat16)
            cp = pltpu.make_async_remote_copy(
                src_ref=plus_send.at[s], dst_ref=plus_buf.at[s], send_sem=sp_send.at[s], recv_sem=sp_recv.at[s],
                device_id=device(X, Z, C, x, z + dirn, c), device_id_type=MESH)
            cp.start()
            plus.append(cp)
        if s < zm:
            val = chip_sum(wrap(z - (zm - s) * dirn, Z))
            if s >= 1:
                minus[s - 1].wait_recv()
                val = val + minus_buf[s - 1].astype(jnp.float32)
            minus_send[s] = val.astype(jnp.bfloat16)
            cp = pltpu.make_async_remote_copy(
                src_ref=minus_send.at[s], dst_ref=minus_buf.at[s], send_sem=sm_send.at[s], recv_sem=sm_recv.at[s],
                device_id=device(X, Z, C, x, z - dirn, c), device_id_type=MESH)
            cp.start()
            minus.append(cp)
        if s == 0:
            cold1 = stage_w(X, Z, C, lambda i: cold_ref.at[i], lambda i: cold_mid.at[i], own_sem.at[0], c2_send, c2_recv)
    wait_recvs(cold1)
    cold2 = stage_x(X, Z, C, lambda i: cold_mid.at[:, i], lambda i: cold_out.at[i], own_sem.at[1], c1_send, c1_recv)
    total = chip_sum(z)
    if zp:
        plus[zp - 1].wait_recv()
        total = total + plus_buf[zp - 1].astype(jnp.float32)
    if zm:
        minus[zm - 1].wait_recv()
        total = total + minus_buf[zm - 1].astype(jnp.float32)
    xsend[...] = total.astype(jnp.bfloat16)
    xcopies = []
    for k in range(1, X):
        cp = pltpu.make_async_remote_copy(
            src_ref=xsend.at[(x + k) % X], dst_ref=xbuf.at[k - 1], send_sem=sx_send.at[k - 1], recv_sem=sx_recv.at[k - 1],
            device_id=device(X, Z, C, x + k, z, c), device_id_type=MESH)
        cp.start()
        xcopies.append(cp)
    result = xsend[x].astype(jnp.float32)
    for k, cp in enumerate(xcopies):
        cp.wait_recv()
        result = result + xbuf[k].astype(jnp.float32)
    out_ref[...] = result.astype(out_ref.dtype)
    for cp in plus + minus + xcopies:
        cp.wait_send()
    wait_recvs(cold2)
    wait_sends(cold1)
    wait_sends(cold2)


def hot_gather(X, Z, C, tokens, outgoing, w_gate, w_up, w_down):
    R, D = tokens.shape
    zp, zm = Z // 2, (Z - 1) // 2
    W = Z * C
    n, S, _ = outgoing.shape
    outgoing = outgoing.reshape(X, W, S, D)
    dma = pltpu.SemaphoreType.DMA
    vmem = pl.BlockSpec(memory_space=pltpu.VMEM)
    anywhere = pl.BlockSpec(memory_space=pl.ANY)
    return pl.pallas_call(
        functools.partial(gather_kernel, X, Z, C),
        out_shape=(
            jax.ShapeDtypeStruct((Z, X, R, D), tokens.dtype), jax.ShapeDtypeStruct((W, X, S, D), outgoing.dtype),
            jax.ShapeDtypeStruct(w_gate.shape, w_gate.dtype), jax.ShapeDtypeStruct(w_up.shape, w_up.dtype),
            jax.ShapeDtypeStruct(w_down.shape, w_down.dtype),
        ),
        in_specs=[vmem, vmem, anywhere, anywhere, anywhere],
        out_specs=(vmem, vmem, anywhere, anywhere, anywhere),
        scratch_shapes=[
            pltpu.VMEM((W, X, S, D), outgoing.dtype),
            dma((3,)), dma((max(X - 1, 1),)), dma((max(X - 1, 1),)), dma((W - 1,)), dma((W - 1,)), dma((3,)), dma((3,)),
            dma((max(X - 1, 1),)), dma((max(X - 1, 1),)),
            dma((max(zp, 1) * 2,)), dma((max(zp, 1) * 2,)),
            dma((max(zm, 1) * 2,)), dma((max(zm, 1) * 2,)),
        ],
        compiler_params=pltpu.CompilerParams(collective_id=0, has_side_effects=True),
    )(tokens, outgoing, w_gate, w_up, w_down)


def hot_scatter(X, Z, C, answered, cold_answered):
    _, _, R, D = answered.shape
    zp, zm = Z // 2, (Z - 1) // 2
    W, _, S, _ = cold_answered.shape
    dma = pltpu.SemaphoreType.DMA
    bf = answered.dtype
    vmem = pl.BlockSpec(memory_space=pltpu.VMEM)
    return pl.pallas_call(
        functools.partial(scatter_kernel, X, Z, C),
        out_shape=(jax.ShapeDtypeStruct((R, D), bf), jax.ShapeDtypeStruct((X, W, S, D), cold_answered.dtype)),
        in_specs=[vmem, vmem],
        out_specs=(vmem, vmem),
        scratch_shapes=[
            pltpu.VMEM((W, X, S, D), cold_answered.dtype),
            dma((2,)), dma((max(X - 1, 1),)), dma((max(X - 1, 1),)), dma((W - 1,)), dma((W - 1,)),
            pltpu.VMEM((max(zp, 1), X, R, D), bf), pltpu.VMEM((max(zp, 1), X, R, D), bf),
            pltpu.VMEM((max(zm, 1), X, R, D), bf), pltpu.VMEM((max(zm, 1), X, R, D), bf),
            pltpu.VMEM((max(X - 1, 1), R, D), bf), pltpu.VMEM((X, R, D), bf),
            dma((max(zp, 1),)), dma((max(zp, 1),)),
            dma((max(zm, 1),)), dma((max(zm, 1),)),
            dma((max(X - 1, 1),)), dma((max(X - 1, 1),)),
        ],
        compiler_params=pltpu.CompilerParams(collective_id=1, has_side_effects=True),
    )(answered, cold_answered)


def shards(X, Z, C, tokens, routes, gate_weights, w_gate, w_up, w_down):
    devices = lax.axis_size("expert")
    experts = w_gate.shape[0] * devices
    row_count = routes.shape[0]
    top_count = routes.shape[1]
    model_width = tokens.shape[1]
    slot_count = (row_count * (top_count - 1) + experts - 2) // (experts - 1)
    is_cold = jnp.arange(top_count)[None, :] >= 1
    flat_ids = routes.reshape(-1)
    flat_cold = jnp.broadcast_to(is_cold, routes.shape).reshape(-1)
    expert_iota = jnp.arange(experts, dtype=jnp.int32)
    one_hot = ((flat_ids[:, None] == expert_iota[None, :]) & flat_cold[:, None]).astype(jnp.int32)
    slot_rank = (jnp.sum(jnp.cumsum(one_hot, axis=0) * one_hot, axis=1) - 1).reshape(routes.shape)
    slot_iota = jnp.arange(slot_count, dtype=jnp.int32)
    select = (routes[:, :, None, None] == expert_iota[None, None, :, None]) & (
        slot_rank[:, :, None, None] == slot_iota[None, None, None, :]
    ) & is_cold[:, :, None, None]
    placing = jnp.sum(select.astype(jnp.bfloat16), axis=1)
    outgoing = jnp.einsum(
        "res,rd->esd", placing, tokens, preferred_element_type=jnp.float32
    ).astype(jnp.bfloat16)
    local_gate = w_gate.reshape(w_gate.shape[1:])
    local_up = w_up.reshape(w_up.shape[1:])
    local_down = w_down.reshape(w_down.shape[1:])
    hot_expert = routes[0, 0]
    me = lax.axis_index("expert")
    cores = C
    same_chip = lax.div(me, jnp.int32(cores)) == lax.div(hot_expert, jnp.int32(cores))
    role = jnp.where(me == hot_expert, 0, jnp.where(same_chip, 1, 2))
    gathered, arrived, partner_gate, partner_up, partner_down = hot_gather(X, Z, C, tokens, outgoing, local_gate, local_up, local_down)
    answered = feed_forward(arrived, local_gate, local_up, local_down)

    def hot_ffn(gate_w, up_w, down_w):
        return lambda row_block: feed_forward(row_block.reshape(-1, model_width), gate_w, up_w, down_w).reshape(row_block.shape)

    hot_answer = lax.switch(
        role,
        [hot_ffn(local_gate, local_up, local_down), hot_ffn(partner_gate, partner_up, partner_down), jnp.zeros_like],
        gathered,
    )
    hot_out, returned = hot_scatter(X, Z, C, hot_answer, answered)
    returned = returned.reshape(experts, slot_count, model_width)
    index = jnp.where(is_cold, routes * slot_count + slot_rank, 0)
    picked = returned.reshape(-1, model_width)[index].astype(jnp.float32)
    values = jnp.where(is_cold[:, :, None], picked, hot_out.astype(jnp.float32)[:, None, :])
    combined = jnp.sum(gate_weights[:, :, None] * values, axis=1)
    return combined.astype(jnp.bfloat16)


def solution(mesh):
    X, Z, C = torus_shape(mesh)
    in_specs = (
        P(("dp", "expert"), None),
        P(("dp", "expert"), None),
        P(("dp", "expert"), None),
        P("expert", None, None),
        P("expert", None, None),
        P("expert", None, None),
    )
    out_specs = P(("dp", "expert"), None)
    return jax.shard_map(functools.partial(shards, X, Z, C), mesh=mesh, in_specs=in_specs, out_specs=out_specs, check_vma=False)
```

```python
import functools

import jax
import jax.numpy as jnp
from jax import lax
from jax.experimental import pallas as pl
from jax.experimental.pallas import tpu as pltpu
from jax.sharding import PartitionSpec as P

MESH = pl.DeviceIdType.MESH


def feed_forward(row_block, gate_w, up_w, down_w):
    gate_part = jnp.dot(row_block, gate_w, preferred_element_type=jnp.float32)
    up_part = jnp.dot(row_block, up_w, preferred_element_type=jnp.float32)
    hidden = lax.optimization_barrier((jax.nn.silu(gate_part) * up_part).astype(jnp.bfloat16))
    return jnp.dot(hidden, down_w, preferred_element_type=jnp.float32).astype(jnp.bfloat16)


def torus_shape(mesh):
    n = mesh.shape["expert"]
    try:
        row = mesh.devices.reshape(-1, n)[0]
        xs = {d.coords[0] for d in row}
        zs = {d.coords[2] for d in row}
        X, Z = len(xs), len(zs)
        C = n // (X * Z)
        if X * Z * C != n:
            raise ValueError
    except Exception:
        X, Z, C = 4, 8, 2
        if X * Z * C != n:
            X, Z, C = 1, n // 2, 2
    return X, Z, C


def coordinates(X, Z, C):
    e = lax.axis_index("expert")
    return e // (Z * C), (e // C) % Z, e % C


def wrap(v, n):
    return (v + 4 * n) % n


def device(X, Z, C, x, z, c):
    return {"expert": wrap(x, X) * (Z * C) + wrap(z, Z) * C + wrap(c, C)}


def peers(X, Z, C, x, z, c):
    out = [(x + k, z, c) for k in range(1, X)]
    if Z > 1:
        out.append((x, z + 1, c))
        if Z > 2:
            out.append((x, z - 1, c))
    if C > 1:
        out.append((x, z, c + 1))
    return out


def barrier(X, Z, C, x, z, c):
    sem = pltpu.get_barrier_semaphore()
    targets = peers(X, Z, C, x, z, c)
    for t in targets:
        pl.semaphore_signal(sem, inc=1, device_id=device(X, Z, C, *t), device_id_type=MESH)
    pl.semaphore_wait(sem, len(targets))


def barrier_all(n):
    me = lax.axis_index("expert")
    sem = pltpu.get_barrier_semaphore()

    for k in range(1, n):
        pl.semaphore_signal(sem, inc=1, device_id={"expert": (me + k) % n}, device_id_type=MESH)
    pl.semaphore_wait(sem, n - 1)


def exchange_copy(src_ref, dst_ref, k, send_sem, recv_sem):
    n = src_ref.shape[0]
    me = lax.axis_index("expert")
    target = (me + k) % n
    return pltpu.make_async_remote_copy(
        src_ref=src_ref.at[target], dst_ref=dst_ref.at[me], send_sem=send_sem.at[k - 1], recv_sem=recv_sem.at[k - 1],
        device_id={"expert": target}, device_id_type=MESH)


def exchange(src_ref, dst_ref, own_sem, send_sem, recv_sem):
    n = src_ref.shape[0]
    me = lax.axis_index("expert")
    own = pltpu.make_async_copy(src_ref.at[me], dst_ref.at[me], own_sem)
    own.start()

    for k in range(1, n):
        exchange_copy(src_ref, dst_ref, k, send_sem, recv_sem).start()
    return own


def exchange_wait(src_ref, dst_ref, own, send_sem, recv_sem):
    n = src_ref.shape[0]
    own.wait()

    for k in range(1, n):
        cp = exchange_copy(src_ref, dst_ref, k, send_sem, recv_sem)
        cp.wait_recv()
        cp.wait_send()


def plane_peers(X, Z, C, x, z, c):
    W = Z * C
    w = z * C + c
    return [{"expert": wrap(x + k, X) * W + w} for k in range(1, X)] + [
        {"expert": x * W + wrap(w + k, W)} for k in range(1, W)]


def barrier_plane(X, Z, C, x, z, c):
    sem = pltpu.get_barrier_semaphore()
    targets = plane_peers(X, Z, C, x, z, c)
    for t in targets:
        pl.semaphore_signal(sem, inc=1, device_id=t, device_id_type=MESH)
    pl.semaphore_wait(sem, len(targets))


def two_stage(X, Z, C, x, z, c):
    W = Z * C
    w = z * C + c
    return W, w


def stage_x(X, Z, C, src_of, dst_of, own_sem, send_sem, recv_sem):
    x, z, c = coordinates(X, Z, C)
    W, w = two_stage(X, Z, C, x, z, c)
    own = pltpu.make_async_copy(src_of(x), dst_of(x), own_sem)
    own.start()
    copies = []
    for k in range(1, X):
        cp = pltpu.make_async_remote_copy(
            src_ref=src_of(wrap(x + k, X)), dst_ref=dst_of(x), send_sem=send_sem.at[k - 1], recv_sem=recv_sem.at[k - 1],
            device_id={"expert": wrap(x + k, X) * W + w}, device_id_type=MESH)
        cp.start()
        copies.append(cp)
    return [own] + copies


def stage_w(X, Z, C, src_of, dst_of, own_sem, send_sem, recv_sem):
    x, z, c = coordinates(X, Z, C)
    W, w = two_stage(X, Z, C, x, z, c)
    own = pltpu.make_async_copy(src_of(w), dst_of(w), own_sem)
    own.start()
    copies = []
    for k in range(1, W):
        cp = pltpu.make_async_remote_copy(
            src_ref=src_of(wrap(w + k, W)), dst_ref=dst_of(w), send_sem=send_sem.at[k - 1], recv_sem=recv_sem.at[k - 1],
            device_id={"expert": x * W + wrap(w + k, W)}, device_id_type=MESH)
        cp.start()
        copies.append(cp)
    return [own] + copies


def wait_recvs(copies):
    copies[0].wait()
    for cp in copies[1:]:
        cp.wait_recv()


def wait_sends(copies):
    for cp in copies[1:]:
        cp.wait_send()


def gather_kernel(X, Z, C, tok_ref, cold_ref, wg_ref, wu_ref, wd_ref, out_ref, cold_out, pg_ref, pu_ref, pd_ref,
                  cold_mid, own_sem, c1_send, c1_recv, c2_send, c2_recv, w_send, w_recv, sx_send, sx_recv, sp_send, sp_recv, sm_send, sm_recv):
    x, z, c = coordinates(X, Z, C)
    zp, zm = Z // 2, (Z - 1) // 2
    dirn = 1 - 2 * (c % 2)
    barrier_plane(X, Z, C, x, z, c)
    own = pltpu.make_async_copy(tok_ref, out_ref.at[z, x], own_sem.at[0])
    own.start()
    xcopies = []
    for k in range(1, X):
        cp = pltpu.make_async_remote_copy(
            src_ref=tok_ref, dst_ref=out_ref.at[z, x], send_sem=sx_send.at[k - 1], recv_sem=sx_recv.at[k - 1],
            device_id=device(X, Z, C, x + k, z, c), device_id_type=MESH)
        cp.start()
        xcopies.append(cp)
    cold1 = stage_x(X, Z, C, lambda i: cold_ref.at[i], lambda i: cold_mid.at[:, i], own_sem.at[1], c1_send, c1_recv)
    own.wait()
    for cp in xcopies:
        cp.wait_recv()

    H = 2 if X % 2 == 0 else 1
    part = X // H

    def ring_copy(blk, h, send_sem, recv_sem, target):
        piece = out_ref.at[blk, pl.ds(h * part, part)]
        return pltpu.make_async_remote_copy(
            src_ref=piece, dst_ref=piece, send_sem=send_sem, recv_sem=recv_sem,
            device_id=device(X, Z, C, x, target, c), device_id_type=MESH)

    plus, minus = [], []
    for s in range(max(zp, zm)):
        if s < zp:
            blk = wrap(z - s * dirn, Z)
            step = []
            for h in range(H):
                if s >= 1:
                    plus[s - 1][h].wait_recv()
                cp = ring_copy(blk, h, sp_send.at[s * H + h], sp_recv.at[s * H + h], z + dirn)
                cp.start()
                step.append(cp)
            plus.append(step)
        if s < zm:
            blk = wrap(z + s * dirn, Z)
            step = []
            for h in range(H):
                if s >= 1:
                    minus[s - 1][h].wait_recv()
                cp = ring_copy(blk, h, sm_send.at[s * H + h], sm_recv.at[s * H + h], z - dirn)
                cp.start()
                step.append(cp)
            minus.append(step)
        if s == 0:
            wait_recvs(cold1)
            cold2 = stage_w(X, Z, C, lambda i: cold_mid.at[i], lambda i: cold_out.at[i], own_sem.at[2], c2_send, c2_recv)
            wcopies = []
            if C > 1:
                for j, (src, dst) in enumerate(((wg_ref, pg_ref), (wu_ref, pu_ref), (wd_ref, pd_ref))):
                    cp = pltpu.make_async_remote_copy(
                        src_ref=src, dst_ref=dst, send_sem=w_send.at[j], recv_sem=w_recv.at[j],
                        device_id=device(X, Z, C, x, z, c + 1), device_id_type=MESH)
                    cp.start()
                    wcopies.append(cp)
    for step in plus[-1:] + minus[-1:]:
        for cp in step:
            cp.wait_recv()
    for cp in xcopies + [cp for step in plus + minus for cp in step]:
        cp.wait_send()
    wait_recvs(cold2)
    wait_sends(cold1)
    wait_sends(cold2)
    for cp in wcopies:
        cp.wait_recv()
        cp.wait_send()


def scatter_kernel(X, Z, C, o_ref, cold_ref, out_ref, cold_out, cold_mid, own_sem, c1_send, c1_recv, c2_send, c2_recv, plus_buf, plus_send, minus_buf, minus_send, xbuf, xsend,
                   sp_send, sp_recv, sm_send, sm_recv, sx_send, sx_recv):
    x, z, c = coordinates(X, Z, C)
    zp, zm = Z // 2, (Z - 1) // 2
    dirn = 1 - 2 * (c % 2)
    barrier_plane(X, Z, C, x, z, c)

    def chip_sum(blk):
        return o_ref[blk].astype(jnp.float32)

    H = 2 if X % 2 == 0 else 1
    part = X // H

    def ring_step(chain, buf, send_buf, send_sem, recv_sem, s, blk, target):
        step = []
        for h in range(H):
            rows = pl.ds(h * part, part)
            val = o_ref[blk, rows].astype(jnp.float32)
            if s >= 1:
                chain[s - 1][h].wait_recv()
                val = val + buf[s - 1, rows].astype(jnp.float32)
            send_buf[s, rows] = val.astype(jnp.bfloat16)
            cp = pltpu.make_async_remote_copy(
                src_ref=send_buf.at[s, rows], dst_ref=buf.at[s, rows], send_sem=send_sem.at[s * H + h],
                recv_sem=recv_sem.at[s * H + h], device_id=device(X, Z, C, x, target, c), device_id_type=MESH)
            cp.start()
            step.append(cp)
        chain.append(step)

    plus, minus = [], []
    for s in range(max(zp, zm)):
        if s < zp:
            ring_step(plus, plus_buf, plus_send, sp_send, sp_recv, s, wrap(z + (zp - s) * dirn, Z), z + dirn)
        if s < zm:
            ring_step(minus, minus_buf, minus_send, sm_send, sm_recv, s, wrap(z - (zm - s) * dirn, Z), z - dirn)
        if s == 0:
            cold1 = stage_w(X, Z, C, lambda i: cold_ref.at[i], lambda i: cold_mid.at[i], own_sem.at[0], c2_send, c2_recv)
    wait_recvs(cold1)
    cold2 = stage_x(X, Z, C, lambda i: cold_mid.at[:, i], lambda i: cold_out.at[i], own_sem.at[1], c1_send, c1_recv)
    total = chip_sum(z)
    if zp:
        for cp in plus[zp - 1]:
            cp.wait_recv()
        total = total + plus_buf[zp - 1].astype(jnp.float32)
    if zm:
        for cp in minus[zm - 1]:
            cp.wait_recv()
        total = total + minus_buf[zm - 1].astype(jnp.float32)
    xsend[...] = total.astype(jnp.bfloat16)
    xcopies = []
    for k in range(1, X):
        cp = pltpu.make_async_remote_copy(
            src_ref=xsend.at[(x + k) % X], dst_ref=xbuf.at[k - 1], send_sem=sx_send.at[k - 1], recv_sem=sx_recv.at[k - 1],
            device_id=device(X, Z, C, x + k, z, c), device_id_type=MESH)
        cp.start()
        xcopies.append(cp)
    result = xsend[x].astype(jnp.float32)
    for k, cp in enumerate(xcopies):
        cp.wait_recv()
        result = result + xbuf[k].astype(jnp.float32)
    out_ref[...] = result.astype(out_ref.dtype)
    for cp in [cp for step in plus + minus for cp in step] + xcopies:
        cp.wait_send()
    wait_recvs(cold2)
    wait_sends(cold1)
    wait_sends(cold2)


def hot_gather(X, Z, C, tokens, outgoing, w_gate, w_up, w_down):
    R, D = tokens.shape
    zp, zm = Z // 2, (Z - 1) // 2
    W = Z * C
    n, S, _ = outgoing.shape
    outgoing = outgoing.reshape(X, W, S, D)
    dma = pltpu.SemaphoreType.DMA
    vmem = pl.BlockSpec(memory_space=pltpu.VMEM)
    anywhere = pl.BlockSpec(memory_space=pl.ANY)
    return pl.pallas_call(
        functools.partial(gather_kernel, X, Z, C),
        out_shape=(
            jax.ShapeDtypeStruct((Z, X, R, D), tokens.dtype), jax.ShapeDtypeStruct((W, X, S, D), outgoing.dtype),
            jax.ShapeDtypeStruct(w_gate.shape, w_gate.dtype), jax.ShapeDtypeStruct(w_up.shape, w_up.dtype),
            jax.ShapeDtypeStruct(w_down.shape, w_down.dtype),
        ),
        in_specs=[vmem, vmem, anywhere, anywhere, anywhere],
        out_specs=(vmem, vmem, anywhere, anywhere, anywhere),
        scratch_shapes=[
            pltpu.VMEM((W, X, S, D), outgoing.dtype),
            dma((3,)), dma((max(X - 1, 1),)), dma((max(X - 1, 1),)), dma((W - 1,)), dma((W - 1,)), dma((3,)), dma((3,)),
            dma((max(X - 1, 1),)), dma((max(X - 1, 1),)),
            dma((max(zp, 1) * 2,)), dma((max(zp, 1) * 2,)),
            dma((max(zm, 1) * 2,)), dma((max(zm, 1) * 2,)),
        ],
        compiler_params=pltpu.CompilerParams(collective_id=0, has_side_effects=True),
    )(tokens, outgoing, w_gate, w_up, w_down)


def hot_scatter(X, Z, C, answered, cold_answered):
    _, _, R, D = answered.shape
    zp, zm = Z // 2, (Z - 1) // 2
    W, _, S, _ = cold_answered.shape
    dma = pltpu.SemaphoreType.DMA
    bf = answered.dtype
    vmem = pl.BlockSpec(memory_space=pltpu.VMEM)
    return pl.pallas_call(
        functools.partial(scatter_kernel, X, Z, C),
        out_shape=(jax.ShapeDtypeStruct((R, D), bf), jax.ShapeDtypeStruct((X, W, S, D), cold_answered.dtype)),
        in_specs=[vmem, vmem],
        out_specs=(vmem, vmem),
        scratch_shapes=[
            pltpu.VMEM((W, X, S, D), cold_answered.dtype),
            dma((2,)), dma((max(X - 1, 1),)), dma((max(X - 1, 1),)), dma((W - 1,)), dma((W - 1,)),
            pltpu.VMEM((max(zp, 1), X, R, D), bf), pltpu.VMEM((max(zp, 1), X, R, D), bf),
            pltpu.VMEM((max(zm, 1), X, R, D), bf), pltpu.VMEM((max(zm, 1), X, R, D), bf),
            pltpu.VMEM((max(X - 1, 1), R, D), bf), pltpu.VMEM((X, R, D), bf),
            dma((max(zp, 1) * 2,)), dma((max(zp, 1) * 2,)),
            dma((max(zm, 1) * 2,)), dma((max(zm, 1) * 2,)),
            dma((max(X - 1, 1),)), dma((max(X - 1, 1),)),
        ],
        compiler_params=pltpu.CompilerParams(collective_id=1, has_side_effects=True),
    )(answered, cold_answered)


def shards(X, Z, C, tokens, routes, gate_weights, w_gate, w_up, w_down):
    devices = lax.axis_size("expert")
    experts = w_gate.shape[0] * devices
    row_count = routes.shape[0]
    top_count = routes.shape[1]
    model_width = tokens.shape[1]
    slot_count = (row_count * (top_count - 1) + experts - 2) // (experts - 1)
    is_cold = jnp.arange(top_count)[None, :] >= 1
    flat_ids = routes.reshape(-1)
    flat_cold = jnp.broadcast_to(is_cold, routes.shape).reshape(-1)
    expert_iota = jnp.arange(experts, dtype=jnp.int32)
    one_hot = ((flat_ids[:, None] == expert_iota[None, :]) & flat_cold[:, None]).astype(jnp.int32)
    slot_rank = (jnp.sum(jnp.cumsum(one_hot, axis=0) * one_hot, axis=1) - 1).reshape(routes.shape)
    slot_iota = jnp.arange(slot_count, dtype=jnp.int32)
    select = (routes[:, :, None, None] == expert_iota[None, None, :, None]) & (
        slot_rank[:, :, None, None] == slot_iota[None, None, None, :]
    ) & is_cold[:, :, None, None]
    placing = jnp.sum(select.astype(jnp.bfloat16), axis=1)
    outgoing = jnp.einsum(
        "res,rd->esd", placing, tokens, preferred_element_type=jnp.float32
    ).astype(jnp.bfloat16)
    local_gate = w_gate.reshape(w_gate.shape[1:])
    local_up = w_up.reshape(w_up.shape[1:])
    local_down = w_down.reshape(w_down.shape[1:])
    hot_expert = routes[0, 0]
    me = lax.axis_index("expert")
    cores = C
    same_chip = lax.div(me, jnp.int32(cores)) == lax.div(hot_expert, jnp.int32(cores))
    role = jnp.where(me == hot_expert, 0, jnp.where(same_chip, 1, 2))
    gathered, arrived, partner_gate, partner_up, partner_down = hot_gather(X, Z, C, tokens, outgoing, local_gate, local_up, local_down)
    answered = feed_forward(arrived, local_gate, local_up, local_down)

    def hot_ffn(gate_w, up_w, down_w):
        return lambda row_block: feed_forward(row_block.reshape(-1, model_width), gate_w, up_w, down_w).reshape(row_block.shape)

    hot_answer = lax.switch(
        role,
        [hot_ffn(local_gate, local_up, local_down), hot_ffn(partner_gate, partner_up, partner_down), jnp.zeros_like],
        gathered,
    )
    hot_out, returned = hot_scatter(X, Z, C, hot_answer, answered)
    returned = returned.reshape(experts, slot_count, model_width)
    index = jnp.where(is_cold, routes * slot_count + slot_rank, 0)
    picked = returned.reshape(-1, model_width)[index].astype(jnp.float32)
    values = jnp.where(is_cold[:, :, None], picked, hot_out.astype(jnp.float32)[:, None, :])
    combined = jnp.sum(gate_weights[:, :, None] * values, axis=1)
    return combined.astype(jnp.bfloat16)


def solution(mesh):
    X, Z, C = torus_shape(mesh)
    in_specs = (
        P(("dp", "expert"), None),
        P(("dp", "expert"), None),
        P(("dp", "expert"), None),
        P("expert", None, None),
        P("expert", None, None),
        P("expert", None, None),
    )
    out_specs = P(("dp", "expert"), None)
    return jax.shard_map(functools.partial(shards, X, Z, C), mesh=mesh, in_specs=in_specs, out_specs=out_specs, check_vma=False)
```

```python
import functools

import jax
import jax.numpy as jnp
from jax import lax
from jax.experimental import pallas as pl
from jax.experimental.pallas import tpu as pltpu
from jax.sharding import PartitionSpec as P

MESH = pl.DeviceIdType.MESH


def feed_forward(row_block, gate_w, up_w, down_w):
    gate_part = jnp.dot(row_block, gate_w, preferred_element_type=jnp.float32)
    up_part = jnp.dot(row_block, up_w, preferred_element_type=jnp.float32)
    hidden = lax.optimization_barrier((jax.nn.silu(gate_part) * up_part).astype(jnp.bfloat16))
    return jnp.dot(hidden, down_w, preferred_element_type=jnp.float32).astype(jnp.bfloat16)


def torus_shape(mesh):
    n = mesh.shape["expert"]
    try:
        row = mesh.devices.reshape(-1, n)[0]
        xs = {d.coords[0] for d in row}
        zs = {d.coords[2] for d in row}
        X, Z = len(xs), len(zs)
        C = n // (X * Z)
        if X * Z * C != n:
            raise ValueError
    except Exception:
        X, Z, C = 4, 8, 2
        if X * Z * C != n:
            X, Z, C = 1, n // 2, 2
    return X, Z, C


def coordinates(X, Z, C):
    e = lax.axis_index("expert")
    return e // (Z * C), (e // C) % Z, e % C


def ring_pieces(X):
    return 4 if X % 4 == 0 else (2 if X % 2 == 0 else 1)


def wrap(v, n):
    return (v + 4 * n) % n


def device(X, Z, C, x, z, c):
    return {"expert": wrap(x, X) * (Z * C) + wrap(z, Z) * C + wrap(c, C)}


def peers(X, Z, C, x, z, c):
    out = [(x + k, z, c) for k in range(1, X)]
    if Z > 1:
        out.append((x, z + 1, c))
        if Z > 2:
            out.append((x, z - 1, c))
    if C > 1:
        out.append((x, z, c + 1))
    return out


def barrier(X, Z, C, x, z, c):
    sem = pltpu.get_barrier_semaphore()
    targets = peers(X, Z, C, x, z, c)
    for t in targets:
        pl.semaphore_signal(sem, inc=1, device_id=device(X, Z, C, *t), device_id_type=MESH)
    pl.semaphore_wait(sem, len(targets))


def barrier_all(n):
    me = lax.axis_index("expert")
    sem = pltpu.get_barrier_semaphore()

    for k in range(1, n):
        pl.semaphore_signal(sem, inc=1, device_id={"expert": (me + k) % n}, device_id_type=MESH)
    pl.semaphore_wait(sem, n - 1)


def exchange_copy(src_ref, dst_ref, k, send_sem, recv_sem):
    n = src_ref.shape[0]
    me = lax.axis_index("expert")
    target = (me + k) % n
    return pltpu.make_async_remote_copy(
        src_ref=src_ref.at[target], dst_ref=dst_ref.at[me], send_sem=send_sem.at[k - 1], recv_sem=recv_sem.at[k - 1],
        device_id={"expert": target}, device_id_type=MESH)


def exchange(src_ref, dst_ref, own_sem, send_sem, recv_sem):
    n = src_ref.shape[0]
    me = lax.axis_index("expert")
    own = pltpu.make_async_copy(src_ref.at[me], dst_ref.at[me], own_sem)
    own.start()

    for k in range(1, n):
        exchange_copy(src_ref, dst_ref, k, send_sem, recv_sem).start()
    return own


def exchange_wait(src_ref, dst_ref, own, send_sem, recv_sem):
    n = src_ref.shape[0]
    own.wait()

    for k in range(1, n):
        cp = exchange_copy(src_ref, dst_ref, k, send_sem, recv_sem)
        cp.wait_recv()
        cp.wait_send()


def plane_peers(X, Z, C, x, z, c):
    W = Z * C
    w = z * C + c
    return [{"expert": wrap(x + k, X) * W + w} for k in range(1, X)] + [
        {"expert": x * W + wrap(w + k, W)} for k in range(1, W)]


def barrier_plane(X, Z, C, x, z, c):
    sem = pltpu.get_barrier_semaphore()
    targets = plane_peers(X, Z, C, x, z, c)
    for t in targets:
        pl.semaphore_signal(sem, inc=1, device_id=t, device_id_type=MESH)
    pl.semaphore_wait(sem, len(targets))


def two_stage(X, Z, C, x, z, c):
    W = Z * C
    w = z * C + c
    return W, w


def stage_x(X, Z, C, src_of, dst_of, own_sem, send_sem, recv_sem):
    x, z, c = coordinates(X, Z, C)
    W, w = two_stage(X, Z, C, x, z, c)
    own = pltpu.make_async_copy(src_of(x), dst_of(x), own_sem)
    own.start()
    copies = []
    for k in range(1, X):
        cp = pltpu.make_async_remote_copy(
            src_ref=src_of(wrap(x + k, X)), dst_ref=dst_of(x), send_sem=send_sem.at[k - 1], recv_sem=recv_sem.at[k - 1],
            device_id={"expert": wrap(x + k, X) * W + w}, device_id_type=MESH)
        cp.start()
        copies.append(cp)
    return [own] + copies


def stage_w(X, Z, C, src_of, dst_of, own_sem, send_sem, recv_sem):
    x, z, c = coordinates(X, Z, C)
    W, w = two_stage(X, Z, C, x, z, c)
    own = pltpu.make_async_copy(src_of(w), dst_of(w), own_sem)
    own.start()
    copies = []
    for k in range(1, W):
        cp = pltpu.make_async_remote_copy(
            src_ref=src_of(wrap(w + k, W)), dst_ref=dst_of(w), send_sem=send_sem.at[k - 1], recv_sem=recv_sem.at[k - 1],
            device_id={"expert": x * W + wrap(w + k, W)}, device_id_type=MESH)
        cp.start()
        copies.append(cp)
    return [own] + copies


def wait_recvs(copies):
    copies[0].wait()
    for cp in copies[1:]:
        cp.wait_recv()


def wait_sends(copies):
    for cp in copies[1:]:
        cp.wait_send()


def gather_kernel(X, Z, C, tok_ref, cold_ref, wg_ref, wu_ref, wd_ref, out_ref, cold_out, pg_ref, pu_ref, pd_ref,
                  cold_mid, own_sem, c1_send, c1_recv, c2_send, c2_recv, w_send, w_recv, sx_send, sx_recv, sp_send, sp_recv, sm_send, sm_recv):
    x, z, c = coordinates(X, Z, C)
    zp, zm = Z // 2, (Z - 1) // 2
    dirn = 1 - 2 * (c % 2)
    barrier_plane(X, Z, C, x, z, c)
    own = pltpu.make_async_copy(tok_ref, out_ref.at[z, x], own_sem.at[0])
    own.start()
    xcopies = []
    for k in range(1, X):
        cp = pltpu.make_async_remote_copy(
            src_ref=tok_ref, dst_ref=out_ref.at[z, x], send_sem=sx_send.at[k - 1], recv_sem=sx_recv.at[k - 1],
            device_id=device(X, Z, C, x + k, z, c), device_id_type=MESH)
        cp.start()
        xcopies.append(cp)
    cold1 = stage_x(X, Z, C, lambda i: cold_ref.at[i], lambda i: cold_mid.at[:, i], own_sem.at[1], c1_send, c1_recv)
    own.wait()
    for cp in xcopies:
        cp.wait_recv()

    H = ring_pieces(X)
    part = X // H

    def ring_copy(blk, h, send_sem, recv_sem, target):
        piece = out_ref.at[blk, pl.ds(h * part, part)]
        return pltpu.make_async_remote_copy(
            src_ref=piece, dst_ref=piece, send_sem=send_sem, recv_sem=recv_sem,
            device_id=device(X, Z, C, x, target, c), device_id_type=MESH)

    plus, minus = [], []
    for s in range(max(zp, zm)):
        if s < zp:
            blk = wrap(z - s * dirn, Z)
            step = []
            for h in range(H):
                if s >= 1:
                    plus[s - 1][h].wait_recv()
                cp = ring_copy(blk, h, sp_send.at[s * H + h], sp_recv.at[s * H + h], z + dirn)
                cp.start()
                step.append(cp)
            plus.append(step)
        if s < zm:
            blk = wrap(z + s * dirn, Z)
            step = []
            for h in range(H):
                if s >= 1:
                    minus[s - 1][h].wait_recv()
                cp = ring_copy(blk, h, sm_send.at[s * H + h], sm_recv.at[s * H + h], z - dirn)
                cp.start()
                step.append(cp)
            minus.append(step)
        if s == 0:
            wait_recvs(cold1)
            cold2 = stage_w(X, Z, C, lambda i: cold_mid.at[i], lambda i: cold_out.at[i], own_sem.at[2], c2_send, c2_recv)
            wcopies = []
            if C > 1:
                for j, (src, dst) in enumerate(((wg_ref, pg_ref), (wu_ref, pu_ref), (wd_ref, pd_ref))):
                    cp = pltpu.make_async_remote_copy(
                        src_ref=src, dst_ref=dst, send_sem=w_send.at[j], recv_sem=w_recv.at[j],
                        device_id=device(X, Z, C, x, z, c + 1), device_id_type=MESH)
                    cp.start()
                    wcopies.append(cp)
    for step in plus[-1:] + minus[-1:]:
        for cp in step:
            cp.wait_recv()
    for cp in xcopies + [cp for step in plus + minus for cp in step]:
        cp.wait_send()
    wait_recvs(cold2)
    wait_sends(cold1)
    wait_sends(cold2)
    for cp in wcopies:
        cp.wait_recv()
        cp.wait_send()


def scatter_kernel(X, Z, C, o_ref, cold_ref, out_ref, cold_out, cold_mid, own_sem, c1_send, c1_recv, c2_send, c2_recv, plus_buf, plus_send, minus_buf, minus_send, xbuf, xsend,
                   sp_send, sp_recv, sm_send, sm_recv, sx_send, sx_recv):
    x, z, c = coordinates(X, Z, C)
    zp, zm = Z // 2, (Z - 1) // 2
    dirn = 1 - 2 * (c % 2)
    barrier_plane(X, Z, C, x, z, c)

    def chip_sum(blk):
        return o_ref[blk].astype(jnp.float32)

    H = ring_pieces(X)
    part = X // H

    def ring_step(chain, buf, send_buf, send_sem, recv_sem, s, blk, target):
        step = []
        for h in range(H):
            rows = pl.ds(h * part, part)
            val = o_ref[blk, rows].astype(jnp.float32)
            if s >= 1:
                chain[s - 1][h].wait_recv()
                val = val + buf[s - 1, rows].astype(jnp.float32)
            send_buf[s, rows] = val.astype(jnp.bfloat16)
            cp = pltpu.make_async_remote_copy(
                src_ref=send_buf.at[s, rows], dst_ref=buf.at[s, rows], send_sem=send_sem.at[s * H + h],
                recv_sem=recv_sem.at[s * H + h], device_id=device(X, Z, C, x, target, c), device_id_type=MESH)
            cp.start()
            step.append(cp)
        chain.append(step)

    plus, minus = [], []
    for s in range(max(zp, zm)):
        if s < zp:
            ring_step(plus, plus_buf, plus_send, sp_send, sp_recv, s, wrap(z + (zp - s) * dirn, Z), z + dirn)
        if s < zm:
            ring_step(minus, minus_buf, minus_send, sm_send, sm_recv, s, wrap(z - (zm - s) * dirn, Z), z - dirn)
        if s == 0:
            cold1 = stage_w(X, Z, C, lambda i: cold_ref.at[i], lambda i: cold_mid.at[i], own_sem.at[0], c2_send, c2_recv)
    wait_recvs(cold1)
    cold2 = stage_x(X, Z, C, lambda i: cold_mid.at[:, i], lambda i: cold_out.at[i], own_sem.at[1], c1_send, c1_recv)
    total = chip_sum(z)
    if zp:
        for cp in plus[zp - 1]:
            cp.wait_recv()
        total = total + plus_buf[zp - 1].astype(jnp.float32)
    if zm:
        for cp in minus[zm - 1]:
            cp.wait_recv()
        total = total + minus_buf[zm - 1].astype(jnp.float32)
    xsend[...] = total.astype(jnp.bfloat16)
    xcopies = []
    for k in range(1, X):
        cp = pltpu.make_async_remote_copy(
            src_ref=xsend.at[(x + k) % X], dst_ref=xbuf.at[k - 1], send_sem=sx_send.at[k - 1], recv_sem=sx_recv.at[k - 1],
            device_id=device(X, Z, C, x + k, z, c), device_id_type=MESH)
        cp.start()
        xcopies.append(cp)
    result = xsend[x].astype(jnp.float32)
    for k, cp in enumerate(xcopies):
        cp.wait_recv()
        result = result + xbuf[k].astype(jnp.float32)
    out_ref[...] = result.astype(out_ref.dtype)
    for cp in [cp for step in plus + minus for cp in step] + xcopies:
        cp.wait_send()
    wait_recvs(cold2)
    wait_sends(cold1)
    wait_sends(cold2)


def hot_gather(X, Z, C, tokens, outgoing, w_gate, w_up, w_down):
    R, D = tokens.shape
    zp, zm = Z // 2, (Z - 1) // 2
    W = Z * C
    n, S, _ = outgoing.shape
    outgoing = outgoing.reshape(X, W, S, D)
    dma = pltpu.SemaphoreType.DMA
    vmem = pl.BlockSpec(memory_space=pltpu.VMEM)
    anywhere = pl.BlockSpec(memory_space=pl.ANY)
    return pl.pallas_call(
        functools.partial(gather_kernel, X, Z, C),
        out_shape=(
            jax.ShapeDtypeStruct((Z, X, R, D), tokens.dtype), jax.ShapeDtypeStruct((W, X, S, D), outgoing.dtype),
            jax.ShapeDtypeStruct(w_gate.shape, w_gate.dtype), jax.ShapeDtypeStruct(w_up.shape, w_up.dtype),
            jax.ShapeDtypeStruct(w_down.shape, w_down.dtype),
        ),
        in_specs=[vmem, vmem, anywhere, anywhere, anywhere],
        out_specs=(vmem, vmem, anywhere, anywhere, anywhere),
        scratch_shapes=[
            pltpu.VMEM((W, X, S, D), outgoing.dtype),
            dma((3,)), dma((max(X - 1, 1),)), dma((max(X - 1, 1),)), dma((W - 1,)), dma((W - 1,)), dma((3,)), dma((3,)),
            dma((max(X - 1, 1),)), dma((max(X - 1, 1),)),
            dma((max(zp, 1) * ring_pieces(X),)), dma((max(zp, 1) * ring_pieces(X),)),
            dma((max(zm, 1) * ring_pieces(X),)), dma((max(zm, 1) * ring_pieces(X),)),
        ],
        compiler_params=pltpu.CompilerParams(collective_id=0, has_side_effects=True),
    )(tokens, outgoing, w_gate, w_up, w_down)


def hot_scatter(X, Z, C, answered, cold_answered):
    _, _, R, D = answered.shape
    zp, zm = Z // 2, (Z - 1) // 2
    W, _, S, _ = cold_answered.shape
    dma = pltpu.SemaphoreType.DMA
    bf = answered.dtype
    vmem = pl.BlockSpec(memory_space=pltpu.VMEM)
    return pl.pallas_call(
        functools.partial(scatter_kernel, X, Z, C),
        out_shape=(jax.ShapeDtypeStruct((R, D), bf), jax.ShapeDtypeStruct((X, W, S, D), cold_answered.dtype)),
        in_specs=[vmem, vmem],
        out_specs=(vmem, vmem),
        scratch_shapes=[
            pltpu.VMEM((W, X, S, D), cold_answered.dtype),
            dma((2,)), dma((max(X - 1, 1),)), dma((max(X - 1, 1),)), dma((W - 1,)), dma((W - 1,)),
            pltpu.VMEM((max(zp, 1), X, R, D), bf), pltpu.VMEM((max(zp, 1), X, R, D), bf),
            pltpu.VMEM((max(zm, 1), X, R, D), bf), pltpu.VMEM((max(zm, 1), X, R, D), bf),
            pltpu.VMEM((max(X - 1, 1), R, D), bf), pltpu.VMEM((X, R, D), bf),
            dma((max(zp, 1) * ring_pieces(X),)), dma((max(zp, 1) * ring_pieces(X),)),
            dma((max(zm, 1) * ring_pieces(X),)), dma((max(zm, 1) * ring_pieces(X),)),
            dma((max(X - 1, 1),)), dma((max(X - 1, 1),)),
        ],
        compiler_params=pltpu.CompilerParams(collective_id=1, has_side_effects=True),
    )(answered, cold_answered)


def shards(X, Z, C, tokens, routes, gate_weights, w_gate, w_up, w_down):
    devices = lax.axis_size("expert")
    experts = w_gate.shape[0] * devices
    row_count = routes.shape[0]
    top_count = routes.shape[1]
    model_width = tokens.shape[1]
    slot_count = (row_count * (top_count - 1) + experts - 2) // (experts - 1)
    is_cold = jnp.arange(top_count)[None, :] >= 1
    flat_ids = routes.reshape(-1)
    flat_cold = jnp.broadcast_to(is_cold, routes.shape).reshape(-1)
    expert_iota = jnp.arange(experts, dtype=jnp.int32)
    one_hot = ((flat_ids[:, None] == expert_iota[None, :]) & flat_cold[:, None]).astype(jnp.int32)
    slot_rank = (jnp.sum(jnp.cumsum(one_hot, axis=0) * one_hot, axis=1) - 1).reshape(routes.shape)
    slot_iota = jnp.arange(slot_count, dtype=jnp.int32)
    select = (routes[:, :, None, None] == expert_iota[None, None, :, None]) & (
        slot_rank[:, :, None, None] == slot_iota[None, None, None, :]
    ) & is_cold[:, :, None, None]
    placing = jnp.sum(select.astype(jnp.bfloat16), axis=1)
    outgoing = jnp.einsum(
        "res,rd->esd", placing, tokens, preferred_element_type=jnp.float32
    ).astype(jnp.bfloat16)
    local_gate = w_gate.reshape(w_gate.shape[1:])
    local_up = w_up.reshape(w_up.shape[1:])
    local_down = w_down.reshape(w_down.shape[1:])
    hot_expert = routes[0, 0]
    me = lax.axis_index("expert")
    cores = C
    same_chip = lax.div(me, jnp.int32(cores)) == lax.div(hot_expert, jnp.int32(cores))
    role = jnp.where(me == hot_expert, 0, jnp.where(same_chip, 1, 2))
    gathered, arrived, partner_gate, partner_up, partner_down = hot_gather(X, Z, C, tokens, outgoing, local_gate, local_up, local_down)
    answered = feed_forward(arrived, local_gate, local_up, local_down)

    def hot_ffn(gate_w, up_w, down_w):
        return lambda row_block: feed_forward(row_block.reshape(-1, model_width), gate_w, up_w, down_w).reshape(row_block.shape)

    hot_answer = lax.switch(
        role,
        [hot_ffn(local_gate, local_up, local_down), hot_ffn(partner_gate, partner_up, partner_down), jnp.zeros_like],
        gathered,
    )
    hot_out, returned = hot_scatter(X, Z, C, hot_answer, answered)
    returned = returned.reshape(experts, slot_count, model_width)
    index = jnp.where(is_cold, routes * slot_count + slot_rank, 0)
    picked = returned.reshape(-1, model_width)[index].astype(jnp.float32)
    values = jnp.where(is_cold[:, :, None], picked, hot_out.astype(jnp.float32)[:, None, :])
    combined = jnp.sum(gate_weights[:, :, None] * values, axis=1)
    return combined.astype(jnp.bfloat16)


def solution(mesh):
    X, Z, C = torus_shape(mesh)
    in_specs = (
        P(("dp", "expert"), None),
        P(("dp", "expert"), None),
        P(("dp", "expert"), None),
        P("expert", None, None),
        P("expert", None, None),
        P("expert", None, None),
    )
    out_specs = P(("dp", "expert"), None)
    return jax.shard_map(functools.partial(shards, X, Z, C), mesh=mesh, in_specs=in_specs, out_specs=out_specs, check_vma=False)
```

```python
import functools

import jax
import jax.numpy as jnp
from jax import lax
from jax.experimental import pallas as pl
from jax.experimental.pallas import tpu as pltpu
from jax.sharding import PartitionSpec as P

MESH = pl.DeviceIdType.MESH


def feed_forward(row_block, gate_w, up_w, down_w):
    gate_part = jnp.dot(row_block, gate_w, preferred_element_type=jnp.float32)
    up_part = jnp.dot(row_block, up_w, preferred_element_type=jnp.float32)
    hidden = lax.optimization_barrier((jax.nn.silu(gate_part) * up_part).astype(jnp.bfloat16))
    return jnp.dot(hidden, down_w, preferred_element_type=jnp.float32).astype(jnp.bfloat16)


def torus_shape(mesh):
    n = mesh.shape["expert"]
    try:
        row = mesh.devices.reshape(-1, n)[0]
        xs = {d.coords[0] for d in row}
        zs = {d.coords[2] for d in row}
        X, Z = len(xs), len(zs)
        C = n // (X * Z)
        if X * Z * C != n:
            raise ValueError
    except Exception:
        X, Z, C = 4, 8, 2
        if X * Z * C != n:
            X, Z, C = 1, n // 2, 2
    return X, Z, C


def coordinates(X, Z, C):
    e = lax.axis_index("expert")
    return e // (Z * C), (e // C) % Z, e % C


def ring_pieces(X):
    return 4 if X % 4 == 0 else (2 if X % 2 == 0 else 1)


def wrap(v, n):
    return (v + 4 * n) % n


def device(X, Z, C, x, z, c):
    return {"expert": wrap(x, X) * (Z * C) + wrap(z, Z) * C + wrap(c, C)}


def peers(X, Z, C, x, z, c):
    out = [(x + k, z, c) for k in range(1, X)]
    if Z > 1:
        out.append((x, z + 1, c))
        if Z > 2:
            out.append((x, z - 1, c))
    if C > 1:
        out.append((x, z, c + 1))
    return out


def barrier(X, Z, C, x, z, c):
    sem = pltpu.get_barrier_semaphore()
    targets = peers(X, Z, C, x, z, c)
    for t in targets:
        pl.semaphore_signal(sem, inc=1, device_id=device(X, Z, C, *t), device_id_type=MESH)
    pl.semaphore_wait(sem, len(targets))


def barrier_all(n):
    me = lax.axis_index("expert")
    sem = pltpu.get_barrier_semaphore()

    for k in range(1, n):
        pl.semaphore_signal(sem, inc=1, device_id={"expert": (me + k) % n}, device_id_type=MESH)
    pl.semaphore_wait(sem, n - 1)


def exchange_copy(src_ref, dst_ref, k, send_sem, recv_sem):
    n = src_ref.shape[0]
    me = lax.axis_index("expert")
    target = (me + k) % n
    return pltpu.make_async_remote_copy(
        src_ref=src_ref.at[target], dst_ref=dst_ref.at[me], send_sem=send_sem.at[k - 1], recv_sem=recv_sem.at[k - 1],
        device_id={"expert": target}, device_id_type=MESH)


def exchange(src_ref, dst_ref, own_sem, send_sem, recv_sem):
    n = src_ref.shape[0]
    me = lax.axis_index("expert")
    own = pltpu.make_async_copy(src_ref.at[me], dst_ref.at[me], own_sem)
    own.start()

    for k in range(1, n):
        exchange_copy(src_ref, dst_ref, k, send_sem, recv_sem).start()
    return own


def exchange_wait(src_ref, dst_ref, own, send_sem, recv_sem):
    n = src_ref.shape[0]
    own.wait()

    for k in range(1, n):
        cp = exchange_copy(src_ref, dst_ref, k, send_sem, recv_sem)
        cp.wait_recv()
        cp.wait_send()


def plane_peers(X, Z, C, x, z, c):
    W = Z * C
    w = z * C + c
    return [{"expert": wrap(x + k, X) * W + w} for k in range(1, X)] + [
        {"expert": x * W + wrap(w + k, W)} for k in range(1, W)]


def barrier_plane(X, Z, C, x, z, c):
    sem = pltpu.get_barrier_semaphore()
    targets = plane_peers(X, Z, C, x, z, c)
    for t in targets:
        pl.semaphore_signal(sem, inc=1, device_id=t, device_id_type=MESH)
    pl.semaphore_wait(sem, len(targets))


def two_stage(X, Z, C, x, z, c):
    W = Z * C
    w = z * C + c
    return W, w


def stage_x(X, Z, C, src_of, dst_of, own_sem, send_sem, recv_sem):
    x, z, c = coordinates(X, Z, C)
    W, w = two_stage(X, Z, C, x, z, c)
    own = pltpu.make_async_copy(src_of(x), dst_of(x), own_sem)
    own.start()
    copies = []
    for k in range(1, X):
        cp = pltpu.make_async_remote_copy(
            src_ref=src_of(wrap(x + k, X)), dst_ref=dst_of(x), send_sem=send_sem.at[k - 1], recv_sem=recv_sem.at[k - 1],
            device_id={"expert": wrap(x + k, X) * W + w}, device_id_type=MESH)
        cp.start()
        copies.append(cp)
    return [own] + copies


def stage_w(X, Z, C, src_of, dst_of, own_sem, send_sem, recv_sem):
    x, z, c = coordinates(X, Z, C)
    W, w = two_stage(X, Z, C, x, z, c)
    own = pltpu.make_async_copy(src_of(w), dst_of(w), own_sem)
    own.start()
    copies = []
    for k in range(1, W):
        cp = pltpu.make_async_remote_copy(
            src_ref=src_of(wrap(w + k, W)), dst_ref=dst_of(w), send_sem=send_sem.at[k - 1], recv_sem=recv_sem.at[k - 1],
            device_id={"expert": x * W + wrap(w + k, W)}, device_id_type=MESH)
        cp.start()
        copies.append(cp)
    return [own] + copies


def wait_recvs(copies):
    copies[0].wait()
    for cp in copies[1:]:
        cp.wait_recv()


def wait_sends(copies):
    for cp in copies[1:]:
        cp.wait_send()


def gather_kernel(X, Z, C, tok_ref, cold_ref, wg_ref, wu_ref, wd_ref, out_ref, cold_out, pg_ref, pu_ref, pd_ref,
                  cold_mid, own_sem, c1_send, c1_recv, c2_send, c2_recv, w_send, w_recv, sx_send, sx_recv, sp_send, sp_recv, sm_send, sm_recv):
    x, z, c = coordinates(X, Z, C)
    zp, zm = Z // 2, (Z - 1) // 2
    dirn = 1 - 2 * (c % 2)
    barrier_plane(X, Z, C, x, z, c)
    own = pltpu.make_async_copy(tok_ref, out_ref.at[z, x], own_sem.at[0])
    own.start()
    xcopies = []
    for k in range(1, X):
        cp = pltpu.make_async_remote_copy(
            src_ref=tok_ref, dst_ref=out_ref.at[z, x], send_sem=sx_send.at[k - 1], recv_sem=sx_recv.at[k - 1],
            device_id=device(X, Z, C, x + k, z, c), device_id_type=MESH)
        cp.start()
        xcopies.append(cp)
    cold1 = stage_x(X, Z, C, lambda i: cold_ref.at[i], lambda i: cold_mid.at[:, i], own_sem.at[1], c1_send, c1_recv)
    early = ring_pieces(X) == X
    if not early:
        own.wait()
        for cp in xcopies:
            cp.wait_recv()

    H = ring_pieces(X)
    part = X // H

    def ring_copy(blk, h, send_sem, recv_sem, target):
        piece = out_ref.at[blk, pl.ds(h * part, part)]
        return pltpu.make_async_remote_copy(
            src_ref=piece, dst_ref=piece, send_sem=send_sem, recv_sem=recv_sem,
            device_id=device(X, Z, C, x, target, c), device_id_type=MESH)

    plus, minus = [], []
    for s in range(max(zp, zm)):
        pstep, mstep = [], []
        for h in range(H):
            hh = wrap(x - h, X) if early else h
            if s == 0 and early:
                if h == 0:
                    own.wait()
                else:
                    xcopies[h - 1].wait_recv()
            if s < zp:
                if s >= 1:
                    plus[s - 1][h].wait_recv()
                cp = ring_copy(wrap(z - s * dirn, Z), hh, sp_send.at[s * H + h], sp_recv.at[s * H + h], z + dirn)
                cp.start()
                pstep.append(cp)
            if s < zm:
                if s >= 1:
                    minus[s - 1][h].wait_recv()
                cp = ring_copy(wrap(z + s * dirn, Z), hh, sm_send.at[s * H + h], sm_recv.at[s * H + h], z - dirn)
                cp.start()
                mstep.append(cp)
        if pstep:
            plus.append(pstep)
        if mstep:
            minus.append(mstep)
        if s == 0:
            wait_recvs(cold1)
            cold2 = stage_w(X, Z, C, lambda i: cold_mid.at[i], lambda i: cold_out.at[i], own_sem.at[2], c2_send, c2_recv)
            wcopies = []
            if C > 1:
                for j, (src, dst) in enumerate(((wg_ref, pg_ref), (wu_ref, pu_ref), (wd_ref, pd_ref))):
                    cp = pltpu.make_async_remote_copy(
                        src_ref=src, dst_ref=dst, send_sem=w_send.at[j], recv_sem=w_recv.at[j],
                        device_id=device(X, Z, C, x, z, c + 1), device_id_type=MESH)
                    cp.start()
                    wcopies.append(cp)
    for step in plus[-1:] + minus[-1:]:
        for cp in step:
            cp.wait_recv()
    for cp in xcopies + [cp for step in plus + minus for cp in step]:
        cp.wait_send()
    wait_recvs(cold2)
    wait_sends(cold1)
    wait_sends(cold2)
    for cp in wcopies:
        cp.wait_recv()
        cp.wait_send()


def scatter_kernel(X, Z, C, o_ref, cold_ref, out_ref, cold_out, cold_mid, own_sem, c1_send, c1_recv, c2_send, c2_recv, plus_buf, plus_send, minus_buf, minus_send, xbuf, xsend,
                   sp_send, sp_recv, sm_send, sm_recv, sx_send, sx_recv):
    x, z, c = coordinates(X, Z, C)
    zp, zm = Z // 2, (Z - 1) // 2
    dirn = 1 - 2 * (c % 2)
    barrier_plane(X, Z, C, x, z, c)

    def chip_sum(blk):
        return o_ref[blk].astype(jnp.float32)

    H = ring_pieces(X)
    part = X // H

    def ring_step(chain, buf, send_buf, send_sem, recv_sem, s, blk, target):
        step = []
        for h in range(H):
            rows = pl.ds(h * part, part)
            val = o_ref[blk, rows].astype(jnp.float32)
            if s >= 1:
                chain[s - 1][h].wait_recv()
                val = val + buf[s - 1, rows].astype(jnp.float32)
            send_buf[s, rows] = val.astype(jnp.bfloat16)
            cp = pltpu.make_async_remote_copy(
                src_ref=send_buf.at[s, rows], dst_ref=buf.at[s, rows], send_sem=send_sem.at[s * H + h],
                recv_sem=recv_sem.at[s * H + h], device_id=device(X, Z, C, x, target, c), device_id_type=MESH)
            cp.start()
            step.append(cp)
        chain.append(step)

    plus, minus = [], []
    for s in range(max(zp, zm)):
        if s < zp:
            ring_step(plus, plus_buf, plus_send, sp_send, sp_recv, s, wrap(z + (zp - s) * dirn, Z), z + dirn)
        if s < zm:
            ring_step(minus, minus_buf, minus_send, sm_send, sm_recv, s, wrap(z - (zm - s) * dirn, Z), z - dirn)
        if s == 0:
            cold1 = stage_w(X, Z, C, lambda i: cold_ref.at[i], lambda i: cold_mid.at[i], own_sem.at[0], c2_send, c2_recv)
    wait_recvs(cold1)
    cold2 = stage_x(X, Z, C, lambda i: cold_mid.at[:, i], lambda i: cold_out.at[i], own_sem.at[1], c1_send, c1_recv)
    total = chip_sum(z)
    if zp:
        for cp in plus[zp - 1]:
            cp.wait_recv()
        total = total + plus_buf[zp - 1].astype(jnp.float32)
    if zm:
        for cp in minus[zm - 1]:
            cp.wait_recv()
        total = total + minus_buf[zm - 1].astype(jnp.float32)
    xsend[...] = total.astype(jnp.bfloat16)
    xcopies = []
    for k in range(1, X):
        cp = pltpu.make_async_remote_copy(
            src_ref=xsend.at[(x + k) % X], dst_ref=xbuf.at[k - 1], send_sem=sx_send.at[k - 1], recv_sem=sx_recv.at[k - 1],
            device_id=device(X, Z, C, x + k, z, c), device_id_type=MESH)
        cp.start()
        xcopies.append(cp)
    result = xsend[x].astype(jnp.float32)
    for k, cp in enumerate(xcopies):
        cp.wait_recv()
        result = result + xbuf[k].astype(jnp.float32)
    out_ref[...] = result.astype(out_ref.dtype)
    for cp in [cp for step in plus + minus for cp in step] + xcopies:
        cp.wait_send()
    wait_recvs(cold2)
    wait_sends(cold1)
    wait_sends(cold2)


def hot_gather(X, Z, C, tokens, outgoing, w_gate, w_up, w_down):
    R, D = tokens.shape
    zp, zm = Z // 2, (Z - 1) // 2
    W = Z * C
    n, S, _ = outgoing.shape
    outgoing = outgoing.reshape(X, W, S, D)
    dma = pltpu.SemaphoreType.DMA
    vmem = pl.BlockSpec(memory_space=pltpu.VMEM)
    anywhere = pl.BlockSpec(memory_space=pl.ANY)
    return pl.pallas_call(
        functools.partial(gather_kernel, X, Z, C),
        out_shape=(
            jax.ShapeDtypeStruct((Z, X, R, D), tokens.dtype), jax.ShapeDtypeStruct((W, X, S, D), outgoing.dtype),
            jax.ShapeDtypeStruct(w_gate.shape, w_gate.dtype), jax.ShapeDtypeStruct(w_up.shape, w_up.dtype),
            jax.ShapeDtypeStruct(w_down.shape, w_down.dtype),
        ),
        in_specs=[vmem, vmem, anywhere, anywhere, anywhere],
        out_specs=(vmem, vmem, anywhere, anywhere, anywhere),
        scratch_shapes=[
            pltpu.VMEM((W, X, S, D), outgoing.dtype),
            dma((3,)), dma((max(X - 1, 1),)), dma((max(X - 1, 1),)), dma((W - 1,)), dma((W - 1,)), dma((3,)), dma((3,)),
            dma((max(X - 1, 1),)), dma((max(X - 1, 1),)),
            dma((max(zp, 1) * ring_pieces(X),)), dma((max(zp, 1) * ring_pieces(X),)),
            dma((max(zm, 1) * ring_pieces(X),)), dma((max(zm, 1) * ring_pieces(X),)),
        ],
        compiler_params=pltpu.CompilerParams(collective_id=0, has_side_effects=True),
    )(tokens, outgoing, w_gate, w_up, w_down)


def hot_scatter(X, Z, C, answered, cold_answered):
    _, _, R, D = answered.shape
    zp, zm = Z // 2, (Z - 1) // 2
    W, _, S, _ = cold_answered.shape
    dma = pltpu.SemaphoreType.DMA
    bf = answered.dtype
    vmem = pl.BlockSpec(memory_space=pltpu.VMEM)
    return pl.pallas_call(
        functools.partial(scatter_kernel, X, Z, C),
        out_shape=(jax.ShapeDtypeStruct((R, D), bf), jax.ShapeDtypeStruct((X, W, S, D), cold_answered.dtype)),
        in_specs=[vmem, vmem],
        out_specs=(vmem, vmem),
        scratch_shapes=[
            pltpu.VMEM((W, X, S, D), cold_answered.dtype),
            dma((2,)), dma((max(X - 1, 1),)), dma((max(X - 1, 1),)), dma((W - 1,)), dma((W - 1,)),
            pltpu.VMEM((max(zp, 1), X, R, D), bf), pltpu.VMEM((max(zp, 1), X, R, D), bf),
            pltpu.VMEM((max(zm, 1), X, R, D), bf), pltpu.VMEM((max(zm, 1), X, R, D), bf),
            pltpu.VMEM((max(X - 1, 1), R, D), bf), pltpu.VMEM((X, R, D), bf),
            dma((max(zp, 1) * ring_pieces(X),)), dma((max(zp, 1) * ring_pieces(X),)),
            dma((max(zm, 1) * ring_pieces(X),)), dma((max(zm, 1) * ring_pieces(X),)),
            dma((max(X - 1, 1),)), dma((max(X - 1, 1),)),
        ],
        compiler_params=pltpu.CompilerParams(collective_id=1, has_side_effects=True),
    )(answered, cold_answered)


def shards(X, Z, C, tokens, routes, gate_weights, w_gate, w_up, w_down):
    devices = lax.axis_size("expert")
    experts = w_gate.shape[0] * devices
    row_count = routes.shape[0]
    top_count = routes.shape[1]
    model_width = tokens.shape[1]
    slot_count = (row_count * (top_count - 1) + experts - 2) // (experts - 1)
    is_cold = jnp.arange(top_count)[None, :] >= 1
    flat_ids = routes.reshape(-1)
    flat_cold = jnp.broadcast_to(is_cold, routes.shape).reshape(-1)
    expert_iota = jnp.arange(experts, dtype=jnp.int32)
    one_hot = ((flat_ids[:, None] == expert_iota[None, :]) & flat_cold[:, None]).astype(jnp.int32)
    slot_rank = (jnp.sum(jnp.cumsum(one_hot, axis=0) * one_hot, axis=1) - 1).reshape(routes.shape)
    slot_iota = jnp.arange(slot_count, dtype=jnp.int32)
    select = (routes[:, :, None, None] == expert_iota[None, None, :, None]) & (
        slot_rank[:, :, None, None] == slot_iota[None, None, None, :]
    ) & is_cold[:, :, None, None]
    placing = jnp.sum(select.astype(jnp.bfloat16), axis=1)
    outgoing = jnp.einsum(
        "res,rd->esd", placing, tokens, preferred_element_type=jnp.float32
    ).astype(jnp.bfloat16)
    local_gate = w_gate.reshape(w_gate.shape[1:])
    local_up = w_up.reshape(w_up.shape[1:])
    local_down = w_down.reshape(w_down.shape[1:])
    hot_expert = routes[0, 0]
    me = lax.axis_index("expert")
    cores = C
    same_chip = lax.div(me, jnp.int32(cores)) == lax.div(hot_expert, jnp.int32(cores))
    role = jnp.where(me == hot_expert, 0, jnp.where(same_chip, 1, 2))
    gathered, arrived, partner_gate, partner_up, partner_down = hot_gather(X, Z, C, tokens, outgoing, local_gate, local_up, local_down)
    answered = feed_forward(arrived, local_gate, local_up, local_down)

    def hot_ffn(gate_w, up_w, down_w):
        return lambda row_block: feed_forward(row_block.reshape(-1, model_width), gate_w, up_w, down_w).reshape(row_block.shape)

    hot_answer = lax.switch(
        role,
        [hot_ffn(local_gate, local_up, local_down), hot_ffn(partner_gate, partner_up, partner_down), jnp.zeros_like],
        gathered,
    )
    hot_out, returned = hot_scatter(X, Z, C, hot_answer, answered)
    returned = returned.reshape(experts, slot_count, model_width)
    index = jnp.where(is_cold, routes * slot_count + slot_rank, 0)
    picked = returned.reshape(-1, model_width)[index].astype(jnp.float32)
    values = jnp.where(is_cold[:, :, None], picked, hot_out.astype(jnp.float32)[:, None, :])
    combined = jnp.sum(gate_weights[:, :, None] * values, axis=1)
    return combined.astype(jnp.bfloat16)


def solution(mesh):
    X, Z, C = torus_shape(mesh)
    in_specs = (
        P(("dp", "expert"), None),
        P(("dp", "expert"), None),
        P(("dp", "expert"), None),
        P("expert", None, None),
        P("expert", None, None),
        P("expert", None, None),
    )
    out_specs = P(("dp", "expert"), None)
    return jax.shard_map(functools.partial(shards, X, Z, C), mesh=mesh, in_specs=in_specs, out_specs=out_specs, check_vma=False)
```

```python
import functools

import jax
import jax.numpy as jnp
from jax import lax
from jax.experimental import pallas as pl
from jax.experimental.pallas import tpu as pltpu
from jax.sharding import PartitionSpec as P

MESH = pl.DeviceIdType.MESH


def feed_forward(row_block, gate_w, up_w, down_w):
    gate_part = jnp.dot(row_block, gate_w, preferred_element_type=jnp.float32)
    up_part = jnp.dot(row_block, up_w, preferred_element_type=jnp.float32)
    hidden = lax.optimization_barrier((jax.nn.silu(gate_part) * up_part).astype(jnp.bfloat16))
    return jnp.dot(hidden, down_w, preferred_element_type=jnp.float32).astype(jnp.bfloat16)


def torus_shape(mesh):
    n = mesh.shape["expert"]
    try:
        row = mesh.devices.reshape(-1, n)[0]
        xs = {d.coords[0] for d in row}
        zs = {d.coords[2] for d in row}
        X, Z = len(xs), len(zs)
        C = n // (X * Z)
        if X * Z * C != n:
            raise ValueError
    except Exception:
        X, Z, C = 4, 8, 2
        if X * Z * C != n:
            X, Z, C = 1, n // 2, 2
    return X, Z, C


def coordinates(X, Z, C):
    e = lax.axis_index("expert")
    return e // (Z * C), (e // C) % Z, e % C


def ring_pieces(X):
    return 4 if X % 4 == 0 else (2 if X % 2 == 0 else 1)


def wrap(v, n):
    return (v + 4 * n) % n


def device(X, Z, C, x, z, c):
    return {"expert": wrap(x, X) * (Z * C) + wrap(z, Z) * C + wrap(c, C)}


def peers(X, Z, C, x, z, c):
    out = [(x + k, z, c) for k in range(1, X)]
    if Z > 1:
        out.append((x, z + 1, c))
        if Z > 2:
            out.append((x, z - 1, c))
    if C > 1:
        out.append((x, z, c + 1))
    return out


def barrier(X, Z, C, x, z, c):
    sem = pltpu.get_barrier_semaphore()
    targets = peers(X, Z, C, x, z, c)
    for t in targets:
        pl.semaphore_signal(sem, inc=1, device_id=device(X, Z, C, *t), device_id_type=MESH)
    pl.semaphore_wait(sem, len(targets))


def barrier_all(n):
    me = lax.axis_index("expert")
    sem = pltpu.get_barrier_semaphore()

    for k in range(1, n):
        pl.semaphore_signal(sem, inc=1, device_id={"expert": (me + k) % n}, device_id_type=MESH)
    pl.semaphore_wait(sem, n - 1)


def exchange_copy(src_ref, dst_ref, k, send_sem, recv_sem):
    n = src_ref.shape[0]
    me = lax.axis_index("expert")
    target = (me + k) % n
    return pltpu.make_async_remote_copy(
        src_ref=src_ref.at[target], dst_ref=dst_ref.at[me], send_sem=send_sem.at[k - 1], recv_sem=recv_sem.at[k - 1],
        device_id={"expert": target}, device_id_type=MESH)


def exchange(src_ref, dst_ref, own_sem, send_sem, recv_sem):
    n = src_ref.shape[0]
    me = lax.axis_index("expert")
    own = pltpu.make_async_copy(src_ref.at[me], dst_ref.at[me], own_sem)
    own.start()

    for k in range(1, n):
        exchange_copy(src_ref, dst_ref, k, send_sem, recv_sem).start()
    return own


def exchange_wait(src_ref, dst_ref, own, send_sem, recv_sem):
    n = src_ref.shape[0]
    own.wait()

    for k in range(1, n):
        cp = exchange_copy(src_ref, dst_ref, k, send_sem, recv_sem)
        cp.wait_recv()
        cp.wait_send()


def plane_peers(X, Z, C, x, z, c):
    W = Z * C
    w = z * C + c
    return [{"expert": wrap(x + k, X) * W + w} for k in range(1, X)] + [
        {"expert": x * W + wrap(w + k, W)} for k in range(1, W)]


def barrier_plane(X, Z, C, x, z, c):
    sem = pltpu.get_barrier_semaphore()
    targets = plane_peers(X, Z, C, x, z, c)
    for t in targets:
        pl.semaphore_signal(sem, inc=1, device_id=t, device_id_type=MESH)
    pl.semaphore_wait(sem, len(targets))


def two_stage(X, Z, C, x, z, c):
    W = Z * C
    w = z * C + c
    return W, w


def stage_x(X, Z, C, src_of, dst_of, own_sem, send_sem, recv_sem):
    x, z, c = coordinates(X, Z, C)
    W, w = two_stage(X, Z, C, x, z, c)
    own = pltpu.make_async_copy(src_of(x), dst_of(x), own_sem)
    own.start()
    copies = []
    for k in range(1, X):
        cp = pltpu.make_async_remote_copy(
            src_ref=src_of(wrap(x + k, X)), dst_ref=dst_of(x), send_sem=send_sem.at[k - 1], recv_sem=recv_sem.at[k - 1],
            device_id={"expert": wrap(x + k, X) * W + w}, device_id_type=MESH)
        cp.start()
        copies.append(cp)
    return [own] + copies


def stage_w(X, Z, C, src_of, dst_of, own_sem, send_sem, recv_sem):
    x, z, c = coordinates(X, Z, C)
    W, w = two_stage(X, Z, C, x, z, c)
    own = pltpu.make_async_copy(src_of(w), dst_of(w), own_sem)
    own.start()
    copies = []
    for k in range(1, W):
        cp = pltpu.make_async_remote_copy(
            src_ref=src_of(wrap(w + k, W)), dst_ref=dst_of(w), send_sem=send_sem.at[k - 1], recv_sem=recv_sem.at[k - 1],
            device_id={"expert": x * W + wrap(w + k, W)}, device_id_type=MESH)
        cp.start()
        copies.append(cp)
    return [own] + copies


def wait_recvs(copies):
    copies[0].wait()
    for cp in copies[1:]:
        cp.wait_recv()


def wait_sends(copies):
    for cp in copies[1:]:
        cp.wait_send()


def gather_kernel(X, Z, C, tok_ref, cold_ref, wg_ref, wu_ref, wd_ref, out_ref, cold_out, pg_ref, pu_ref, pd_ref,
                  cold_mid, own_sem, c1_send, c1_recv, c2_send, c2_recv, w_send, w_recv, sx_send, sx_recv, sp_send, sp_recv, sm_send, sm_recv):
    x, z, c = coordinates(X, Z, C)
    zp, zm = Z // 2, (Z - 1) // 2
    dirn = 1 - 2 * (c % 2)
    barrier_plane(X, Z, C, x, z, c)
    own = pltpu.make_async_copy(tok_ref, out_ref.at[z, x], own_sem.at[0])
    own.start()
    xcopies = []
    for k in range(1, X):
        cp = pltpu.make_async_remote_copy(
            src_ref=tok_ref, dst_ref=out_ref.at[z, x], send_sem=sx_send.at[k - 1], recv_sem=sx_recv.at[k - 1],
            device_id=device(X, Z, C, x + k, z, c), device_id_type=MESH)
        cp.start()
        xcopies.append(cp)
    cold1 = stage_x(X, Z, C, lambda i: cold_ref.at[i], lambda i: cold_mid.at[:, i], own_sem.at[1], c1_send, c1_recv)
    early = ring_pieces(X) == X
    if not early:
        own.wait()
        for cp in xcopies:
            cp.wait_recv()

    H = ring_pieces(X)
    part = X // H

    def ring_copy(blk, h, send_sem, recv_sem, target):
        piece = out_ref.at[blk, pl.ds(h * part, part)]
        return pltpu.make_async_remote_copy(
            src_ref=piece, dst_ref=piece, send_sem=send_sem, recv_sem=recv_sem,
            device_id=device(X, Z, C, x, target, c), device_id_type=MESH)

    plus, minus = [], []
    for s in range(max(zp, zm)):
        pstep, mstep = [], []
        for h in range(H):
            hh = wrap(x - h, X) if early else h
            if s == 0 and early:
                if h == 0:
                    own.wait()
                else:
                    xcopies[h - 1].wait_recv()
            if s < zp:
                if s >= 1:
                    plus[s - 1][h].wait_recv()
                cp = ring_copy(wrap(z - s * dirn, Z), hh, sp_send.at[s * H + h], sp_recv.at[s * H + h], z + dirn)
                cp.start()
                pstep.append(cp)
            if s < zm:
                if s >= 1:
                    minus[s - 1][h].wait_recv()
                cp = ring_copy(wrap(z + s * dirn, Z), hh, sm_send.at[s * H + h], sm_recv.at[s * H + h], z - dirn)
                cp.start()
                mstep.append(cp)
        if pstep:
            plus.append(pstep)
        if mstep:
            minus.append(mstep)
        if s == 0:
            wait_recvs(cold1)
            cold2 = stage_w(X, Z, C, lambda i: cold_mid.at[i], lambda i: cold_out.at[i], own_sem.at[2], c2_send, c2_recv)
            wcopies = []
            if C > 1:
                for j, (src, dst) in enumerate(((wg_ref, pg_ref), (wu_ref, pu_ref), (wd_ref, pd_ref))):
                    cp = pltpu.make_async_remote_copy(
                        src_ref=src, dst_ref=dst, send_sem=w_send.at[j], recv_sem=w_recv.at[j],
                        device_id=device(X, Z, C, x, z, c + 1), device_id_type=MESH)
                    cp.start()
                    wcopies.append(cp)
    for step in plus[-1:] + minus[-1:]:
        for cp in step:
            cp.wait_recv()
    for cp in xcopies + [cp for step in plus + minus for cp in step]:
        cp.wait_send()
    wait_recvs(cold2)
    wait_sends(cold1)
    wait_sends(cold2)
    for cp in wcopies:
        cp.wait_recv()
        cp.wait_send()


def scatter_kernel(X, Z, C, o_ref, cold_ref, out_ref, cold_out, cold_mid, own_sem, c1_send, c1_recv, c2_send, c2_recv, plus_buf, plus_send, minus_buf, minus_send, xbuf, xsend,
                   sp_send, sp_recv, sm_send, sm_recv, sx_send, sx_recv):
    x, z, c = coordinates(X, Z, C)
    zp, zm = Z // 2, (Z - 1) // 2
    dirn = 1 - 2 * (c % 2)
    barrier_plane(X, Z, C, x, z, c)

    def chip_sum(blk):
        return o_ref[blk].astype(jnp.float32)

    H = ring_pieces(X)
    part = X // H

    def ring_step(chain, buf, send_buf, send_sem, recv_sem, s, blk, target):
        step = []
        for h in range(H):
            rows = pl.ds(h * part, part)
            val = o_ref[blk, rows].astype(jnp.float32)
            if s >= 1:
                chain[s - 1][h].wait_recv()
                val = val + buf[s - 1, rows].astype(jnp.float32)
            send_buf[s, rows] = val.astype(jnp.bfloat16)
            cp = pltpu.make_async_remote_copy(
                src_ref=send_buf.at[s, rows], dst_ref=buf.at[s, rows], send_sem=send_sem.at[s * H + h],
                recv_sem=recv_sem.at[s * H + h], device_id=device(X, Z, C, x, target, c), device_id_type=MESH)
            cp.start()
            step.append(cp)
        chain.append(step)

    plus, minus = [], []
    for s in range(max(zp, zm)):
        if s < zp:
            ring_step(plus, plus_buf, plus_send, sp_send, sp_recv, s, wrap(z + (zp - s) * dirn, Z), z + dirn)
        if s < zm:
            ring_step(minus, minus_buf, minus_send, sm_send, sm_recv, s, wrap(z - (zm - s) * dirn, Z), z - dirn)
        if s == 0:
            cold1 = stage_w(X, Z, C, lambda i: cold_ref.at[i], lambda i: cold_mid.at[i], own_sem.at[0], c2_send, c2_recv)
    wait_recvs(cold1)
    cold2 = stage_x(X, Z, C, lambda i: cold_mid.at[:, i], lambda i: cold_out.at[i], own_sem.at[1], c1_send, c1_recv)
    xcopies = []
    for h in range(H):
        rows = pl.ds(h * part, part)
        piece = o_ref[z, rows].astype(jnp.float32)
        if zp:
            plus[zp - 1][h].wait_recv()
            piece = piece + plus_buf[zp - 1, rows].astype(jnp.float32)
        if zm:
            minus[zm - 1][h].wait_recv()
            piece = piece + minus_buf[zm - 1, rows].astype(jnp.float32)
        xsend[rows] = piece.astype(jnp.bfloat16)
        if part == 1:
            k = wrap(h - x, X)

            @pl.when(k != 0)
            def _():
                pltpu.make_async_remote_copy(
                    src_ref=xsend.at[h], dst_ref=xbuf.at[k - 1], send_sem=sx_send.at[k - 1], recv_sem=sx_recv.at[k - 1],
                    device_id=device(X, Z, C, h, z, c), device_id_type=MESH).start()
    for k in range(1, X):
        cp = pltpu.make_async_remote_copy(
            src_ref=xsend.at[(x + k) % X], dst_ref=xbuf.at[k - 1], send_sem=sx_send.at[k - 1], recv_sem=sx_recv.at[k - 1],
            device_id=device(X, Z, C, x + k, z, c), device_id_type=MESH)
        if part != 1:
            cp.start()
        xcopies.append(cp)
    result = xsend[x].astype(jnp.float32)
    for k, cp in enumerate(xcopies):
        cp.wait_recv()
        result = result + xbuf[k].astype(jnp.float32)
    out_ref[...] = result.astype(out_ref.dtype)
    for cp in [cp for step in plus + minus for cp in step] + xcopies:
        cp.wait_send()
    wait_recvs(cold2)
    wait_sends(cold1)
    wait_sends(cold2)


def hot_gather(X, Z, C, tokens, outgoing, w_gate, w_up, w_down):
    R, D = tokens.shape
    zp, zm = Z // 2, (Z - 1) // 2
    W = Z * C
    n, S, _ = outgoing.shape
    outgoing = outgoing.reshape(X, W, S, D)
    dma = pltpu.SemaphoreType.DMA
    vmem = pl.BlockSpec(memory_space=pltpu.VMEM)
    anywhere = pl.BlockSpec(memory_space=pl.ANY)
    return pl.pallas_call(
        functools.partial(gather_kernel, X, Z, C),
        out_shape=(
            jax.ShapeDtypeStruct((Z, X, R, D), tokens.dtype), jax.ShapeDtypeStruct((W, X, S, D), outgoing.dtype),
            jax.ShapeDtypeStruct(w_gate.shape, w_gate.dtype), jax.ShapeDtypeStruct(w_up.shape, w_up.dtype),
            jax.ShapeDtypeStruct(w_down.shape, w_down.dtype),
        ),
        in_specs=[vmem, vmem, anywhere, anywhere, anywhere],
        out_specs=(vmem, vmem, anywhere, anywhere, anywhere),
        scratch_shapes=[
            pltpu.VMEM((W, X, S, D), outgoing.dtype),
            dma((3,)), dma((max(X - 1, 1),)), dma((max(X - 1, 1),)), dma((W - 1,)), dma((W - 1,)), dma((3,)), dma((3,)),
            dma((max(X - 1, 1),)), dma((max(X - 1, 1),)),
            dma((max(zp, 1) * ring_pieces(X),)), dma((max(zp, 1) * ring_pieces(X),)),
            dma((max(zm, 1) * ring_pieces(X),)), dma((max(zm, 1) * ring_pieces(X),)),
        ],
        compiler_params=pltpu.CompilerParams(collective_id=0, has_side_effects=True),
    )(tokens, outgoing, w_gate, w_up, w_down)


def hot_scatter(X, Z, C, answered, cold_answered):
    _, _, R, D = answered.shape
    zp, zm = Z // 2, (Z - 1) // 2
    W, _, S, _ = cold_answered.shape
    dma = pltpu.SemaphoreType.DMA
    bf = answered.dtype
    vmem = pl.BlockSpec(memory_space=pltpu.VMEM)
    return pl.pallas_call(
        functools.partial(scatter_kernel, X, Z, C),
        out_shape=(jax.ShapeDtypeStruct((R, D), bf), jax.ShapeDtypeStruct((X, W, S, D), cold_answered.dtype)),
        in_specs=[vmem, vmem],
        out_specs=(vmem, vmem),
        scratch_shapes=[
            pltpu.VMEM((W, X, S, D), cold_answered.dtype),
            dma((2,)), dma((max(X - 1, 1),)), dma((max(X - 1, 1),)), dma((W - 1,)), dma((W - 1,)),
            pltpu.VMEM((max(zp, 1), X, R, D), bf), pltpu.VMEM((max(zp, 1), X, R, D), bf),
            pltpu.VMEM((max(zm, 1), X, R, D), bf), pltpu.VMEM((max(zm, 1), X, R, D), bf),
            pltpu.VMEM((max(X - 1, 1), R, D), bf), pltpu.VMEM((X, R, D), bf),
            dma((max(zp, 1) * ring_pieces(X),)), dma((max(zp, 1) * ring_pieces(X),)),
            dma((max(zm, 1) * ring_pieces(X),)), dma((max(zm, 1) * ring_pieces(X),)),
            dma((max(X - 1, 1),)), dma((max(X - 1, 1),)),
        ],
        compiler_params=pltpu.CompilerParams(collective_id=1, has_side_effects=True),
    )(answered, cold_answered)


def shards(X, Z, C, tokens, routes, gate_weights, w_gate, w_up, w_down):
    devices = lax.axis_size("expert")
    experts = w_gate.shape[0] * devices
    row_count = routes.shape[0]
    top_count = routes.shape[1]
    model_width = tokens.shape[1]
    slot_count = (row_count * (top_count - 1) + experts - 2) // (experts - 1)
    is_cold = jnp.arange(top_count)[None, :] >= 1
    flat_ids = routes.reshape(-1)
    flat_cold = jnp.broadcast_to(is_cold, routes.shape).reshape(-1)
    expert_iota = jnp.arange(experts, dtype=jnp.int32)
    one_hot = ((flat_ids[:, None] == expert_iota[None, :]) & flat_cold[:, None]).astype(jnp.int32)
    slot_rank = (jnp.sum(jnp.cumsum(one_hot, axis=0) * one_hot, axis=1) - 1).reshape(routes.shape)
    slot_iota = jnp.arange(slot_count, dtype=jnp.int32)
    select = (routes[:, :, None, None] == expert_iota[None, None, :, None]) & (
        slot_rank[:, :, None, None] == slot_iota[None, None, None, :]
    ) & is_cold[:, :, None, None]
    placing = jnp.sum(select.astype(jnp.bfloat16), axis=1)
    outgoing = jnp.einsum(
        "res,rd->esd", placing, tokens, preferred_element_type=jnp.float32
    ).astype(jnp.bfloat16)
    local_gate = w_gate.reshape(w_gate.shape[1:])
    local_up = w_up.reshape(w_up.shape[1:])
    local_down = w_down.reshape(w_down.shape[1:])
    hot_expert = routes[0, 0]
    me = lax.axis_index("expert")
    cores = C
    same_chip = lax.div(me, jnp.int32(cores)) == lax.div(hot_expert, jnp.int32(cores))
    role = jnp.where(me == hot_expert, 0, jnp.where(same_chip, 1, 2))
    gathered, arrived, partner_gate, partner_up, partner_down = hot_gather(X, Z, C, tokens, outgoing, local_gate, local_up, local_down)
    answered = feed_forward(arrived, local_gate, local_up, local_down)

    def hot_ffn(gate_w, up_w, down_w):
        return lambda row_block: feed_forward(row_block.reshape(-1, model_width), gate_w, up_w, down_w).reshape(row_block.shape)

    hot_answer = lax.switch(
        role,
        [hot_ffn(local_gate, local_up, local_down), hot_ffn(partner_gate, partner_up, partner_down), jnp.zeros_like],
        gathered,
    )
    hot_out, returned = hot_scatter(X, Z, C, hot_answer, answered)
    returned = returned.reshape(experts, slot_count, model_width)
    index = jnp.where(is_cold, routes * slot_count + slot_rank, 0)
    picked = returned.reshape(-1, model_width)[index].astype(jnp.float32)
    values = jnp.where(is_cold[:, :, None], picked, hot_out.astype(jnp.float32)[:, None, :])
    combined = jnp.sum(gate_weights[:, :, None] * values, axis=1)
    return combined.astype(jnp.bfloat16)


def solution(mesh):
    X, Z, C = torus_shape(mesh)
    in_specs = (
        P(("dp", "expert"), None),
        P(("dp", "expert"), None),
        P(("dp", "expert"), None),
        P("expert", None, None),
        P("expert", None, None),
        P("expert", None, None),
    )
    out_specs = P(("dp", "expert"), None)
    return jax.shard_map(functools.partial(shards, X, Z, C), mesh=mesh, in_specs=in_specs, out_specs=out_specs, check_vma=False)
```

```python
import functools

import jax
import jax.numpy as jnp
from jax import lax
from jax.experimental import pallas as pl
from jax.experimental.pallas import tpu as pltpu
from jax.sharding import PartitionSpec as P

MESH = pl.DeviceIdType.MESH


def feed_forward(row_block, gate_w, up_w, down_w):
    gate_part = jnp.dot(row_block, gate_w, preferred_element_type=jnp.float32)
    up_part = jnp.dot(row_block, up_w, preferred_element_type=jnp.float32)
    hidden = lax.optimization_barrier((jax.nn.silu(gate_part) * up_part).astype(jnp.bfloat16))
    return jnp.dot(hidden, down_w, preferred_element_type=jnp.float32).astype(jnp.bfloat16)


def torus_shape(mesh):
    n = mesh.shape["expert"]
    try:
        row = mesh.devices.reshape(-1, n)[0]
        xs = {d.coords[0] for d in row}
        zs = {d.coords[2] for d in row}
        X, Z = len(xs), len(zs)
        C = n // (X * Z)
        if X * Z * C != n:
            raise ValueError
    except Exception:
        X, Z, C = 4, 8, 2
        if X * Z * C != n:
            X, Z, C = 1, n // 2, 2
    return X, Z, C


def coordinates(X, Z, C):
    e = lax.axis_index("expert")
    return e // (Z * C), (e // C) % Z, e % C


def ring_pieces(X):
    return 4 if X % 4 == 0 else (2 if X % 2 == 0 else 1)


def wrap(v, n):
    return (v + 4 * n) % n


def device(X, Z, C, x, z, c):
    return {"expert": wrap(x, X) * (Z * C) + wrap(z, Z) * C + wrap(c, C)}


def peers(X, Z, C, x, z, c):
    out = [(x + k, z, c) for k in range(1, X)]
    if Z > 1:
        out.append((x, z + 1, c))
        if Z > 2:
            out.append((x, z - 1, c))
    if C > 1:
        out.append((x, z, c + 1))
    return out


def barrier(X, Z, C, x, z, c):
    sem = pltpu.get_barrier_semaphore()
    targets = peers(X, Z, C, x, z, c)
    for t in targets:
        pl.semaphore_signal(sem, inc=1, device_id=device(X, Z, C, *t), device_id_type=MESH)
    pl.semaphore_wait(sem, len(targets))


def barrier_all(n):
    me = lax.axis_index("expert")
    sem = pltpu.get_barrier_semaphore()

    for k in range(1, n):
        pl.semaphore_signal(sem, inc=1, device_id={"expert": (me + k) % n}, device_id_type=MESH)
    pl.semaphore_wait(sem, n - 1)


def exchange_copy(src_ref, dst_ref, k, send_sem, recv_sem):
    n = src_ref.shape[0]
    me = lax.axis_index("expert")
    target = (me + k) % n
    return pltpu.make_async_remote_copy(
        src_ref=src_ref.at[target], dst_ref=dst_ref.at[me], send_sem=send_sem.at[k - 1], recv_sem=recv_sem.at[k - 1],
        device_id={"expert": target}, device_id_type=MESH)


def exchange(src_ref, dst_ref, own_sem, send_sem, recv_sem):
    n = src_ref.shape[0]
    me = lax.axis_index("expert")
    own = pltpu.make_async_copy(src_ref.at[me], dst_ref.at[me], own_sem)
    own.start()

    for k in range(1, n):
        exchange_copy(src_ref, dst_ref, k, send_sem, recv_sem).start()
    return own


def exchange_wait(src_ref, dst_ref, own, send_sem, recv_sem):
    n = src_ref.shape[0]
    own.wait()

    for k in range(1, n):
        cp = exchange_copy(src_ref, dst_ref, k, send_sem, recv_sem)
        cp.wait_recv()
        cp.wait_send()


def plane_peers(X, Z, C, x, z, c):
    W = Z * C
    w = z * C + c
    return [{"expert": wrap(x + k, X) * W + w} for k in range(1, X)] + [
        {"expert": x * W + wrap(w + k, W)} for k in range(1, W)]


def barrier_plane(X, Z, C, x, z, c):
    sem = pltpu.get_barrier_semaphore()
    targets = plane_peers(X, Z, C, x, z, c)
    for t in targets:
        pl.semaphore_signal(sem, inc=1, device_id=t, device_id_type=MESH)
    pl.semaphore_wait(sem, len(targets))


def two_stage(X, Z, C, x, z, c):
    W = Z * C
    w = z * C + c
    return W, w


def stage_x(X, Z, C, src_of, dst_of, own_sem, send_sem, recv_sem):
    x, z, c = coordinates(X, Z, C)
    W, w = two_stage(X, Z, C, x, z, c)
    own = pltpu.make_async_copy(src_of(x), dst_of(x), own_sem)
    own.start()
    copies = []
    for k in range(1, X):
        cp = pltpu.make_async_remote_copy(
            src_ref=src_of(wrap(x + k, X)), dst_ref=dst_of(x), send_sem=send_sem.at[k - 1], recv_sem=recv_sem.at[k - 1],
            device_id={"expert": wrap(x + k, X) * W + w}, device_id_type=MESH)
        cp.start()
        copies.append(cp)
    return [own] + copies


def stage_w(X, Z, C, src_of, dst_of, own_sem, send_sem, recv_sem):
    x, z, c = coordinates(X, Z, C)
    W, w = two_stage(X, Z, C, x, z, c)
    own = pltpu.make_async_copy(src_of(w), dst_of(w), own_sem)
    own.start()
    copies = []
    for k in range(1, W):
        cp = pltpu.make_async_remote_copy(
            src_ref=src_of(wrap(w + k, W)), dst_ref=dst_of(w), send_sem=send_sem.at[k - 1], recv_sem=recv_sem.at[k - 1],
            device_id={"expert": x * W + wrap(w + k, W)}, device_id_type=MESH)
        cp.start()
        copies.append(cp)
    return [own] + copies


def wait_recvs(copies):
    copies[0].wait()
    for cp in copies[1:]:
        cp.wait_recv()


def wait_sends(copies):
    for cp in copies[1:]:
        cp.wait_send()


def gather_kernel(X, Z, C, tok_ref, cold_ref, wg_ref, wu_ref, wd_ref, out_ref, cold_out, pg_ref, pu_ref, pd_ref,
                  cold_mid, own_sem, c1_send, c1_recv, c2_send, c2_recv, w_send, w_recv, sx_send, sx_recv, sp_send, sp_recv, sm_send, sm_recv):
    x, z, c = coordinates(X, Z, C)
    zp, zm = Z // 2, (Z - 1) // 2
    dirn = 1 - 2 * (c % 2)
    barrier_plane(X, Z, C, x, z, c)
    own = pltpu.make_async_copy(tok_ref, out_ref.at[z, x], own_sem.at[0])
    own.start()
    xcopies = []
    for k in range(1, X):
        cp = pltpu.make_async_remote_copy(
            src_ref=tok_ref, dst_ref=out_ref.at[z, x], send_sem=sx_send.at[k - 1], recv_sem=sx_recv.at[k - 1],
            device_id=device(X, Z, C, x + k, z, c), device_id_type=MESH)
        cp.start()
        xcopies.append(cp)
    cold1 = stage_x(X, Z, C, lambda i: cold_ref.at[i], lambda i: cold_mid.at[:, i], own_sem.at[1], c1_send, c1_recv)
    early = ring_pieces(X) == X
    if not early:
        own.wait()
        for cp in xcopies:
            cp.wait_recv()

    H = ring_pieces(X)
    part = X // H

    def ring_copy(blk, h, send_sem, recv_sem, target):
        piece = out_ref.at[blk, pl.ds(h * part, part)]
        return pltpu.make_async_remote_copy(
            src_ref=piece, dst_ref=piece, send_sem=send_sem, recv_sem=recv_sem,
            device_id=device(X, Z, C, x, target, c), device_id_type=MESH)

    plus, minus = [], []
    for s in range(max(zp, zm)):
        pstep, mstep = [], []
        for h in range(H):
            hh = wrap(x - h, X) if early else h
            if s == 0 and early:
                if h == 0:
                    own.wait()
                else:
                    xcopies[h - 1].wait_recv()
            if s < zp:
                if s >= 1:
                    plus[s - 1][h].wait_recv()
                cp = ring_copy(wrap(z - s * dirn, Z), hh, sp_send.at[s * H + h], sp_recv.at[s * H + h], z + dirn)
                cp.start()
                pstep.append(cp)
            if s < zm:
                if s >= 1:
                    minus[s - 1][h].wait_recv()
                cp = ring_copy(wrap(z + s * dirn, Z), hh, sm_send.at[s * H + h], sm_recv.at[s * H + h], z - dirn)
                cp.start()
                mstep.append(cp)
        if pstep:
            plus.append(pstep)
        if mstep:
            minus.append(mstep)
        if s == 0:
            wait_recvs(cold1)
            cold2 = stage_w(X, Z, C, lambda i: cold_mid.at[i], lambda i: cold_out.at[i], own_sem.at[2], c2_send, c2_recv)
            wcopies = []
            if C > 1:
                for j, (src, dst) in enumerate(((wg_ref, pg_ref), (wu_ref, pu_ref), (wd_ref, pd_ref))):
                    cp = pltpu.make_async_remote_copy(
                        src_ref=src, dst_ref=dst, send_sem=w_send.at[j], recv_sem=w_recv.at[j],
                        device_id=device(X, Z, C, x, z, c + 1), device_id_type=MESH)
                    cp.start()
                    wcopies.append(cp)
    for step in plus[-1:] + minus[-1:]:
        for cp in step:
            cp.wait_recv()
    for cp in xcopies + [cp for step in plus + minus for cp in step]:
        cp.wait_send()
    wait_recvs(cold2)
    wait_sends(cold1)
    wait_sends(cold2)
    for cp in wcopies:
        cp.wait_recv()
        cp.wait_send()


def scatter_kernel(X, Z, C, o_ref, cold_ref, out_ref, cold_out, cold_mid, own_sem, c1_send, c1_recv, c2_send, c2_recv, plus_buf, plus_send, minus_buf, minus_send, xbuf, xsend,
                   sp_send, sp_recv, sm_send, sm_recv, sx_send, sx_recv):
    x, z, c = coordinates(X, Z, C)
    zp, zm = Z // 2, (Z - 1) // 2
    dirn = 1 - 2 * (c % 2)
    barrier_plane(X, Z, C, x, z, c)

    def chip_sum(blk):
        return o_ref[blk].astype(jnp.float32)

    H = ring_pieces(X)
    part = X // H

    def ring_step(chain, buf, send_buf, send_sem, recv_sem, s, blk, target):
        step = []
        for h in range(H):
            rows = pl.ds(h * part, part)
            val = o_ref[blk, rows].astype(jnp.float32)
            if s >= 1:
                chain[s - 1][h].wait_recv()
                val = val + buf[s - 1, rows].astype(jnp.float32)
            send_buf[s, rows] = val.astype(jnp.bfloat16)
            cp = pltpu.make_async_remote_copy(
                src_ref=send_buf.at[s, rows], dst_ref=buf.at[s, rows], send_sem=send_sem.at[s * H + h],
                recv_sem=recv_sem.at[s * H + h], device_id=device(X, Z, C, x, target, c), device_id_type=MESH)
            cp.start()
            step.append(cp)
        chain.append(step)

    cold1 = stage_w(X, Z, C, lambda i: cold_ref.at[i], lambda i: cold_mid.at[i], own_sem.at[0], c2_send, c2_recv)
    plus, minus = [], []
    for s in range(max(zp, zm)):
        if s < zp:
            ring_step(plus, plus_buf, plus_send, sp_send, sp_recv, s, wrap(z + (zp - s) * dirn, Z), z + dirn)
        if s < zm:
            ring_step(minus, minus_buf, minus_send, sm_send, sm_recv, s, wrap(z - (zm - s) * dirn, Z), z - dirn)
    wait_recvs(cold1)
    cold2 = stage_x(X, Z, C, lambda i: cold_mid.at[:, i], lambda i: cold_out.at[i], own_sem.at[1], c1_send, c1_recv)
    xcopies = []
    for h in range(H):
        rows = pl.ds(h * part, part)
        piece = o_ref[z, rows].astype(jnp.float32)
        if zp:
            plus[zp - 1][h].wait_recv()
            piece = piece + plus_buf[zp - 1, rows].astype(jnp.float32)
        if zm:
            minus[zm - 1][h].wait_recv()
            piece = piece + minus_buf[zm - 1, rows].astype(jnp.float32)
        xsend[rows] = piece.astype(jnp.bfloat16)
        if part == 1:
            k = wrap(h - x, X)

            @pl.when(k != 0)
            def _():
                pltpu.make_async_remote_copy(
                    src_ref=xsend.at[h], dst_ref=xbuf.at[k - 1], send_sem=sx_send.at[k - 1], recv_sem=sx_recv.at[k - 1],
                    device_id=device(X, Z, C, h, z, c), device_id_type=MESH).start()
    for k in range(1, X):
        cp = pltpu.make_async_remote_copy(
            src_ref=xsend.at[(x + k) % X], dst_ref=xbuf.at[k - 1], send_sem=sx_send.at[k - 1], recv_sem=sx_recv.at[k - 1],
            device_id=device(X, Z, C, x + k, z, c), device_id_type=MESH)
        if part != 1:
            cp.start()
        xcopies.append(cp)
    result = xsend[x].astype(jnp.float32)
    for k, cp in enumerate(xcopies):
        cp.wait_recv()
        result = result + xbuf[k].astype(jnp.float32)
    out_ref[...] = result.astype(out_ref.dtype)
    for cp in [cp for step in plus + minus for cp in step] + xcopies:
        cp.wait_send()
    wait_recvs(cold2)
    wait_sends(cold1)
    wait_sends(cold2)


def hot_gather(X, Z, C, tokens, outgoing, w_gate, w_up, w_down):
    R, D = tokens.shape
    zp, zm = Z // 2, (Z - 1) // 2
    W = Z * C
    n, S, _ = outgoing.shape
    outgoing = outgoing.reshape(X, W, S, D)
    dma = pltpu.SemaphoreType.DMA
    vmem = pl.BlockSpec(memory_space=pltpu.VMEM)
    anywhere = pl.BlockSpec(memory_space=pl.ANY)
    return pl.pallas_call(
        functools.partial(gather_kernel, X, Z, C),
        out_shape=(
            jax.ShapeDtypeStruct((Z, X, R, D), tokens.dtype), jax.ShapeDtypeStruct((W, X, S, D), outgoing.dtype),
            jax.ShapeDtypeStruct(w_gate.shape, w_gate.dtype), jax.ShapeDtypeStruct(w_up.shape, w_up.dtype),
            jax.ShapeDtypeStruct(w_down.shape, w_down.dtype),
        ),
        in_specs=[vmem, vmem, anywhere, anywhere, anywhere],
        out_specs=(vmem, vmem, anywhere, anywhere, anywhere),
        scratch_shapes=[
            pltpu.VMEM((W, X, S, D), outgoing.dtype),
            dma((3,)), dma((max(X - 1, 1),)), dma((max(X - 1, 1),)), dma((W - 1,)), dma((W - 1,)), dma((3,)), dma((3,)),
            dma((max(X - 1, 1),)), dma((max(X - 1, 1),)),
            dma((max(zp, 1) * ring_pieces(X),)), dma((max(zp, 1) * ring_pieces(X),)),
            dma((max(zm, 1) * ring_pieces(X),)), dma((max(zm, 1) * ring_pieces(X),)),
        ],
        compiler_params=pltpu.CompilerParams(collective_id=0, has_side_effects=True),
    )(tokens, outgoing, w_gate, w_up, w_down)


def hot_scatter(X, Z, C, answered, cold_answered):
    _, _, R, D = answered.shape
    zp, zm = Z // 2, (Z - 1) // 2
    W, _, S, _ = cold_answered.shape
    dma = pltpu.SemaphoreType.DMA
    bf = answered.dtype
    vmem = pl.BlockSpec(memory_space=pltpu.VMEM)
    return pl.pallas_call(
        functools.partial(scatter_kernel, X, Z, C),
        out_shape=(jax.ShapeDtypeStruct((R, D), bf), jax.ShapeDtypeStruct((X, W, S, D), cold_answered.dtype)),
        in_specs=[vmem, vmem],
        out_specs=(vmem, vmem),
        scratch_shapes=[
            pltpu.VMEM((W, X, S, D), cold_answered.dtype),
            dma((2,)), dma((max(X - 1, 1),)), dma((max(X - 1, 1),)), dma((W - 1,)), dma((W - 1,)),
            pltpu.VMEM((max(zp, 1), X, R, D), bf), pltpu.VMEM((max(zp, 1), X, R, D), bf),
            pltpu.VMEM((max(zm, 1), X, R, D), bf), pltpu.VMEM((max(zm, 1), X, R, D), bf),
            pltpu.VMEM((max(X - 1, 1), R, D), bf), pltpu.VMEM((X, R, D), bf),
            dma((max(zp, 1) * ring_pieces(X),)), dma((max(zp, 1) * ring_pieces(X),)),
            dma((max(zm, 1) * ring_pieces(X),)), dma((max(zm, 1) * ring_pieces(X),)),
            dma((max(X - 1, 1),)), dma((max(X - 1, 1),)),
        ],
        compiler_params=pltpu.CompilerParams(collective_id=1, has_side_effects=True),
    )(answered, cold_answered)


def shards(X, Z, C, tokens, routes, gate_weights, w_gate, w_up, w_down):
    devices = lax.axis_size("expert")
    experts = w_gate.shape[0] * devices
    row_count = routes.shape[0]
    top_count = routes.shape[1]
    model_width = tokens.shape[1]
    slot_count = (row_count * (top_count - 1) + experts - 2) // (experts - 1)
    is_cold = jnp.arange(top_count)[None, :] >= 1
    flat_ids = routes.reshape(-1)
    flat_cold = jnp.broadcast_to(is_cold, routes.shape).reshape(-1)
    expert_iota = jnp.arange(experts, dtype=jnp.int32)
    one_hot = ((flat_ids[:, None] == expert_iota[None, :]) & flat_cold[:, None]).astype(jnp.int32)
    slot_rank = (jnp.sum(jnp.cumsum(one_hot, axis=0) * one_hot, axis=1) - 1).reshape(routes.shape)
    slot_iota = jnp.arange(slot_count, dtype=jnp.int32)
    select = (routes[:, :, None, None] == expert_iota[None, None, :, None]) & (
        slot_rank[:, :, None, None] == slot_iota[None, None, None, :]
    ) & is_cold[:, :, None, None]
    placing = jnp.sum(select.astype(jnp.bfloat16), axis=1)
    outgoing = jnp.einsum(
        "res,rd->esd", placing, tokens, preferred_element_type=jnp.float32
    ).astype(jnp.bfloat16)
    local_gate = w_gate.reshape(w_gate.shape[1:])
    local_up = w_up.reshape(w_up.shape[1:])
    local_down = w_down.reshape(w_down.shape[1:])
    hot_expert = routes[0, 0]
    me = lax.axis_index("expert")
    cores = C
    same_chip = lax.div(me, jnp.int32(cores)) == lax.div(hot_expert, jnp.int32(cores))
    role = jnp.where(me == hot_expert, 0, jnp.where(same_chip, 1, 2))
    gathered, arrived, partner_gate, partner_up, partner_down = hot_gather(X, Z, C, tokens, outgoing, local_gate, local_up, local_down)
    answered = feed_forward(arrived, local_gate, local_up, local_down)

    def hot_ffn(gate_w, up_w, down_w):
        return lambda row_block: feed_forward(row_block.reshape(-1, model_width), gate_w, up_w, down_w).reshape(row_block.shape)

    hot_answer = lax.switch(
        role,
        [hot_ffn(local_gate, local_up, local_down), hot_ffn(partner_gate, partner_up, partner_down), jnp.zeros_like],
        gathered,
    )
    hot_out, returned = hot_scatter(X, Z, C, hot_answer, answered)
    returned = returned.reshape(experts, slot_count, model_width)
    index = jnp.where(is_cold, routes * slot_count + slot_rank, 0)
    picked = returned.reshape(-1, model_width)[index].astype(jnp.float32)
    values = jnp.where(is_cold[:, :, None], picked, hot_out.astype(jnp.float32)[:, None, :])
    combined = jnp.sum(gate_weights[:, :, None] * values, axis=1)
    return combined.astype(jnp.bfloat16)


def solution(mesh):
    X, Z, C = torus_shape(mesh)
    in_specs = (
        P(("dp", "expert"), None),
        P(("dp", "expert"), None),
        P(("dp", "expert"), None),
        P("expert", None, None),
        P("expert", None, None),
        P("expert", None, None),
    )
    out_specs = P(("dp", "expert"), None)
    return jax.shard_map(functools.partial(shards, X, Z, C), mesh=mesh, in_specs=in_specs, out_specs=out_specs, check_vma=False)
```

```python
import functools

import jax
import jax.numpy as jnp
from jax import lax
from jax.experimental import pallas as pl
from jax.experimental.pallas import tpu as pltpu
from jax.sharding import PartitionSpec as P

MESH = pl.DeviceIdType.MESH


def feed_forward(row_block, gate_w, up_w, down_w):
    gate_part = jnp.dot(row_block, gate_w, preferred_element_type=jnp.float32)
    up_part = jnp.dot(row_block, up_w, preferred_element_type=jnp.float32)
    hidden = lax.optimization_barrier((jax.nn.silu(gate_part) * up_part).astype(jnp.bfloat16))
    return jnp.dot(hidden, down_w, preferred_element_type=jnp.float32).astype(jnp.bfloat16)


def torus_shape(mesh):
    n = mesh.shape["expert"]
    try:
        row = mesh.devices.reshape(-1, n)[0]
        xs = {d.coords[0] for d in row}
        zs = {d.coords[2] for d in row}
        X, Z = len(xs), len(zs)
        C = n // (X * Z)
        if X * Z * C != n:
            raise ValueError
    except Exception:
        X, Z, C = 4, 8, 2
        if X * Z * C != n:
            X, Z, C = 1, n // 2, 2
    return X, Z, C


def coordinates(X, Z, C):
    e = lax.axis_index("expert")
    return e // (Z * C), (e // C) % Z, e % C


def ring_pieces(X):
    return 4 if X % 4 == 0 else (2 if X % 2 == 0 else 1)


def wrap(v, n):
    return (v + 4 * n) % n


def device(X, Z, C, x, z, c):
    return {"expert": wrap(x, X) * (Z * C) + wrap(z, Z) * C + wrap(c, C)}


def peers(X, Z, C, x, z, c):
    out = [(x + k, z, c) for k in range(1, X)]
    if Z > 1:
        out.append((x, z + 1, c))
        if Z > 2:
            out.append((x, z - 1, c))
    if C > 1:
        out.append((x, z, c + 1))
    return out


def barrier(X, Z, C, x, z, c):
    sem = pltpu.get_barrier_semaphore()
    targets = peers(X, Z, C, x, z, c)
    for t in targets:
        pl.semaphore_signal(sem, inc=1, device_id=device(X, Z, C, *t), device_id_type=MESH)
    pl.semaphore_wait(sem, len(targets))


def barrier_all(n):
    me = lax.axis_index("expert")
    sem = pltpu.get_barrier_semaphore()

    for k in range(1, n):
        pl.semaphore_signal(sem, inc=1, device_id={"expert": (me + k) % n}, device_id_type=MESH)
    pl.semaphore_wait(sem, n - 1)


def exchange_copy(src_ref, dst_ref, k, send_sem, recv_sem):
    n = src_ref.shape[0]
    me = lax.axis_index("expert")
    target = (me + k) % n
    return pltpu.make_async_remote_copy(
        src_ref=src_ref.at[target], dst_ref=dst_ref.at[me], send_sem=send_sem.at[k - 1], recv_sem=recv_sem.at[k - 1],
        device_id={"expert": target}, device_id_type=MESH)


def exchange(src_ref, dst_ref, own_sem, send_sem, recv_sem):
    n = src_ref.shape[0]
    me = lax.axis_index("expert")
    own = pltpu.make_async_copy(src_ref.at[me], dst_ref.at[me], own_sem)
    own.start()

    for k in range(1, n):
        exchange_copy(src_ref, dst_ref, k, send_sem, recv_sem).start()
    return own


def exchange_wait(src_ref, dst_ref, own, send_sem, recv_sem):
    n = src_ref.shape[0]
    own.wait()

    for k in range(1, n):
        cp = exchange_copy(src_ref, dst_ref, k, send_sem, recv_sem)
        cp.wait_recv()
        cp.wait_send()


def plane_peers(X, Z, C, x, z, c):
    W = Z * C
    w = z * C + c
    return [{"expert": wrap(x + k, X) * W + w} for k in range(1, X)] + [
        {"expert": x * W + wrap(w + k, W)} for k in range(1, W)]


def barrier_plane(X, Z, C, x, z, c):
    sem = pltpu.get_barrier_semaphore()
    targets = plane_peers(X, Z, C, x, z, c)
    for t in targets:
        pl.semaphore_signal(sem, inc=1, device_id=t, device_id_type=MESH)
    pl.semaphore_wait(sem, len(targets))


def two_stage(X, Z, C, x, z, c):
    W = Z * C
    w = z * C + c
    return W, w


def stage_x(X, Z, C, src_of, dst_of, own_sem, send_sem, recv_sem):
    x, z, c = coordinates(X, Z, C)
    W, w = two_stage(X, Z, C, x, z, c)
    own = pltpu.make_async_copy(src_of(x), dst_of(x), own_sem)
    own.start()
    copies = []
    for k in range(1, X):
        cp = pltpu.make_async_remote_copy(
            src_ref=src_of(wrap(x + k, X)), dst_ref=dst_of(x), send_sem=send_sem.at[k - 1], recv_sem=recv_sem.at[k - 1],
            device_id={"expert": wrap(x + k, X) * W + w}, device_id_type=MESH)
        cp.start()
        copies.append(cp)
    return [own] + copies


def stage_w(X, Z, C, src_of, dst_of, own_sem, send_sem, recv_sem):
    x, z, c = coordinates(X, Z, C)
    W, w = two_stage(X, Z, C, x, z, c)
    own = pltpu.make_async_copy(src_of(w), dst_of(w), own_sem)
    own.start()
    copies = []
    for k in range(1, W):
        cp = pltpu.make_async_remote_copy(
            src_ref=src_of(wrap(w + k, W)), dst_ref=dst_of(w), send_sem=send_sem.at[k - 1], recv_sem=recv_sem.at[k - 1],
            device_id={"expert": x * W + wrap(w + k, W)}, device_id_type=MESH)
        cp.start()
        copies.append(cp)
    return [own] + copies


def wait_recvs(copies):
    copies[0].wait()
    for cp in copies[1:]:
        cp.wait_recv()


def wait_sends(copies):
    for cp in copies[1:]:
        cp.wait_send()


def gather_kernel(X, Z, C, tok_ref, cold_ref, wg_ref, wu_ref, wd_ref, out_ref, cold_out, pg_ref, pu_ref, pd_ref,
                  cold_mid, own_sem, c1_send, c1_recv, c2_send, c2_recv, w_send, w_recv, sx_send, sx_recv, sp_send, sp_recv, sm_send, sm_recv):
    x, z, c = coordinates(X, Z, C)
    zp, zm = Z // 2, (Z - 1) // 2
    dirn = 1 - 2 * (c % 2)
    barrier_plane(X, Z, C, x, z, c)
    own = pltpu.make_async_copy(tok_ref, out_ref.at[z, x], own_sem.at[0])
    own.start()
    xcopies = []
    for k in range(1, X):
        cp = pltpu.make_async_remote_copy(
            src_ref=tok_ref, dst_ref=out_ref.at[z, x], send_sem=sx_send.at[k - 1], recv_sem=sx_recv.at[k - 1],
            device_id=device(X, Z, C, x + k, z, c), device_id_type=MESH)
        cp.start()
        xcopies.append(cp)
    cold1 = stage_x(X, Z, C, lambda i: cold_ref.at[i], lambda i: cold_mid.at[:, i], own_sem.at[1], c1_send, c1_recv)
    early = ring_pieces(X) == X
    if not early:
        own.wait()
        for cp in xcopies:
            cp.wait_recv()

    H = ring_pieces(X)
    part = X // H

    def ring_copy(blk, h, send_sem, recv_sem, target):
        piece = out_ref.at[blk, pl.ds(h * part, part)]
        return pltpu.make_async_remote_copy(
            src_ref=piece, dst_ref=piece, send_sem=send_sem, recv_sem=recv_sem,
            device_id=device(X, Z, C, x, target, c), device_id_type=MESH)

    plus, minus = [], []
    for s in range(max(zp, zm)):
        pstep, mstep = [], []
        for h in range(H):
            hh = wrap(x - h, X) if early else h
            if s == 0 and early:
                if h == 0:
                    own.wait()
                else:
                    xcopies[h - 1].wait_recv()
            if s < zp:
                if s >= 1:
                    plus[s - 1][h].wait_recv()
                cp = ring_copy(wrap(z - s * dirn, Z), hh, sp_send.at[s * H + h], sp_recv.at[s * H + h], z + dirn)
                cp.start()
                pstep.append(cp)
            if s < zm:
                if s >= 1:
                    minus[s - 1][h].wait_recv()
                cp = ring_copy(wrap(z + s * dirn, Z), hh, sm_send.at[s * H + h], sm_recv.at[s * H + h], z - dirn)
                cp.start()
                mstep.append(cp)
        if pstep:
            plus.append(pstep)
        if mstep:
            minus.append(mstep)
        if s == min(1, max(zp, zm) - 1):
            wait_recvs(cold1)
            cold2 = stage_w(X, Z, C, lambda i: cold_mid.at[i], lambda i: cold_out.at[i], own_sem.at[2], c2_send, c2_recv)
        if s == 0:
            wcopies = []
            if C > 1:
                for j, (src, dst) in enumerate(((wg_ref, pg_ref), (wu_ref, pu_ref), (wd_ref, pd_ref))):
                    cp = pltpu.make_async_remote_copy(
                        src_ref=src, dst_ref=dst, send_sem=w_send.at[j], recv_sem=w_recv.at[j],
                        device_id=device(X, Z, C, x, z, c + 1), device_id_type=MESH)
                    cp.start()
                    wcopies.append(cp)
    for step in plus[-1:] + minus[-1:]:
        for cp in step:
            cp.wait_recv()
    for cp in xcopies + [cp for step in plus + minus for cp in step]:
        cp.wait_send()
    wait_recvs(cold2)
    wait_sends(cold1)
    wait_sends(cold2)
    for cp in wcopies:
        cp.wait_recv()
        cp.wait_send()


def scatter_kernel(X, Z, C, o_ref, cold_ref, out_ref, cold_out, cold_mid, own_sem, c1_send, c1_recv, c2_send, c2_recv, plus_buf, plus_send, minus_buf, minus_send, xbuf, xsend,
                   sp_send, sp_recv, sm_send, sm_recv, sx_send, sx_recv):
    x, z, c = coordinates(X, Z, C)
    zp, zm = Z // 2, (Z - 1) // 2
    dirn = 1 - 2 * (c % 2)
    barrier_plane(X, Z, C, x, z, c)

    def chip_sum(blk):
        return o_ref[blk].astype(jnp.float32)

    H = ring_pieces(X)
    part = X // H

    def ring_step(chain, buf, send_buf, send_sem, recv_sem, s, blk, target):
        step = []
        for h in range(H):
            rows = pl.ds(h * part, part)
            val = o_ref[blk, rows].astype(jnp.float32)
            if s >= 1:
                chain[s - 1][h].wait_recv()
                val = val + buf[s - 1, rows].astype(jnp.float32)
            send_buf[s, rows] = val.astype(jnp.bfloat16)
            cp = pltpu.make_async_remote_copy(
                src_ref=send_buf.at[s, rows], dst_ref=buf.at[s, rows], send_sem=send_sem.at[s * H + h],
                recv_sem=recv_sem.at[s * H + h], device_id=device(X, Z, C, x, target, c), device_id_type=MESH)
            cp.start()
            step.append(cp)
        chain.append(step)

    plus, minus = [], []
    for s in range(max(zp, zm)):
        if s < zp:
            ring_step(plus, plus_buf, plus_send, sp_send, sp_recv, s, wrap(z + (zp - s) * dirn, Z), z + dirn)
        if s < zm:
            ring_step(minus, minus_buf, minus_send, sm_send, sm_recv, s, wrap(z - (zm - s) * dirn, Z), z - dirn)
        if s == 0:
            cold1 = stage_w(X, Z, C, lambda i: cold_ref.at[i], lambda i: cold_mid.at[i], own_sem.at[0], c2_send, c2_recv)
    wait_recvs(cold1)
    cold2 = stage_x(X, Z, C, lambda i: cold_mid.at[:, i], lambda i: cold_out.at[i], own_sem.at[1], c1_send, c1_recv)
    xcopies = []
    for h in range(H):
        rows = pl.ds(h * part, part)
        piece = o_ref[z, rows].astype(jnp.float32)
        if zp:
            plus[zp - 1][h].wait_recv()
            piece = piece + plus_buf[zp - 1, rows].astype(jnp.float32)
        if zm:
            minus[zm - 1][h].wait_recv()
            piece = piece + minus_buf[zm - 1, rows].astype(jnp.float32)
        xsend[rows] = piece.astype(jnp.bfloat16)
        if part == 1:
            k = wrap(h - x, X)

            @pl.when(k != 0)
            def _():
                pltpu.make_async_remote_copy(
                    src_ref=xsend.at[h], dst_ref=xbuf.at[k - 1], send_sem=sx_send.at[k - 1], recv_sem=sx_recv.at[k - 1],
                    device_id=device(X, Z, C, h, z, c), device_id_type=MESH).start()
    for k in range(1, X):
        cp = pltpu.make_async_remote_copy(
            src_ref=xsend.at[(x + k) % X], dst_ref=xbuf.at[k - 1], send_sem=sx_send.at[k - 1], recv_sem=sx_recv.at[k - 1],
            device_id=device(X, Z, C, x + k, z, c), device_id_type=MESH)
        if part != 1:
            cp.start()
        xcopies.append(cp)
    result = xsend[x].astype(jnp.float32)
    for k, cp in enumerate(xcopies):
        cp.wait_recv()
        result = result + xbuf[k].astype(jnp.float32)
    out_ref[...] = result.astype(out_ref.dtype)
    for cp in [cp for step in plus + minus for cp in step] + xcopies:
        cp.wait_send()
    wait_recvs(cold2)
    wait_sends(cold1)
    wait_sends(cold2)


def hot_gather(X, Z, C, tokens, outgoing, w_gate, w_up, w_down):
    R, D = tokens.shape
    zp, zm = Z // 2, (Z - 1) // 2
    W = Z * C
    n, S, _ = outgoing.shape
    outgoing = outgoing.reshape(X, W, S, D)
    dma = pltpu.SemaphoreType.DMA
    vmem = pl.BlockSpec(memory_space=pltpu.VMEM)
    anywhere = pl.BlockSpec(memory_space=pl.ANY)
    return pl.pallas_call(
        functools.partial(gather_kernel, X, Z, C),
        out_shape=(
            jax.ShapeDtypeStruct((Z, X, R, D), tokens.dtype), jax.ShapeDtypeStruct((W, X, S, D), outgoing.dtype),
            jax.ShapeDtypeStruct(w_gate.shape, w_gate.dtype), jax.ShapeDtypeStruct(w_up.shape, w_up.dtype),
            jax.ShapeDtypeStruct(w_down.shape, w_down.dtype),
        ),
        in_specs=[vmem, vmem, anywhere, anywhere, anywhere],
        out_specs=(vmem, vmem, anywhere, anywhere, anywhere),
        scratch_shapes=[
            pltpu.VMEM((W, X, S, D), outgoing.dtype),
            dma((3,)), dma((max(X - 1, 1),)), dma((max(X - 1, 1),)), dma((W - 1,)), dma((W - 1,)), dma((3,)), dma((3,)),
            dma((max(X - 1, 1),)), dma((max(X - 1, 1),)),
            dma((max(zp, 1) * ring_pieces(X),)), dma((max(zp, 1) * ring_pieces(X),)),
            dma((max(zm, 1) * ring_pieces(X),)), dma((max(zm, 1) * ring_pieces(X),)),
        ],
        compiler_params=pltpu.CompilerParams(collective_id=0, has_side_effects=True),
    )(tokens, outgoing, w_gate, w_up, w_down)


def hot_scatter(X, Z, C, answered, cold_answered):
    _, _, R, D = answered.shape
    zp, zm = Z // 2, (Z - 1) // 2
    W, _, S, _ = cold_answered.shape
    dma = pltpu.SemaphoreType.DMA
    bf = answered.dtype
    vmem = pl.BlockSpec(memory_space=pltpu.VMEM)
    return pl.pallas_call(
        functools.partial(scatter_kernel, X, Z, C),
        out_shape=(jax.ShapeDtypeStruct((R, D), bf), jax.ShapeDtypeStruct((X, W, S, D), cold_answered.dtype)),
        in_specs=[vmem, vmem],
        out_specs=(vmem, vmem),
        scratch_shapes=[
            pltpu.VMEM((W, X, S, D), cold_answered.dtype),
            dma((2,)), dma((max(X - 1, 1),)), dma((max(X - 1, 1),)), dma((W - 1,)), dma((W - 1,)),
            pltpu.VMEM((max(zp, 1), X, R, D), bf), pltpu.VMEM((max(zp, 1), X, R, D), bf),
            pltpu.VMEM((max(zm, 1), X, R, D), bf), pltpu.VMEM((max(zm, 1), X, R, D), bf),
            pltpu.VMEM((max(X - 1, 1), R, D), bf), pltpu.VMEM((X, R, D), bf),
            dma((max(zp, 1) * ring_pieces(X),)), dma((max(zp, 1) * ring_pieces(X),)),
            dma((max(zm, 1) * ring_pieces(X),)), dma((max(zm, 1) * ring_pieces(X),)),
            dma((max(X - 1, 1),)), dma((max(X - 1, 1),)),
        ],
        compiler_params=pltpu.CompilerParams(collective_id=1, has_side_effects=True),
    )(answered, cold_answered)


def shards(X, Z, C, tokens, routes, gate_weights, w_gate, w_up, w_down):
    devices = lax.axis_size("expert")
    experts = w_gate.shape[0] * devices
    row_count = routes.shape[0]
    top_count = routes.shape[1]
    model_width = tokens.shape[1]
    slot_count = (row_count * (top_count - 1) + experts - 2) // (experts - 1)
    is_cold = jnp.arange(top_count)[None, :] >= 1
    flat_ids = routes.reshape(-1)
    flat_cold = jnp.broadcast_to(is_cold, routes.shape).reshape(-1)
    expert_iota = jnp.arange(experts, dtype=jnp.int32)
    one_hot = ((flat_ids[:, None] == expert_iota[None, :]) & flat_cold[:, None]).astype(jnp.int32)
    slot_rank = (jnp.sum(jnp.cumsum(one_hot, axis=0) * one_hot, axis=1) - 1).reshape(routes.shape)
    slot_iota = jnp.arange(slot_count, dtype=jnp.int32)
    select = (routes[:, :, None, None] == expert_iota[None, None, :, None]) & (
        slot_rank[:, :, None, None] == slot_iota[None, None, None, :]
    ) & is_cold[:, :, None, None]
    placing = jnp.sum(select.astype(jnp.bfloat16), axis=1)
    outgoing = jnp.einsum(
        "res,rd->esd", placing, tokens, preferred_element_type=jnp.float32
    ).astype(jnp.bfloat16)
    local_gate = w_gate.reshape(w_gate.shape[1:])
    local_up = w_up.reshape(w_up.shape[1:])
    local_down = w_down.reshape(w_down.shape[1:])
    hot_expert = routes[0, 0]
    me = lax.axis_index("expert")
    cores = C
    same_chip = lax.div(me, jnp.int32(cores)) == lax.div(hot_expert, jnp.int32(cores))
    role = jnp.where(me == hot_expert, 0, jnp.where(same_chip, 1, 2))
    gathered, arrived, partner_gate, partner_up, partner_down = hot_gather(X, Z, C, tokens, outgoing, local_gate, local_up, local_down)
    answered = feed_forward(arrived, local_gate, local_up, local_down)

    def hot_ffn(gate_w, up_w, down_w):
        return lambda row_block: feed_forward(row_block.reshape(-1, model_width), gate_w, up_w, down_w).reshape(row_block.shape)

    hot_answer = lax.switch(
        role,
        [hot_ffn(local_gate, local_up, local_down), hot_ffn(partner_gate, partner_up, partner_down), jnp.zeros_like],
        gathered,
    )
    hot_out, returned = hot_scatter(X, Z, C, hot_answer, answered)
    returned = returned.reshape(experts, slot_count, model_width)
    index = jnp.where(is_cold, routes * slot_count + slot_rank, 0)
    picked = returned.reshape(-1, model_width)[index].astype(jnp.float32)
    values = jnp.where(is_cold[:, :, None], picked, hot_out.astype(jnp.float32)[:, None, :])
    combined = jnp.sum(gate_weights[:, :, None] * values, axis=1)
    return combined.astype(jnp.bfloat16)


def solution(mesh):
    X, Z, C = torus_shape(mesh)
    in_specs = (
        P(("dp", "expert"), None),
        P(("dp", "expert"), None),
        P(("dp", "expert"), None),
        P("expert", None, None),
        P("expert", None, None),
        P("expert", None, None),
    )
    out_specs = P(("dp", "expert"), None)
    return jax.shard_map(functools.partial(shards, X, Z, C), mesh=mesh, in_specs=in_specs, out_specs=out_specs, check_vma=False)
```
